32 devices in a mesh: shard: 4 (over y, core), ctx: 4 (over z), tp: 2 (over x).
Axes of the slice: x: 2, y: 2, z: 4, core: 2. Of those that a mesh axis runs over, the one named last changes fastest.
Arguments:
- layer_input: bfloat16 [4, 1024, 1024], P('shard', 'ctx'), may hold values from -6 to 6
- attn_norm: bfloat16 [1024], P(('shard', 'ctx')), may hold values from 0.5 to 1.5
- w_query: bfloat16 [1024, 1024], P(('shard', 'ctx'), 'tp'), may hold values from -0.25 to 0.25
- w_key: bfloat16 [1024, 512], P(('shard', 'ctx'), 'tp'), may hold values from -0.25 to 0.25
- w_value: bfloat16 [1024, 512], P(('shard', 'ctx'), 'tp'), may hold values from -0.1875 to 0.1875
- w_out: bfloat16 [1024, 1024], P('tp', ('shard', 'ctx')), may hold values from -1.5 to 1.5
- moe_norm: bfloat16 [1024], P(('shard', 'ctx')), may hold values from 0.5 to 1.5
- expert_weights: bfloat16 [32, 3, 1024, 512], P('ctx', None, 'shard', 'tp')
- expert_ids: int32 [4, 1024, 8], P('shard', 'ctx'), may hold values from 0 to 31, as said below
- slot_ids: int32 [4, 1024, 8], P('shard', 'ctx'), may hold values from 0 to 96, as said below
- gate_values: float32 [4, 1024, 8], P('shard', 'ctx'), may hold values from 0.06 to 0.25
- piece_starts: int32 [4, 1], P('shard'), may hold values from 0 to 768, as said below
- grad_out: bfloat16 [4, 1024, 1024], P('shard', 'ctx'), may hold values from -6 to 6
Outputs:
- output: bfloat16 [4, 1024, 1024], P('shard', 'ctx')
- input_grad: bfloat16 [4, 1024, 1024], P('shard', 'ctx')
- attn_norm_grad: float32 [1024], P(('shard', 'ctx'))
- query_grad: float32 [1024, 1024], P(('shard', 'ctx'), 'tp')
- key_grad: float32 [1024, 512], P(('shard', 'ctx'), 'tp')
- value_grad: float32 [1024, 512], P(('shard', 'ctx'), 'tp')
- out_grad: float32 [1024, 1024], P('tp', ('shard', 'ctx'))
- moe_norm_grad: float32 [1024], P(('shard', 'ctx'))
- expert_grad: float32 [32, 3, 1024, 512], P('ctx', None, 'shard', 'tp')
The draws below stay inside these ranges and needn't reach their ends.
Inputs may be any that keep to these rules, and one draw needn't show every extreme that they name: `expert_ids`: each row names 8 different experts. `slot_ids`: within each aligned group of 256 positions of a sequence, the pairs (position, k) that name an expert get slots 0, 1, 2, ... in order of position and then of k; a pair whose rank is 96 or more gets 96 and is dropped. In every group some expert is named 96 times or more, and in every sequence one expert is so in all of its groups. `piece_starts`: piece k of a sequence starts between k * 4 * 256 and k * 4 * 256 + 3 * 256; in the first sequence the first piece starts at 0 and the last at the latest start allowed; when a sequence has only one piece, that piece starts at the latest start allowed.
All inputs are finite; a program needn't handle non-finite values.
Results may differ from the reference program's by a relative error of at most 0.018.
Values may be sent and summed in bfloat16 or wider, within the bound.
No kernel may reach another device: no remote copies, remote signals or barrier semaphores. Data moves between devices by JAX's collectives and lax.ppermute only.
A program may use at most 192 MiB of HBM per device.

```python
import math
import jax
import jax.numpy as jnp
from jax import lax

D = 1024
HEADS = 16
KV_HEADS = 8
HEAD_DIM = 64
EXPERTS = 32
EXPERT_FF = 512
TOPK = 8
PIECE = 256
TOK_DEV = 256
SEQS = 4
LENGTH = 1024
CAP = 96
PIECES = 1


def route_tables(key):
    base = jax.random.fold_in(key, 11)
    key_list = jax.random.split(base, 6)
    groups = LENGTH // TOK_DEV
    noise_part = jax.random.randint(key_list[0], (SEQS, groups, TOK_DEV, EXPERTS), 0, 65536)
    expert_bias = jax.random.randint(key_list[1], (SEQS, groups, 1, EXPERTS), 0, 32768)
    hot_sequence = jax.random.randint(key_list[2], (SEQS, 1, 1, 1), 0, EXPERTS)
    hot_group = jax.random.randint(key_list[3], (SEQS, groups, 1, 1), 0, EXPERTS)
    experts_row = jnp.arange(EXPERTS, dtype=jnp.int32)

    def half_mask(mask_key):
        raw_order = jax.random.randint(mask_key, (SEQS, groups, TOK_DEV), 0, 65536) * TOK_DEV + jnp.arange(TOK_DEV, dtype=jnp.int32)
        rank_in = jnp.argsort(jnp.argsort(raw_order, axis=-1), axis=-1)
        return (rank_in < TOK_DEV // 2)[..., None]
    boost_part = jnp.where(half_mask(key_list[4]) & (experts_row == hot_sequence), 131072, 0)
    boost_part = boost_part + jnp.where(half_mask(key_list[5]) & (experts_row == hot_group), 131072, 0)
    scores = (noise_part + expert_bias + boost_part) * EXPERTS + experts_row
    chosen = lax.top_k(scores, TOPK)[1].astype(jnp.int32)
    onehot = (chosen[..., None] == experts_row).astype(jnp.int32).reshape(SEQS, groups, TOK_DEV * TOPK, EXPERTS)
    rank_in = jnp.sum((jnp.cumsum(onehot, axis=2) - 1) * onehot, axis=-1)
    slot_table = jnp.minimum(rank_in, CAP).reshape(SEQS, LENGTH, TOPK).astype(jnp.int32)
    return (chosen.reshape(SEQS, LENGTH, TOPK), slot_table)


def draw_expert_ids(key, part):
    return route_tables(key)[0]


def draw_slot_ids(key, part):
    return route_tables(key)[1]


def draw_piece_starts(key, part):
    offsets = jax.random.randint(jax.random.fold_in(key, 23), (SEQS, PIECES), 0, 3 * PIECE + 1)
    offsets = offsets.at[0, 0].set(0)
    offsets = offsets.at[0, PIECES - 1].set(3 * PIECE)
    return (jnp.arange(PIECES, dtype=jnp.int32)[None, :] * 4 * PIECE + offsets).astype(jnp.int32)


def draw_expert_weights(key, part):
    weight_key = jax.random.fold_in(key, 31)
    shape = (EXPERTS, 3, D, EXPERT_FF)
    entries = jnp.clip(jax.random.normal(weight_key, shape, jnp.float32), -6.0, 6.0)
    factors = jnp.array([D ** (-0.5), D ** (-0.5), 4.0 * EXPERT_FF ** (-0.5)], jnp.float32)
    return (entries * factors[None, :, None, None]).astype(jnp.bfloat16)


def levels(rng, extent, pieces, least, largest):
    def one(axis_at, shards_of):
        heights = jax.random.uniform(jax.random.fold_in(jax.random.fold_in(rng, 6), axis_at), (shards_of,), jnp.float32, least / len(pieces), largest / len(pieces))
        return jnp.repeat(jnp.exp(heights), extent[axis_at] // shards_of).reshape((-1,) + (1,) * (len(extent) - axis_at - 1))

    factor_of = one(*pieces[0])
    for cut in pieces[1:]:
        factor_of = factor_of * one(*cut)
    return factor_of


def normal_values(stream_key, dims, width, limit, shards=(), kind=jnp.bfloat16):
    result = jax.random.normal(stream_key, dims, jnp.float32) * width
    if len(shards) > 0:
        result = levels(stream_key, dims, shards, -0.22, 0.18) * result
    return jnp.clip(result, min=-limit, max=limit).astype(kind)


def setup_inputs(seed: int = 0) -> dict:
    arg_keys = jax.random.split(jax.random.key(seed), 14)
    layer_input = normal_values(arg_keys[0], (SEQS, LENGTH, D), 1.0, 6.0, ((0, 4), (1, 4)))
    attn_norm = jnp.clip(1.0 + 0.1 * jax.random.normal(arg_keys[1], (D,), jnp.float32), 0.5, 1.5).astype(jnp.bfloat16)
    w_query = normal_values(arg_keys[2], (D, HEADS * HEAD_DIM), (D // 2) ** -0.5, 0.25, ((0, 16), (1, 2)))
    w_key = normal_values(arg_keys[3], (D, KV_HEADS * HEAD_DIM), (D // 2) ** -0.5, 0.25, ((0, 16), (1, 2)))
    w_value = normal_values(arg_keys[4], (D, KV_HEADS * HEAD_DIM), D ** -0.5, 0.1875, ((0, 16), (1, 2)))
    w_out = normal_values(arg_keys[5], (HEADS * HEAD_DIM, D), (HEADS * HEAD_DIM // 64) ** -0.5, 1.5, ((0, 2), (1, 16)))
    moe_norm = jnp.clip(1.0 + 0.1 * jax.random.normal(arg_keys[6], (D,), jnp.float32), 0.5, 1.5).astype(jnp.bfloat16)
    expert_weights = draw_expert_weights(jax.random.fold_in(arg_keys[13], 71), 0)
    expert_ids = draw_expert_ids(jax.random.fold_in(arg_keys[13], 71), 0)
    slot_ids = draw_slot_ids(jax.random.fold_in(arg_keys[13], 71), 0)
    gate_values = jnp.clip(jnp.exp(math.log(0.25) - 1.4271164 * jax.random.uniform(arg_keys[10], (SEQS, LENGTH, TOPK), jnp.float32) ** levels(arg_keys[10], (SEQS, LENGTH, TOPK), ((0, 4), (1, 4)), -0.2, 0.2)), 0.06, 0.25)
    piece_starts = draw_piece_starts(jax.random.fold_in(arg_keys[13], 71), 0)
    grad_out = normal_values(arg_keys[12], (SEQS, LENGTH, D), 1.0, 6.0, ((0, 4), (1, 4)))
    return dict(layer_input=layer_input, attn_norm=attn_norm, w_query=w_query, w_key=w_key, w_value=w_value, w_out=w_out, moe_norm=moe_norm, expert_weights=expert_weights, expert_ids=expert_ids, slot_ids=slot_ids, gate_values=gate_values, piece_starts=piece_starts, grad_out=grad_out)


EPS = 1e-06
MASKED = -1e+30
HIGHEST = lax.Precision.HIGHEST

@jax.custom_vjp
def low(v):
    return lax.optimization_barrier(v.astype(jnp.bfloat16)).astype(jnp.float32)

@jax.custom_vjp
def low_back(v):
    return v

def low_keep(v):
    return (low(v), None)

def low_pass(kept, grad):
    return (grad,)

def back_keep(v):
    return (v, None)

def back_low(kept, grad):
    return (low(grad),)
low.defvjp(low_keep, low_pass)
low_back.defvjp(back_keep, back_low)

def matmul_high(left_side, right_side):
    return jnp.dot(left_side, right_side, precision=HIGHEST)

def norm_scale(values, gain):
    return values * lax.rsqrt(lax.optimization_barrier(jnp.mean(values * values, axis=-1, keepdims=True)) + EPS) * gain

def rotate(values, positions, direction):
    half_dim = values.shape[-1] // 2
    frequency = 1.0 / 10000.0 ** (jnp.arange(half_dim, dtype=jnp.float32) * 2.0 / values.shape[-1])
    angles = positions.astype(jnp.float32)[:, None] * frequency[None, :]
    cosine = jnp.cos(angles)[:, None, :]
    sine_part = direction * jnp.sin(angles)[:, None, :]
    first_half = values[..., :half_dim]
    second = values[..., half_dim:]
    return jnp.concatenate([first_half * cosine - second * sine_part, second * cosine + first_half * sine_part], axis=-1)

def picture_of(positions, starts):
    inside = (positions[:, None] >= starts[None, :]) & (positions[:, None] < starts[None, :] + PIECE)
    labels = jnp.arange(1, starts.shape[0] + 1, dtype=jnp.int32)
    return lax.optimization_barrier(jnp.sum(jnp.where(inside, labels[None, :], 0), axis=-1)).astype(jnp.int32)

def visible(query_pos, key_pos, query_label, key_label):
    causal = key_pos[None, :] <= query_pos[:, None]
    same_piece = (query_label[:, None] == key_label[None, :]) & (query_label[:, None] > 0)
    return causal | same_piece

def sequence_forward(weights, sequence, starts, chosen_all, slot_all, gate_all):
    gain_one, w_query, w_key, w_value, w_out, gain_two, w_expert = weights
    length = sequence.shape[0]
    group_size = HEADS // KV_HEADS
    score_scale = HEAD_DIM ** (-0.5)
    positions = jnp.arange(length, dtype=jnp.int32)
    normed_one = low(norm_scale(sequence, gain_one))
    queries = low(rotate(low_back(matmul_high(normed_one, w_query)).reshape(length, HEADS, HEAD_DIM), positions, 1.0))
    queries = queries.reshape(length, KV_HEADS, group_size, HEAD_DIM)
    keys = low(rotate(low_back(matmul_high(normed_one, w_key)).reshape(length, KV_HEADS, HEAD_DIM), positions, 1.0))
    values = low(low_back(matmul_high(normed_one, w_value))).reshape(length, KV_HEADS, HEAD_DIM)
    key_label = picture_of(positions, starts)
    key_span = math.gcd(length, 512)

    def attend(block_args):
        query_part, part_pos = block_args
        scores = low_back(jnp.einsum('qhgd,khd->hgqk', query_part, keys, precision=HIGHEST) * score_scale)
        visible_mask = visible(part_pos, positions, picture_of(part_pos, starts), key_label)
        scores = jnp.where(visible_mask[None, None], scores, MASKED)
        row_max = lax.optimization_barrier(jnp.max(scores, axis=-1, keepdims=True))
        expo = jnp.exp(scores - row_max)
        probs = expo / lax.optimization_barrier(jnp.sum(expo, axis=-1, keepdims=True))
        return jnp.einsum('hgqk,khd->qhgd', low(probs), values, precision=HIGHEST)
    attended = lax.map(jax.checkpoint(attend), (queries.reshape(length // key_span, key_span, KV_HEADS, group_size, HEAD_DIM), positions.reshape(length // key_span, key_span)))
    mixed = low_back(low(attended.reshape(length, HEADS * HEAD_DIM)))
    residual = sequence + low_back(matmul_high(mixed, w_out))
    normed_two = low(norm_scale(residual, gain_two))
    groups = length // TOK_DEV

    def route_group(group_args):
        block, chosen, slot, weight = group_args
        capacity_rows = EXPERTS * CAP
        slot_index = jnp.where(slot < CAP, chosen * CAP + slot, capacity_rows).reshape(-1).astype(jnp.int32)
        owner_row = jnp.repeat(jnp.arange(TOK_DEV, dtype=jnp.int32), TOPK)
        source = jnp.full((capacity_rows + 1,), TOK_DEV, jnp.int32).at[slot_index].set(owner_row)[:capacity_rows]
        padded = jnp.concatenate([block, jnp.zeros((1, D), block.dtype)], axis=0)
        dispatched = padded[source].reshape(EXPERTS, CAP, D)
        gate_lin = low_back(jnp.einsum('ecd,edf->ecf', dispatched, w_expert[:, 0], precision=HIGHEST))
        up_lin = low_back(jnp.einsum('ecd,edf->ecf', dispatched, w_expert[:, 1], precision=HIGHEST))
        hidden_act = low(jax.nn.silu(gate_lin) * up_lin)
        expert_out = low_back(jnp.einsum('ecf,edf->ecd', hidden_act, w_expert[:, 2], precision=HIGHEST))
        padded_out = jnp.concatenate([expert_out.reshape(capacity_rows, D), jnp.zeros((1, D), expert_out.dtype)], axis=0)
        picked = padded_out[slot_index].reshape(TOK_DEV, TOPK, D)
        return lax.optimization_barrier(jnp.sum(weight[:, :, None] * picked, axis=1))
    moe = lax.map(jax.checkpoint(route_group), (normed_two.reshape(groups, TOK_DEV, D), chosen_all.reshape(groups, TOK_DEV, TOPK), slot_all.reshape(groups, TOK_DEV, TOPK), gate_all.reshape(groups, TOK_DEV, TOPK)))
    return residual + moe.reshape(length, D)

def reference(layer_input, attn_norm, w_query, w_key, w_value, w_out, moe_norm, expert_weights, expert_ids, slot_ids, gate_values, piece_starts, grad_out):
    weights = tuple((item.astype(jnp.float32) for item in (attn_norm, w_query, w_key, w_value, w_out, moe_norm, expert_weights)))
    inputs = layer_input.astype(jnp.float32)
    gate_float = gate_values.astype(jnp.float32)

    def forward(sequences, weight_set):

        def one_sequence(seq_args):
            return sequence_forward(weight_set, *seq_args)
        return lax.map(jax.checkpoint(one_sequence), (sequences, piece_starts, expert_ids, slot_ids, gate_float))
    output, pull_back = jax.vjp(forward, inputs, weights)
    input_grad, weight_grads = pull_back(grad_out.astype(jnp.float32))
    return (output.astype(jnp.bfloat16), input_grad.astype(jnp.bfloat16), weight_grads[0], weight_grads[1], weight_grads[2], weight_grads[3], weight_grads[4], weight_grads[5], weight_grads[6])
```

```python
import functools

import jax
import jax.numpy as jnp
from jax import lax
from jax.experimental import pallas as pl
from jax.experimental.pallas import tpu as pltpu
from jax.sharding import PartitionSpec as P

HEAD_DIM = 64
EXPERTS = 32
TOPK = 8
PIECE = 256
CAP = 96
EPS = 1e-06
MASKED = -1e30
LANES = 128
F32 = jnp.float32
BF16 = jnp.bfloat16


def swap(value, axis, distance):
    size = lax.axis_size(axis)
    return lax.ppermute(value, axis, [(i, i ^ distance) for i in range(size)])


def spread(value, axis):
    size = lax.axis_size(axis)
    copies = jnp.broadcast_to(value[None], (size,) + value.shape)
    return lax.all_to_all(copies, axis, 0, 0, tiled=True)


def dot_nn(a, b):
    return lax.dot_general(a, b, (((1,), (0,)), ((), ())), preferred_element_type=F32)


def dot_nt(a, b):
    return lax.dot_general(a, b, (((1,), (1,)), ((), ())), preferred_element_type=F32)


def dot_tn(a, b):
    return lax.dot_general(a, b, (((0,), (0,)), ((), ())), preferred_element_type=F32)


def cost(flops, moved, special=0):
    return pl.CostEstimate(flops=int(flops), bytes_accessed=int(moved), transcendentals=int(special))


def params(megabytes=56):
    return pltpu.CompilerParams(vmem_limit_bytes=megabytes * 1024 * 1024)


def sds(shape, dtype):
    return jax.ShapeDtypeStruct(shape, dtype)


def whole(shape):
    return pl.BlockSpec(shape, lambda *_: (0,) * len(shape))


def turn(value, cosine, sine):
    lane = lax.broadcasted_iota(jnp.int32, (value.shape[0], LANES), 1) % HEAD_DIM
    first = lane < HEAD_DIM // 2
    parts = []
    for j in range(value.shape[1] // LANES):
        chunk = value[:, j * LANES : (j + 1) * LANES]
        partner = jnp.where(
            first,
            pltpu.roll(chunk, LANES - HEAD_DIM // 2, 1),
            pltpu.roll(chunk, HEAD_DIM // 2, 1),
        )
        parts.append(chunk * cosine + partner * sine)
    return parts[0] if len(parts) == 1 else jnp.concatenate(parts, axis=1)


def own_first(ref, scalars, half):
    own = scalars[2] * half
    other = (1 - scalars[2]) * half
    return jnp.concatenate(
        [
            ref[pl.ds(pl.multiple_of(own, half), half)],
            ref[pl.ds(pl.multiple_of(other, half), half)],
        ],
        axis=0,
    )


def columns(scalars, p, width):
    return pl.ds(pl.multiple_of((scalars[0] ^ p) * width, width), width)


def front(scalars, layer_input, pieces, cos_table, sin_table, widths):
    tokens, model = layer_input.shape
    quarter = pieces[0].shape[0]
    q_width, kv_width = widths
    heads = q_width + 2 * kv_width
    half = tokens // 2
    count = len(pieces)

    def body(sc, x_ref, *rest):
        piece_refs = rest[:count]
        cos_ref, sin_ref, xn_ref, q_ref, kv_ref, gain_ref = rest[count:]
        values = own_first(x_ref, sc, half).astype(F32)
        rows = lax.broadcasted_iota(jnp.int32, (quarter, quarter), 0)
        diagonal = rows == lax.broadcasted_iota(jnp.int32, (quarter, quarter), 1)
        for p in range(count):
            gains = piece_refs[p][:, heads : heads + LANES].astype(F32)
            for k in range(2):
                row = jnp.sum(jnp.where(diagonal, gains[:, k : k + 1], 0.0), axis=0, keepdims=True)
                gain_ref[k : k + 1, columns(sc, p, quarter)] = row
        inverse = lax.rsqrt(jnp.mean(values * values, axis=-1, keepdims=True) + EPS)
        xn_ref[...] = (values * inverse * gain_ref[0:1, :]).astype(BF16)
        total = None
        for p in range(count):
            part = dot_nn(xn_ref[:, columns(sc, p, quarter)], piece_refs[p][:, :heads])
            total = part if total is None else total + part
        cosine, sine = cos_ref[...], sin_ref[...]
        q_ref[...] = (turn(total[:, :q_width], cosine, sine).astype(BF16) * HEAD_DIM**-0.5).astype(
            BF16
        )
        kv_ref[:, :kv_width] = turn(total[:, q_width : q_width + kv_width], cosine, sine).astype(
            BF16
        )
        kv_ref[:, kv_width:] = total[:, q_width + kv_width :].astype(BF16)

    return pl.pallas_call(
        body,
        out_shape=[
            sds((tokens, model), BF16),
            sds((tokens, q_width), BF16),
            sds((tokens, 2 * kv_width), BF16),
            sds((8, model), F32),
        ],
        grid_spec=pltpu.PrefetchScalarGridSpec(
            num_scalar_prefetch=1,
            grid=(1,),
            in_specs=[whole(layer_input.shape)]
            + [whole(p.shape) for p in pieces]
            + [whole(cos_table.shape), whole(sin_table.shape)],
            out_specs=[
                whole((tokens, model)),
                whole((tokens, q_width)),
                whole((tokens, 2 * kv_width)),
                whole((8, model)),
            ],
        ),
        compiler_params=params(),
        cost_estimate=cost(2 * tokens * model * heads, 2 * model * (2 * tokens + heads)),
        name="front",
    )(scalars, layer_input, *pieces, cos_table, sin_table)


def inside_piece(position, start):
    return (position >= start) & (position < start + PIECE)


def seen_bias(sc, query_pos, key_pos, piece_count):
    seen = key_pos <= query_pos
    for k in range(piece_count):
        start = sc[3 + k]
        seen = seen | (inside_piece(query_pos, start) & inside_piece(key_pos, start))
    return jnp.where(seen, 0.0, MASKED)


def token_position(sc, index, group, tokens):
    return group * tokens + (index ^ (sc[2] * (tokens // 2)))


def attend(scalars, queries, kv_all, out_pieces, piece_count):
    tokens, q_width = queries.shape
    length, kv2 = kv_all.shape
    kv_width = kv2 // 2
    kv_heads = kv_width // HEAD_DIM
    pair_blocks = kv_width // LANES
    count = len(out_pieces)
    quarter = out_pieces[0].shape[0]
    model = quarter * count
    half = tokens // 2

    def body(sc, q_ref, k_ref, v_ref, *rest):
        out_refs = rest[:count]
        mixed_ref, lse_ref, own_ref, send_ref, bias_ref = rest[count:]
        c = pl.program_id(0)

        @pl.when(c == 0)
        def _():
            rows = lax.broadcasted_iota(jnp.int32, (tokens, length), 0)
            cols = lax.broadcasted_iota(jnp.int32, (tokens, length), 1)
            query_pos = token_position(sc, rows, sc[1], tokens)
            key_pos = token_position(sc, cols % tokens, cols // tokens, tokens)
            bias_ref[...] = seen_bias(sc, query_pos, key_pos, piece_count)

        low = lax.broadcasted_iota(jnp.int32, (1, LANES), 1) < HEAD_DIM
        mine = low == (c % 2 == 0)
        keys = k_ref[...].astype(F32)
        keys = jnp.where(mine, keys, pltpu.roll(keys, HEAD_DIM, 1)).astype(BF16)
        vals = v_ref[...].astype(F32)
        vals = jnp.where(mine, vals, pltpu.roll(vals, HEAD_DIM, 1)).astype(BF16)
        query = q_ref[...]
        zero = jnp.zeros_like(query)
        outs, lses = [], []
        for part in (jnp.where(low, query, zero), jnp.where(low, zero, query)):
            scores = dot_nt(part, keys) + bias_ref[...]
            top = jnp.max(scores, axis=-1, keepdims=True)
            expo = jnp.exp(scores - top)
            total = jnp.sum(expo, axis=-1, keepdims=True)
            probs = expo * (1.0 / total)
            outs.append(dot_nn(probs.astype(BF16), vals))
            lses.append(top + jnp.log(total))
        mixed_ref[:, pl.ds(pl.multiple_of(c * LANES, LANES), LANES)] = jnp.where(
            low, outs[0], outs[1]
        ).astype(BF16)
        lse_ref[...] = jnp.where(low, lses[0], lses[1])

        @pl.when(c == kv_heads - 1)
        def _():
            mixed = mixed_ref[...]
            for p in range(count):
                part = dot_nt(mixed, out_refs[p][...])
                own_ref[:, columns(sc, p, quarter)] = part[:half]
                send_ref[:, columns(sc, p, quarter)] = part[half:].astype(BF16)

    return pl.pallas_call(
        body,
        out_shape=[
            sds((tokens, q_width), BF16),
            sds((tokens, kv_heads * LANES), F32),
            sds((half, model), F32),
            sds((half, model), BF16),
        ],
        grid_spec=pltpu.PrefetchScalarGridSpec(
            num_scalar_prefetch=1,
            grid=(kv_heads,),
            in_specs=[
                pl.BlockSpec((tokens, LANES), lambda c, sc: (0, c)),
                pl.BlockSpec((length, LANES), lambda c, sc: (0, c // 2)),
                pl.BlockSpec((length, LANES), lambda c, sc: (0, pair_blocks + c // 2)),
            ]
            + [whole(p.shape) for p in out_pieces],
            out_specs=[
                whole((tokens, q_width)),
                pl.BlockSpec((tokens, LANES), lambda c, sc: (0, c)),
                whole((half, model)),
                whole((half, model)),
            ],
            scratch_shapes=[pltpu.VMEM((tokens, length), F32)],
        ),
        compiler_params=params(),
        cost_estimate=cost(
            16 * tokens * length * LANES + 2 * tokens * q_width * model,
            4 * length * kv2 + 8 * tokens * model,
            2 * kv_heads * tokens * length,
        ),
        name="attend",
    )(scalars, queries, kv_all, kv_all, *out_pieces)


def second_norm(scalars, layer_input, own, received, gains):
    tokens, model = layer_input.shape
    half = tokens // 2

    def body(sc, x_ref, own_ref, rec_ref, gain_ref, res_ref, norm_ref):
        start = pl.multiple_of(sc[2] * half, half)
        residual = (
            x_ref[pl.ds(start, half)].astype(F32) + own_ref[...] + rec_ref[...].astype(F32)
        )
        inverse = lax.rsqrt(jnp.mean(residual * residual, axis=-1, keepdims=True) + EPS)
        res_ref[...] = residual
        norm_ref[...] = (residual * inverse * gain_ref[1:2, :]).astype(BF16)

    return pl.pallas_call(
        body,
        out_shape=[sds((half, model), F32), sds((half, model), BF16)],
        grid_spec=pltpu.PrefetchScalarGridSpec(
            num_scalar_prefetch=1,
            grid=(1,),
            in_specs=[
                whole((tokens, model)),
                whole((half, model)),
                whole((half, model)),
                whole((8, model)),
            ],
            out_specs=[whole((half, model)), whole((half, model))],
        ),
        compiler_params=params(),
        cost_estimate=cost(10 * half * model, 16 * half * model),
        name="second_norm",
    )(scalars, layer_input, own, received, gains)


def experts(scalars, far, rows_in, grads_in, tables, weights, first_slot):
    half, model = rows_in[0].shape
    tokens = 2 * half
    local, _, quarter, hidden = weights[0].shape
    count = len(weights)
    per_group = 2 * local
    side_rows = local * CAP

    def body(sc, *refs):
        x_refs, refs = refs[:4], refs[4:]
        g_refs, refs = refs[:4], refs[4:]
        t_refs, refs = refs[:2], refs[2:]
        w_refs, refs = refs[:count], refs[count:]
        na_ref, nb_ref, ya_ref, yb_ref, d_ref, go_ref, h_ref = refs[:7]
        st_ref, gate_ref, ns_ref, ys_ref = refs[7:]
        e = pl.program_id(0)

        @pl.when(e == 0)
        def _():
            base = sc[1] * per_group + (sc[0] % 2) * local
            slot_row = lax.broadcasted_iota(jnp.int32, (CAP, tokens), 0).astype(F32)
            for side in range(2):
                table = t_refs[side][0]
                ids, slots, gates = (
                    table[:TOPK],
                    table[TOPK : 2 * TOPK] - CAP,
                    table[2 * TOPK : 3 * TOPK],
                )
                picks = []
                for k in range(local):
                    hit = ids == (base + k).astype(F32)
                    slot = jnp.sum(jnp.where(hit, slots, 0.0), axis=0, keepdims=True) + CAP
                    gate = jnp.sum(jnp.where(hit, gates, 0.0), axis=0, keepdims=True)
                    pick = slot_row == slot
                    weight = jnp.sum(jnp.where(pick, gate, 0.0), axis=1, keepdims=True)
                    gate_ref[k, side * CAP : (side + 1) * CAP, :] = jnp.broadcast_to(
                        weight, (CAP, LANES)
                    )
                    picks.append(jnp.where(pick, 1.0, 0.0))
                pick = jnp.concatenate(picks, axis=0)
                st_ref[side] = pick.T.astype(BF16)
                pick = pick.astype(BF16)
                for p in range(count):
                    cols = columns(sc, p, quarter)
                    block = jnp.concatenate(
                        [x_refs[2 * side][:, cols], x_refs[2 * side + 1][:, cols]], axis=0
                    )
                    got = dot_nn(pick, block).astype(BF16)
                    block = jnp.concatenate(
                        [g_refs[2 * side][0, :, cols], g_refs[2 * side + 1][0, :, cols]], axis=0
                    )
                    grad = dot_nn(pick, block)
                    for k in range(local):
                        rows = slice(side * CAP, (side + 1) * CAP)
                        d_ref[k, rows, p * quarter : (p + 1) * quarter] = got[
                            k * CAP : (k + 1) * CAP
                        ]
                        go_ref[k, rows, p * quarter : (p + 1) * quarter] = (
                            grad[k * CAP : (k + 1) * CAP] * gate_ref[k, rows, 0:1]
                        ).astype(BF16)

        gate = up = act_grad = None
        for p in range(count):
            cols = slice(p * quarter, (p + 1) * quarter)
            rows = d_ref[e, :, cols]
            a = dot_nn(rows, w_refs[p][0, 0])
            b = dot_nn(rows, w_refs[p][0, 1])
            c = dot_nn(go_ref[e, :, cols], w_refs[p][0, 2])
            gate = a if gate is None else gate + a
            up = b if up is None else up + b
            act_grad = c if act_grad is None else act_grad + c
        sig = jax.nn.sigmoid(gate)
        silu = gate * sig
        act = (silu * up).astype(BF16)
        up_grad = (act_grad * silu).astype(BF16)
        gate_grad = (act_grad * up * sig * (1.0 + gate * (1.0 - sig))).astype(BF16)
        h_ref[e, :, :hidden] = act
        h_ref[e, :, hidden : 2 * hidden] = gate_grad
        h_ref[e, :, 2 * hidden :] = up_grad
        weight = gate_ref[e, :, 0:1]
        for p in range(count):
            cols = slice(p * quarter, (p + 1) * quarter)
            ns_ref[e, :, cols] = (
                dot_nt(gate_grad, w_refs[p][0, 0]) + dot_nt(up_grad, w_refs[p][0, 1])
            ).astype(BF16)
            ys_ref[e, :, cols] = (dot_nt(act, w_refs[p][0, 2]) * weight).astype(BF16)

        @pl.when(e == local - 1)
        def _():
            for side, (n_ref, y_ref) in enumerate(((na_ref, ya_ref), (nb_ref, yb_ref))):
                place = st_ref[side]
                for p in range(count):
                    cols = slice(p * quarter, (p + 1) * quarter)
                    rows = slice(side * CAP, (side + 1) * CAP)
                    for source, target in ((ns_ref, n_ref), (ys_ref, y_ref)):
                        stacked = jnp.concatenate(
                            [source[k, rows, cols] for k in range(local)], axis=0
                        )
                        target[:, columns(sc, p, quarter)] = dot_nn(place, stacked).astype(
                            target.dtype
                        )

    group = lambda e, sc: (sc[1] ^ far, 0, 0)
    moved = 2 * count * local * 3 * quarter * hidden + 40 * tokens * model
    return pl.pallas_call(
        body,
        out_shape=[
            sds((tokens, model), F32),
            sds((tokens, model), BF16),
            sds((tokens, model), F32),
            sds((tokens, model), BF16),
            sds((local, 2 * CAP, model), BF16),
            sds((local, 2 * CAP, model), BF16),
            sds((local, 2 * CAP, 3 * hidden), BF16),
        ],
        grid_spec=pltpu.PrefetchScalarGridSpec(
            num_scalar_prefetch=1,
            grid=(local,),
            in_specs=[whole((half, model))] * 4
            + [pl.BlockSpec((1, half, model), group)] * 4
            + [pl.BlockSpec((1, 3 * TOPK, tokens), group)] * 2
            + [pl.BlockSpec((1, 3, quarter, hidden), lambda e, sc: (e, 0, 0, 0))] * count,
            out_specs=[whole((tokens, model))] * 4
            + [
                whole((local, 2 * CAP, model)),
                whole((local, 2 * CAP, model)),
                whole((local, 2 * CAP, 3 * hidden)),
            ],
            scratch_shapes=[
                pltpu.VMEM((2, tokens, side_rows), BF16),
                pltpu.VMEM((local, 2 * CAP, LANES), F32),
                pltpu.VMEM((local, 2 * CAP, model), BF16),
                pltpu.VMEM((local, 2 * CAP, model), BF16),
            ],
        ),
        compiler_params=params(),
        cost_estimate=cost(
            2 * local * 2 * CAP * model * (6 * hidden + 4 * tokens), moved, local * 2 * CAP * hidden
        ),
        name="experts",
    )(scalars, *rows_in, *grads_in, *tables, *weights)


def expert_weight_grads(row_sets, grad_sets, hidden_sets, quarter):
    groups = len(row_sets)
    local, rows, model = row_sets[0].shape
    hidden = hidden_sets[0].shape[2] // 3
    count = model // quarter
    step = min(groups, 4)

    def body(*refs):
        d_refs, go_refs, h_refs = refs[:groups], refs[groups : 2 * groups], refs[2 * groups : 3 * groups]
        out_refs = refs[3 * groups :]
        for p in range(count):
            cols = slice(p * quarter, (p + 1) * quarter)
            sums = [None, None, None]
            for start in range(0, groups, step):
                chosen = range(start, start + step)
                left = jnp.concatenate([d_refs[g][0, :, cols] for g in chosen], axis=0)
                left_out = jnp.concatenate([go_refs[g][0, :, cols] for g in chosen], axis=0)
                right = jnp.concatenate([h_refs[g][0] for g in chosen], axis=0)
                parts = (
                    dot_tn(left, right[:, hidden : 2 * hidden]),
                    dot_tn(left, right[:, 2 * hidden :]),
                    dot_tn(left_out, right[:, :hidden]),
                )
                sums = [a if b is None else a + b for a, b in zip(parts, sums)]
            for k in range(3):
                out_refs[p][0, k] = sums[k].astype(out_refs[p].dtype)

    by_expert = lambda shape: pl.BlockSpec((1,) + shape, lambda e: (e,) + (0,) * len(shape))
    out = (local, 3, quarter, hidden)
    return pl.pallas_call(
        body,
        out_shape=[sds(out, F32), sds(out, F32), sds(out, BF16), sds(out, BF16)],
        grid=(local,),
        in_specs=[by_expert((rows, model))] * (2 * groups)
        + [by_expert((rows, 3 * hidden))] * groups,
        out_specs=[by_expert((3, quarter, hidden))] * 4,
        compiler_params=params(),
        cost_estimate=cost(
            6 * local * rows * groups * model * hidden,
            2 * groups * local * rows * (2 * model + 3 * hidden) + 3 * local * 3 * model * hidden,
        ),
        name="expert_weight_grads",
    )(*row_sets, *grad_sets, *hidden_sets)


def middle_grad(scalars, parts, residual, grad_out, gains):
    tokens, model = grad_out.shape
    half = tokens // 2
    count = len(parts)

    def body(sc, *refs):
        part_refs = refs[:count]
        res_ref, go_ref, gain_ref, rg_ref, branch_ref, sum_ref = refs[count:]
        total = part_refs[0][...].astype(F32)
        for k in range(1, count):
            total = total + part_refs[k][...].astype(F32)
        residual = res_ref[...]
        start = pl.multiple_of(sc[2] * half, half)
        inverse = lax.rsqrt(jnp.mean(residual * residual, axis=-1, keepdims=True) + EPS)
        scaled = gain_ref[1:2, :] * total
        shift = jnp.mean(scaled * residual, axis=-1, keepdims=True)
        grad = (
            go_ref[pl.ds(start, half)].astype(F32)
            + inverse * scaled
            - residual * (inverse * inverse * inverse * shift)
        )
        rg_ref[...] = grad
        branch_ref[...] = grad.astype(BF16)
        sum_ref[...] = jnp.broadcast_to(
            jnp.sum(total * residual * inverse, axis=0, keepdims=True), (8, model)
        )

    return pl.pallas_call(
        body,
        out_shape=[sds((half, model), F32), sds((half, model), BF16), sds((8, model), F32)],
        grid_spec=pltpu.PrefetchScalarGridSpec(
            num_scalar_prefetch=1,
            grid=(1,),
            in_specs=[whole((half, model))] * (count + 1)
            + [whole((tokens, model)), whole((8, model))],
            out_specs=[whole((half, model)), whole((half, model)), whole((8, model))],
        ),
        compiler_params=params(),
        cost_estimate=cost(20 * half * model, 24 * half * model),
        name="middle_grad",
    )(scalars, *parts, residual, grad_out, gains)


def attend_grad(scalars, branch, queries, kv_all, lse, out_pieces, cos_table, sin_table, piece_count):
    tokens, q_width = queries.shape
    length, kv2 = kv_all.shape
    kv_width = kv2 // 2
    kv_heads = kv_width // HEAD_DIM
    pair_blocks = kv_width // LANES
    count = len(out_pieces)
    quarter = out_pieces[0].shape[0]
    model = quarter * count
    half = tokens // 2

    def body(sc, b0_ref, b1_ref, q_ref, k_ref, v_ref, lse_ref, cos_ref, sin_ref, *rest):
        out_refs = rest[:count]
        dq_ref, dkv_ref, mg_ref, bias_ref = rest[count:]
        c = pl.program_id(0)

        @pl.when(c == 0)
        def _():
            cols = lax.broadcasted_iota(jnp.int32, (length, tokens), 0)
            rows = lax.broadcasted_iota(jnp.int32, (length, tokens), 1)
            query_pos = token_position(sc, rows, sc[1], tokens)
            key_pos = token_position(sc, cols % tokens, cols // tokens, tokens)
            bias_ref[...] = seen_bias(sc, query_pos, key_pos, piece_count)
            total = None
            for p in range(count):
                col = columns(sc, p, quarter)
                block = jnp.concatenate([b0_ref[:, col], b1_ref[:, col]], axis=0)
                part = dot_nn(block, out_refs[p][...])
                total = part if total is None else total + part
            mg_ref[...] = total.astype(BF16)

        low = lax.broadcasted_iota(jnp.int32, (1, LANES), 1) < HEAD_DIM
        mine = low == (c % 2 == 0)
        keys = k_ref[...].astype(F32)
        keys = jnp.where(mine, keys, pltpu.roll(keys, HEAD_DIM, 1)).astype(BF16)
        vals = v_ref[...].astype(F32)
        vals = jnp.where(mine, vals, pltpu.roll(vals, HEAD_DIM, 1)).astype(BF16)
        query = q_ref[...]
        grad = mg_ref[:, pl.ds(pl.multiple_of(c * LANES, LANES), LANES)]
        zero = jnp.zeros_like(query)
        lse_t = lse_ref[...].T
        dqs = []
        dk = dv = None
        for g in range(2):
            query_g = jnp.where(low, query, zero) if g == 0 else jnp.where(low, zero, query)
            grad_g = jnp.where(low, grad, zero) if g == 0 else jnp.where(low, zero, grad)
            scores = dot_nt(keys, query_g) + bias_ref[...]
            probs = jnp.exp(scores - lse_t[g * HEAD_DIM : g * HEAD_DIM + 1])
            prob_grad = dot_nt(vals, grad_g)
            delta = jnp.sum(probs * prob_grad, axis=0, keepdims=True)
            score_grad = (probs * (prob_grad - delta)).astype(BF16)
            dqs.append(dot_tn(score_grad, keys))
            dk_g = dot_nn(score_grad, query_g)
            dv_g = dot_nn(probs.astype(BF16), grad_g)
            dk = dk_g if dk is None else dk + dk_g
            dv = dv_g if dv is None else dv + dv_g
        dq = jnp.where(low, dqs[0], dqs[1]) * HEAD_DIM**-0.5
        dq_ref[...] = turn(dq, cos_ref[...], -sin_ref[...]).astype(BF16)
        for k, value in ((0, dk), (pair_blocks, dv)):
            value = (value + pltpu.roll(value, HEAD_DIM, 1)).astype(BF16)
            where = pl.ds(pl.multiple_of((k + c // 2) * LANES, LANES), LANES)
            dkv_ref[:, where] = jnp.where(mine, value, dkv_ref[:, where])

    return pl.pallas_call(
        body,
        out_shape=[sds((tokens, q_width), BF16), sds((length, kv2), BF16)],
        grid_spec=pltpu.PrefetchScalarGridSpec(
            num_scalar_prefetch=1,
            grid=(kv_heads,),
            in_specs=[
                whole((half, model)),
                whole((half, model)),
                pl.BlockSpec((tokens, LANES), lambda c, sc: (0, c)),
                pl.BlockSpec((length, LANES), lambda c, sc: (0, c // 2)),
                pl.BlockSpec((length, LANES), lambda c, sc: (0, pair_blocks + c // 2)),
                pl.BlockSpec((tokens, LANES), lambda c, sc: (0, c)),
                whole((tokens, LANES)),
                whole((tokens, LANES)),
            ]
            + [whole(p.shape) for p in out_pieces],
            out_specs=[
                pl.BlockSpec((tokens, LANES), lambda c, sc: (0, c)),
                whole((length, kv2)),
            ],
            scratch_shapes=[
                pltpu.VMEM((tokens, q_width), BF16),
                pltpu.VMEM((length, tokens), F32),
            ],
        ),
        compiler_params=params(),
        cost_estimate=cost(
            40 * tokens * length * LANES + 2 * tokens * q_width * model,
            6 * length * kv2 + 8 * tokens * model,
            2 * kv_heads * tokens * length,
        ),
        name="attend_grad",
    )(scalars, *branch, queries, kv_all, kv_all, lse, cos_table, sin_table, *out_pieces)


def outer(scalars, left, right, extra, quarter, name):
    tokens, model = right.shape[0], left[0].shape[1]
    width = right.shape[1]
    count = model // quarter
    out_width = width + (LANES if extra is not None else 0)
    extras = [] if extra is None else [extra]

    def body(sc, *refs):
        left_refs, refs = refs[: len(left)], refs[len(left) :]
        right_ref, refs = refs[0], refs[1:]
        extra_refs, out_refs = refs[: len(extras)], refs[len(extras) :]
        values = right_ref[...]
        for p in range(count):
            cols = columns(sc, p, quarter)
            blocks = [r[:, cols] for r in left_refs]
            block = blocks[0] if len(blocks) == 1 else jnp.concatenate(blocks, axis=0)
            out_refs[p][:, :width] = dot_tn(block, values).astype(out_refs[p].dtype)
            if extras:
                rows = lax.broadcasted_iota(jnp.int32, (quarter, quarter), 0)
                diagonal = rows == lax.broadcasted_iota(jnp.int32, (quarter, quarter), 1)
                row = extra_refs[0][0:1, cols]
                column = jnp.sum(jnp.where(diagonal, row, 0.0), axis=1, keepdims=True)
                out_refs[p][:, width:] = jnp.broadcast_to(column, (quarter, LANES)).astype(
                    out_refs[p].dtype
                )

    out = (quarter, out_width)
    return pl.pallas_call(
        body,
        out_shape=[sds(out, F32), sds(out, BF16), sds(out, F32), sds(out, BF16)],
        grid_spec=pltpu.PrefetchScalarGridSpec(
            num_scalar_prefetch=1,
            grid=(1,),
            in_specs=[whole(a.shape) for a in (*left, right, *extras)],
            out_specs=[whole(out)] * 4,
        ),
        compiler_params=params(),
        cost_estimate=cost(
            2 * tokens * model * width, 2 * tokens * (model + width) + 3 * model * width
        ),
        name=name,
    )(scalars, *left, right, *extras)


def reduce_rows(parts):
    own, send, far, far_send = parts
    kept = own + swap(send, "shard", 1).astype(F32)
    passed = (far + swap(far_send, "shard", 1).astype(F32)).astype(BF16)
    total = (kept + swap(passed, "shard", 2).astype(F32)).astype(BF16)
    groups = lax.axis_size("ctx")
    rows = total.shape[0] // groups
    got = lax.all_to_all(total.reshape(groups, rows, total.shape[1]), "ctx", 0, 0, tiled=True)
    return jnp.sum(got.astype(F32), axis=0)


def back(scalars, dq, dkv, normed, pieces, cos_table, sin_table):
    tokens, model = normed.shape
    groups, _, kv2 = dkv.shape
    q_width = dq.shape[1]
    kv_width = kv2 // 2
    heads = q_width + kv2
    count = len(pieces)
    quarter = pieces[0].shape[0]
    half = tokens // 2

    def body(sc, dq_ref, dkv_ref, xn_ref, cos_ref, sin_ref, *rest):
        piece_refs = rest[:count]
        own_ref, send_ref = rest[count : count + 2]
        grad_refs = rest[count + 2 :]
        total = dkv_ref[0].astype(F32)
        for g in range(1, groups):
            total = total + dkv_ref[g].astype(F32)
        dk = turn(total[:, :kv_width], cos_ref[...], -sin_ref[...]).astype(BF16)
        dl_kv = jnp.concatenate([dk, total[:, kv_width:].astype(BF16)], axis=1)
        dl_q = dq_ref[...]
        for p in range(count):
            cols = columns(sc, p, quarter)
            part = dot_nt(dl_q, piece_refs[p][:, :q_width]) + dot_nt(
                dl_kv, piece_refs[p][:, q_width:heads]
            )
            own_ref[:, cols] = part[:half]
            send_ref[:, cols] = part[half:].astype(BF16)
            grad_refs[p][...] = dot_tn(xn_ref[:, cols], dl_kv).astype(grad_refs[p].dtype)

    out = (quarter, kv2)
    return pl.pallas_call(
        body,
        out_shape=[
            sds((half, model), F32),
            sds((half, model), BF16),
            sds(out, F32),
            sds(out, BF16),
            sds(out, F32),
            sds(out, BF16),
        ],
        grid_spec=pltpu.PrefetchScalarGridSpec(
            num_scalar_prefetch=1,
            grid=(1,),
            in_specs=[
                whole(a.shape) for a in (dq, dkv, normed, cos_table, sin_table, *pieces)
            ],
            out_specs=[whole((half, model))] * 2 + [whole(out)] * 4,
        ),
        compiler_params=params(),
        cost_estimate=cost(
            2 * tokens * model * (heads + kv2), 2 * model * (heads + 4 * tokens + 2 * kv2)
        ),
        name="back",
    )(scalars, dq, dkv, normed, cos_table, sin_table, *pieces)


def last_grad(scalars, layer_input, own, received, residual_grad, gains):
    tokens, model = layer_input.shape
    half = tokens // 2

    def body(sc, x_ref, own_ref, rec_ref, rg_ref, gain_ref, out_ref):
        start = pl.multiple_of(sc[2] * half, half)
        values = x_ref[pl.ds(start, half)].astype(F32)
        inverse = lax.rsqrt(jnp.mean(values * values, axis=-1, keepdims=True) + EPS)
        scaled = gain_ref[0:1, :] * (own_ref[...] + rec_ref[...].astype(F32))
        shift = jnp.mean(scaled * values, axis=-1, keepdims=True)
        out_ref[...] = (
            rg_ref[...] + inverse * scaled - values * (inverse * inverse * inverse * shift)
        ).astype(BF16)

    return pl.pallas_call(
        body,
        out_shape=sds((half, model), BF16),
        grid_spec=pltpu.PrefetchScalarGridSpec(
            num_scalar_prefetch=1,
            grid=(1,),
            in_specs=[
                whole((tokens, model)),
                whole((half, model)),
                whole((half, model)),
                whole((half, model)),
                whole((8, model)),
            ],
            out_specs=whole((half, model)),
        ),
        compiler_params=params(),
        cost_estimate=cost(12 * half * model, 14 * half * model),
        name="last_grad",
    )(scalars, layer_input, own, received, residual_grad, gains)


def local(
    layer_input,
    attn_norm,
    w_query,
    w_key,
    w_value,
    w_out,
    moe_norm,
    expert_weights,
    expert_ids,
    slot_ids,
    gate_values,
    piece_starts,
    grad_out,
):
    _, tokens, model = layer_input.shape
    half = tokens // 2
    groups = lax.axis_size("ctx")
    shard = lax.axis_index("shard")
    group = lax.axis_index("ctx")
    side = lax.axis_index("tp")
    piece_count = piece_starts.shape[1]
    scalars = jnp.concatenate(
        [jnp.stack([shard, group, side]).astype(jnp.int32), piece_starts[0]]
    )
    flat_input = layer_input[0]
    flat_grad = grad_out[0]
    q_width, kv_width = w_query.shape[1], w_key.shape[1]
    rows_here = w_query.shape[0]
    quarter = rows_here * groups

    qkv_block = jnp.concatenate(
        [
            w_query,
            w_key,
            w_value,
            attn_norm[:, None],
            moe_norm[:, None],
            jnp.zeros((rows_here, LANES - 2), BF16),
        ],
        axis=1,
    )
    block_0 = spread(qkv_block, "ctx").reshape(quarter, -1)
    block_2 = swap(block_0, "shard", 2)
    qkv_pieces = [block_0, swap(block_0, "shard", 1), block_2, swap(block_2, "shard", 1)]

    out_0 = spread(w_out.T, "ctx").reshape(quarter, -1)
    out_0, block_2 = lax.optimization_barrier((out_0, block_2))
    out_2 = swap(out_0, "shard", 2)
    out_pieces = [out_0, swap(out_0, "shard", 1), out_2, swap(out_2, "shard", 1)]

    table = jnp.concatenate(
        [
            expert_ids[0].T.astype(F32),
            slot_ids[0].T.astype(F32),
            gate_values[0].T,
        ],
        axis=0,
    )
    table = jnp.where(
        side == 0, table, jnp.concatenate([table[:, half:], table[:, :half]], axis=1)
    )
    table_own = spread(table, "ctx")
    table_mate = swap(table_own, "shard", 1)

    local_experts = expert_weights.shape[0] // 2
    core = shard % 2
    mine = lax.dynamic_slice_in_dim(expert_weights, core * local_experts, local_experts, 0)
    given = lax.dynamic_slice_in_dim(expert_weights, (1 - core) * local_experts, local_experts, 0)
    taken = swap(given, "shard", 1)
    mine, taken, out_2 = lax.optimization_barrier((mine, taken, out_2))
    expert_pieces = [mine, taken, swap(mine, "shard", 2), swap(taken, "shard", 2)]

    positions = (
        group * tokens + (jnp.arange(tokens, dtype=jnp.int32) ^ (side * half).astype(jnp.int32))
    ).astype(F32)
    lane = jnp.arange(LANES, dtype=jnp.int32)
    step = (lane % (HEAD_DIM // 2)).astype(F32)
    angles = positions[:, None] * (1.0 / 10000.0 ** (step * 2.0 / HEAD_DIM))[None, :]
    cos_table = jnp.cos(angles)
    sin_table = jnp.sin(angles) * jnp.where(lane % HEAD_DIM < HEAD_DIM // 2, -1.0, 1.0)[None, :]

    normed_one, queries, kv_here, gains = front(
        scalars, flat_input, qkv_pieces, cos_table, sin_table, (q_width, kv_width)
    )
    kv_all = spread(kv_here, "ctx").reshape(groups * tokens, 2 * kv_width)

    own_grad = lax.dynamic_slice_in_dim(flat_grad, side * half, half, 0)
    own_grad, kv_all = lax.optimization_barrier((own_grad, kv_all))
    grads_a0 = spread(own_grad, "ctx")
    grads_a1 = swap(grads_a0, "tp", 1)
    grads_in = [grads_a0, grads_a1, swap(grads_a0, "shard", 1), swap(grads_a1, "shard", 1)]

    mixed, lse, attention_own, attention_send = attend(
        scalars, queries, kv_all, out_pieces, piece_count
    )
    residual, normed_two = second_norm(
        scalars, flat_input, attention_own, swap(attention_send, "tp", 1), gains
    )

    norm_parts, out_parts = [], []
    row_sets, grad_sets, hidden_sets = [], [], []
    arrived = [normed_two] + [swap(normed_two, "ctx", b) for b in range(1, groups)]
    for b in range(groups):
        a0 = arrived[b]
        a1 = swap(a0, "tp", 1)
        rows_in = [a0, a1, swap(a0, "shard", 1), swap(a1, "shard", 1)]
        norm_a, norm_b, out_a, out_b, rows, grads, hiddens = experts(
            scalars, b, rows_in, grads_in, [table_own, table_mate], expert_pieces, None
        )
        row_sets.append(rows)
        grad_sets.append(grads)
        hidden_sets.append(hiddens)
        for parts, own, mate in ((norm_parts, norm_a, norm_b), (out_parts, out_a, out_b)):
            both = swap(mate, "shard", 1)
            sent = (own[half:] + both[half:].astype(F32)).astype(BF16)
            kept = own[:half] + both[:half].astype(F32) + swap(sent, "tp", 1).astype(F32)
            parts.append(kept if b == 0 else swap(kept.astype(BF16), "ctx", b))

    residual_grad, branch_own, gain_row = middle_grad(
        scalars, norm_parts, residual, flat_grad, gains
    )
    branch = [branch_own, swap(branch_own, "tp", 1)]

    def natural(own):
        other = swap(own, "tp", 1)
        return jnp.where(
            side == 0,
            jnp.concatenate([own, other], axis=0),
            jnp.concatenate([other, own], axis=0),
        )[None]

    out_sum = residual
    for part in out_parts:
        out_sum = out_sum + part.astype(F32)
    output = natural(out_sum.astype(BF16))

    keep_0, keep_1, send_2, send_3 = expert_weight_grads(
        row_sets, grad_sets, hidden_sets, expert_pieces[0].shape[2]
    )
    grad_0 = keep_0 + swap(send_2, "shard", 2).astype(F32)
    grad_1 = (keep_1 + swap(send_3, "shard", 2).astype(F32)).astype(BF16)
    grad_1 = swap(grad_1, "shard", 1).astype(F32)
    expert_grad = jnp.where(
        core == 0,
        jnp.concatenate([grad_0, grad_1], axis=0),
        jnp.concatenate([grad_1, grad_0], axis=0),
    )

    out_grad = reduce_rows(outer(scalars, branch, mixed, gain_row, quarter, "out_grad"))
    moe_sum = out_grad[:, q_width]
    moe_norm_grad = moe_sum + swap(moe_sum, "tp", 1)
    out_grad = out_grad[:, :q_width].T

    dq, dkv_parts = attend_grad(
        scalars, branch, queries, kv_all, lse, out_pieces, cos_table, sin_table, piece_count
    )
    dkv = lax.all_to_all(
        dkv_parts.reshape(groups, tokens, 2 * kv_width), "ctx", 0, 0, tiled=True
    )
    query_grad = reduce_rows(outer(scalars, [normed_one], dq, None, quarter, "query_grad"))
    normed_own, normed_send, *kv_parts = back(
        scalars, dq, dkv, normed_one, qkv_pieces, cos_table, sin_table
    )
    input_half = last_grad(
        scalars, flat_input, normed_own, swap(normed_send, "tp", 1), residual_grad, gains
    )
    input_grad = natural(input_half)
    kv_grad = reduce_rows(kv_parts)
    key_grad, value_grad = kv_grad[:, :kv_width], kv_grad[:, kv_width:]
    attn_sum = (
        jnp.sum(w_query.astype(F32) * query_grad, axis=1)
        + jnp.sum(w_key.astype(F32) * key_grad, axis=1)
        + jnp.sum(w_value.astype(F32) * value_grad, axis=1)
    )
    attn_norm_grad = (attn_sum + swap(attn_sum, "tp", 1)) / attn_norm.astype(F32)
    return (
        output,
        input_grad,
        attn_norm_grad,
        query_grad,
        key_grad,
        value_grad,
        out_grad,
        moe_norm_grad,
        expert_grad,
    )


def solution(mesh):
    in_specs = (
        P("shard", "ctx", None),
        P(("shard", "ctx")),
        P(("shard", "ctx"), "tp"),
        P(("shard", "ctx"), "tp"),
        P(("shard", "ctx"), "tp"),
        P("tp", ("shard", "ctx")),
        P(("shard", "ctx")),
        P("ctx", None, "shard", "tp"),
        P("shard", "ctx", None),
        P("shard", "ctx", None),
        P("shard", "ctx", None),
        P("shard", None),
        P("shard", "ctx", None),
    )
    out_specs = (
        P("shard", "ctx", None),
        P("shard", "ctx", None),
        P(("shard", "ctx")),
        P(("shard", "ctx"), "tp"),
        P(("shard", "ctx"), "tp"),
        P(("shard", "ctx"), "tp"),
        P("tp", ("shard", "ctx")),
        P(("shard", "ctx")),
        P("ctx", None, "shard", "tp"),
    )
    return jax.shard_map(local, mesh=mesh, in_specs=in_specs, out_specs=out_specs, check_vma=False)
```

```python
import functools

import jax
import jax.numpy as jnp
from jax import lax
from jax.experimental import pallas as pl
from jax.experimental.pallas import tpu as pltpu
from jax.sharding import PartitionSpec as P

HEAD_DIM = 64
EXPERTS = 32
TOPK = 8
PIECE = 256
CAP = 96
EPS = 1e-06
MASKED = -1e30
LANES = 128
F32 = jnp.float32
BF16 = jnp.bfloat16


def swap(value, axis, distance):
    size = lax.axis_size(axis)
    return lax.ppermute(value, axis, [(i, i ^ distance) for i in range(size)])


def spread(value, axis):
    size = lax.axis_size(axis)
    copies = jnp.broadcast_to(value[None], (size,) + value.shape)
    return lax.all_to_all(copies, axis, 0, 0, tiled=True)


def after(value, *others):
    return lax.optimization_barrier((value,) + others)[0]


def fence(*values):
    return lax.optimization_barrier(values)


def dot_nn(a, b):
    return lax.dot_general(a, b, (((1,), (0,)), ((), ())), preferred_element_type=F32)


def dot_nt(a, b):
    return lax.dot_general(a, b, (((1,), (1,)), ((), ())), preferred_element_type=F32)


def dot_tn(a, b):
    return lax.dot_general(a, b, (((0,), (0,)), ((), ())), preferred_element_type=F32)


def cost(flops, moved, special=0):
    return pl.CostEstimate(flops=int(flops), bytes_accessed=int(moved), transcendentals=int(special))


def params(megabytes, length=0):
    megabytes = 58 if length > 1024 else megabytes
    return pltpu.CompilerParams(vmem_limit_bytes=megabytes * 1024 * 1024)


def sds(shape, dtype):
    return jax.ShapeDtypeStruct(shape, dtype)


def whole(shape):
    return pl.BlockSpec(shape, lambda *_: (0,) * len(shape))


def turn(value, cosine, sine):
    lane = lax.broadcasted_iota(jnp.int32, (value.shape[0], LANES), 1) % HEAD_DIM
    first = lane < HEAD_DIM // 2
    parts = []
    for j in range(value.shape[1] // LANES):
        chunk = value[:, j * LANES : (j + 1) * LANES]
        partner = jnp.where(
            first,
            pltpu.roll(chunk, LANES - HEAD_DIM // 2, 1),
            pltpu.roll(chunk, HEAD_DIM // 2, 1),
        )
        parts.append(chunk * cosine + partner * sine)
    return parts[0] if len(parts) == 1 else jnp.concatenate(parts, axis=1)


def rows_at(index, size):
    return pl.ds(pl.multiple_of(index * size, size), size)


def columns(scalars, p, width):
    return pl.ds(pl.multiple_of((scalars[0] ^ p) * width, width), width)


def front(scalars, layer_input, others, pieces, cos_table, sin_table, widths):
    tokens, model = layer_input.shape
    quarter = pieces[0].shape[0]
    q_width, kv_width = widths
    heads = q_width + 2 * kv_width
    gain_column = pieces[0].shape[1] - LANES
    half = tokens // 2
    count = len(pieces)
    groups = 1 + len(others) // 2
    length = groups * tokens

    def body(sc, x_ref, *rest):
        other_refs, rest = rest[: len(others)], rest[len(others) :]
        piece_refs = rest[:count]
        cos_ref, sin_ref, xn_ref, q_ref, kv_ref, gain_ref = rest[count:]
        rows = lax.broadcasted_iota(jnp.int32, (quarter, quarter), 0)
        diagonal = rows == lax.broadcasted_iota(jnp.int32, (quarter, quarter), 1)
        for p in range(count):
            gains = piece_refs[p][:, gain_column : gain_column + LANES].astype(F32)
            for k in range(2):
                row = jnp.sum(jnp.where(diagonal, gains[:, k : k + 1], 0.0), axis=0, keepdims=True)
                gain_ref[k : k + 1, columns(sc, p, quarter)] = row
        gain = gain_ref[0:1, :]
        for b in range(groups):
            for h in range(2):
                if b == 0:
                    values = x_ref[rows_at(sc[2] ^ h, half)].astype(F32)
                else:
                    values = other_refs[2 * (b - 1) + h][...].astype(F32)
                inverse = lax.rsqrt(jnp.mean(values * values, axis=-1, keepdims=True) + EPS)
                xn_ref[rows_at(2 * (sc[1] ^ b) + h, half)] = (values * inverse * gain).astype(BF16)

        own = rows_at(sc[1], tokens)
        total = None
        for p in range(count):
            part = dot_nn(xn_ref[own, columns(sc, p, quarter)], piece_refs[p][:, :q_width])
            total = part if total is None else total + part
        total = turn(total, cos_ref[own], sin_ref[own]).astype(BF16)
        q_ref[...] = (total * HEAD_DIM**-0.5).astype(BF16)

        @pl.loop(0, groups)
        def _(g):
            here = rows_at(g, tokens)
            total = None
            for p in range(count):
                part = dot_nn(xn_ref[here, columns(sc, p, quarter)], piece_refs[p][:, q_width:heads])
                total = part if total is None else total + part
            kv_ref[here, :kv_width] = turn(total[:, :kv_width], cos_ref[here], sin_ref[here]).astype(
                BF16
            )
            kv_ref[here, kv_width:] = total[:, kv_width:].astype(BF16)

    outs = [
        ((length, model), BF16),
        ((tokens, q_width), BF16),
        ((length, 2 * kv_width), BF16),
        ((8, model), F32),
    ]
    arrays = (layer_input, *others, *pieces, cos_table, sin_table)
    return pl.pallas_call(
        body,
        out_shape=[sds(*o) for o in outs],
        grid_spec=pltpu.PrefetchScalarGridSpec(
            num_scalar_prefetch=1,
            grid=(1,),
            in_specs=[whole(a.shape) for a in arrays],
            out_specs=[whole(o[0]) for o in outs],
        ),
        compiler_params=params(58),
        cost_estimate=cost(
            2 * model * (tokens * q_width + length * 2 * kv_width),
            2 * model * (2 * length + heads) + 2 * length * (kv_width + 2 * LANES),
        ),
        name="front",
    )(scalars, *arrays)


def inside_piece(position, start):
    return (position >= start) & (position < start + PIECE)


def seen_bias(sc, query_pos, key_pos, piece_count):
    seen = key_pos <= query_pos
    for k in range(piece_count):
        start = sc[3 + k]
        seen = seen | (inside_piece(query_pos, start) & inside_piece(key_pos, start))
    return jnp.where(seen, 0.0, MASKED)


def token_position(sc, index, group, tokens):
    return group * tokens + (index ^ (sc[2] * (tokens // 2)))


def attend(scalars, queries, kv_all, out_pieces, piece_count):
    tokens, q_width = queries.shape
    length, kv2 = kv_all.shape
    kv_width = kv2 // 2
    kv_heads = kv_width // HEAD_DIM
    heads = q_width + kv2
    pair_blocks = kv_width // LANES
    count = len(out_pieces)
    quarter = out_pieces[0].shape[0]
    model = quarter * count
    half = tokens // 2

    def body(sc, q_ref, k_ref, v_ref, *rest):
        out_refs = rest[:count]
        mixed_ref, lse_ref, own_ref, send_ref, bias_ref = rest[count:]
        c = pl.program_id(0)

        @pl.when(c == 0)
        def _():
            rows = lax.broadcasted_iota(jnp.int32, (tokens, length), 0)
            cols = lax.broadcasted_iota(jnp.int32, (tokens, length), 1)
            query_pos = token_position(sc, rows, sc[1], tokens)
            key_pos = token_position(sc, cols % tokens, cols // tokens, tokens)
            bias_ref[...] = seen_bias(sc, query_pos, key_pos, piece_count)

        low = lax.broadcasted_iota(jnp.int32, (1, LANES), 1) < HEAD_DIM
        mine = low == (c % 2 == 0)
        keys = k_ref[...].astype(F32)
        keys = jnp.where(mine, keys, pltpu.roll(keys, HEAD_DIM, 1)).astype(BF16)
        vals = v_ref[...].astype(F32)
        vals = jnp.where(mine, vals, pltpu.roll(vals, HEAD_DIM, 1)).astype(BF16)
        query = q_ref[...]
        zero = jnp.zeros_like(query)
        outs, lses = [], []
        for part in (jnp.where(low, query, zero), jnp.where(low, zero, query)):
            scores = dot_nt(part, keys) + bias_ref[...]
            top = jnp.max(scores, axis=-1, keepdims=True)
            expo = jnp.exp(scores - top)
            total = jnp.sum(expo, axis=-1, keepdims=True)
            probs = expo * (1.0 / total)
            outs.append(dot_nn(probs.astype(BF16), vals))
            lses.append(top + jnp.log(total))
        mixed_ref[:, pl.ds(pl.multiple_of(c * LANES, LANES), LANES)] = jnp.where(
            low, outs[0], outs[1]
        ).astype(BF16)
        lse_ref[...] = jnp.where(low, lses[0], lses[1])

        @pl.when(c == kv_heads - 1)
        def _():
            mixed = mixed_ref[...]
            for p in range(count):
                part = dot_nt(mixed, out_refs[p][...])
                own_ref[:, columns(sc, p, quarter)] = part[:half]
                send_ref[:, columns(sc, p, quarter)] = part[half:].astype(BF16)

    return pl.pallas_call(
        body,
        out_shape=[
            sds((tokens, q_width), BF16),
            sds((tokens, kv_heads * LANES), F32),
            sds((half, model), F32),
            sds((half, model), BF16),
        ],
        grid_spec=pltpu.PrefetchScalarGridSpec(
            num_scalar_prefetch=1,
            grid=(kv_heads,),
            in_specs=[
                pl.BlockSpec((tokens, LANES), lambda c, sc: (0, c)),
                pl.BlockSpec((length, LANES), lambda c, sc: (0, c // 2)),
                pl.BlockSpec((length, LANES), lambda c, sc: (0, pair_blocks + c // 2)),
            ]
            + [pl.BlockSpec((quarter, q_width), lambda c, sc: (0, heads // q_width))] * count,
            out_specs=[
                whole((tokens, q_width)),
                pl.BlockSpec((tokens, LANES), lambda c, sc: (0, c)),
                whole((half, model)),
                whole((half, model)),
            ],
            scratch_shapes=[pltpu.VMEM((tokens, length), F32)],
        ),
        compiler_params=params(58),
        cost_estimate=cost(
            16 * tokens * length * LANES + 2 * tokens * q_width * model,
            4 * length * kv2 + 8 * tokens * model,
            2 * kv_heads * tokens * length,
        ),
        name="attend",
    )(scalars, queries, kv_all, kv_all, *out_pieces)


def second_norm(scalars, layer_input, own, received, gains):
    tokens, model = layer_input.shape
    half = tokens // 2

    def body(sc, x_ref, own_ref, rec_ref, gain_ref, res_ref, norm_ref):
        start = pl.multiple_of(sc[2] * half, half)
        residual = (
            x_ref[pl.ds(start, half)].astype(F32) + own_ref[...] + rec_ref[...].astype(F32)
        )
        inverse = lax.rsqrt(jnp.mean(residual * residual, axis=-1, keepdims=True) + EPS)
        res_ref[...] = residual
        norm_ref[...] = (residual * inverse * gain_ref[1:2, :]).astype(BF16)

    return pl.pallas_call(
        body,
        out_shape=[sds((half, model), F32), sds((half, model), BF16)],
        grid_spec=pltpu.PrefetchScalarGridSpec(
            num_scalar_prefetch=1,
            grid=(1,),
            in_specs=[
                whole((tokens, model)),
                whole((half, model)),
                whole((half, model)),
                whole((8, model)),
            ],
            out_specs=[whole((half, model)), whole((half, model))],
        ),
        compiler_params=params(8),
        cost_estimate=cost(10 * half * model, 16 * half * model),
        name="second_norm",
    )(scalars, layer_input, own, received, gains)


def experts(scalars, fars, rows_in, grads_in, weights):
    k, _, half, model = rows_in[0].shape
    tokens = 2 * half
    local, quarter, hidden = weights[0].shape
    count = model // quarter
    per_group = 2 * local
    blocks = [(side, g) for side in range(2) for g in range(k)]
    rows_each = len(blocks) * CAP

    def body(sc, *refs):
        x_refs, refs = refs[:2], refs[2:]
        g_refs, refs = refs[:2], refs[2:]
        w_refs, refs = refs[: len(weights)], refs[len(weights) :]
        na_ref, nb_ref, ya_ref, yb_ref, h_ref, d_out, go_out = refs[:7]
        st_ref, gate_ref, ns_ref, ys_ref, d_ref, go_ref, sems = refs[7:]

        def weight(p, e, m):
            return w_refs[3 * p + m][e]

        copies = (
            pltpu.make_async_copy(d_ref, d_out, sems.at[0]),
            pltpu.make_async_copy(go_ref, go_out, sems.at[1]),
        )
        base = sc[1] * per_group + (sc[0] % 2) * local
        slot_row = lax.broadcasted_iota(jnp.int32, (CAP, tokens), 0).astype(F32)
        for n, (side, g) in enumerate(blocks):
            place = sc[1] ^ fars[g]
            rows = slice(n * CAP, (n + 1) * CAP)
            table = g_refs[side][place, :, model : model + LANES].astype(F32).T
            ids, slots = table[:TOPK], table[TOPK : 2 * TOPK] - CAP
            gates = table[2 * TOPK : 3 * TOPK] + table[3 * TOPK : 4 * TOPK]
            picks = []
            for e in range(local):
                hit = ids == (base + e).astype(F32)
                slot = jnp.sum(jnp.where(hit, slots, 0.0), axis=0, keepdims=True) + CAP
                gate = jnp.sum(jnp.where(hit, gates, 0.0), axis=0, keepdims=True)
                pick = slot_row == slot
                value = jnp.sum(jnp.where(pick, gate, 0.0), axis=1, keepdims=True)
                gate_ref[e, rows, :] = jnp.broadcast_to(value, (CAP, LANES))
                picks.append(jnp.where(pick, 1.0, 0.0))
            pick = jnp.concatenate(picks, axis=0)
            st_ref[n] = pick.T.astype(BF16)
            pick = pick.astype(BF16)
            for p in range(count):
                cols = columns(sc, p, quarter)
                values = jnp.concatenate(
                    [x_refs[side][g, 0, :, cols], x_refs[side][g, 1, :, cols]], axis=0
                )
                got = dot_nn(pick, values).astype(BF16)
                grad = dot_nn(pick, g_refs[side][place, :, cols])
                for e in range(local):
                    here = slice(e * CAP, (e + 1) * CAP)
                    d_ref[e, rows, p * quarter : (p + 1) * quarter] = got[here]
                    go_ref[e, rows, p * quarter : (p + 1) * quarter] = (
                        grad[here] * gate_ref[e, rows, 0:1]
                    ).astype(BF16)
        for copy in copies:
            copy.start()

        @pl.loop(0, local)
        def _(e):
            gate = up = act_grad = None
            for p in range(count):
                cols = slice(p * quarter, (p + 1) * quarter)
                rows = d_ref[e, :, cols]
                a = dot_nn(rows, weight(p, e, 0))
                b = dot_nn(rows, weight(p, e, 1))
                c = dot_nn(go_ref[e, :, cols], weight(p, e, 2))
                gate = a if gate is None else gate + a
                up = b if up is None else up + b
                act_grad = c if act_grad is None else act_grad + c
            sig = jax.nn.sigmoid(gate)
            silu = gate * sig
            act = (silu * up).astype(BF16)
            up_grad = (act_grad * silu).astype(BF16)
            gate_grad = (act_grad * up * sig * (1.0 + gate * (1.0 - sig))).astype(BF16)
            h_ref[e, :, :hidden] = act
            h_ref[e, :, hidden : 2 * hidden] = gate_grad
            h_ref[e, :, 2 * hidden :] = up_grad
            scale = gate_ref[e, :, 0:1]
            for p in range(count):
                cols = slice(p * quarter, (p + 1) * quarter)
                ns_ref[e, :, cols] = (
                    dot_nt(gate_grad, weight(p, e, 0)) + dot_nt(up_grad, weight(p, e, 1))
                ).astype(BF16)
                ys_ref[e, :, cols] = (dot_nt(act, weight(p, e, 2)) * scale).astype(BF16)

        for n, (side, g) in enumerate(blocks):
            place = st_ref[n]
            rows = slice(n * CAP, (n + 1) * CAP)
            for p in range(count):
                cols = slice(p * quarter, (p + 1) * quarter)
                target = columns(sc, p, quarter)
                for source, out in ((ns_ref, (na_ref, nb_ref)), (ys_ref, (ya_ref, yb_ref))):
                    stacked = jnp.concatenate([source[e, rows, cols] for e in range(local)], axis=0)
                    out[side][g, :, target] = dot_nn(place, stacked).astype(BF16)
        for copy in copies:
            copy.wait()

    anywhere = pl.BlockSpec(memory_space=pl.ANY)
    resident = pl.BlockSpec(memory_space=pltpu.VMEM)
    sums = sds((k, tokens, model), BF16)
    rows = sds((local, rows_each, model), BF16)
    return pl.pallas_call(
        body,
        out_shape=[sums] * 4 + [sds((local, rows_each, 3 * hidden), BF16), rows, rows],
        grid_spec=pltpu.PrefetchScalarGridSpec(
            num_scalar_prefetch=1,
            grid=(1,),
            in_specs=[resident] * (4 + len(weights)),
            out_specs=[resident] * 5 + [anywhere] * 2,
            scratch_shapes=[
                pltpu.VMEM((len(blocks), tokens, local * CAP), BF16),
                pltpu.VMEM((local, rows_each, LANES), F32),
                pltpu.VMEM((local, rows_each, model), BF16),
                pltpu.VMEM((local, rows_each, model), BF16),
                pltpu.VMEM((local, rows_each, model), BF16),
                pltpu.VMEM((local, rows_each, model), BF16),
                pltpu.SemaphoreType.DMA((2,)),
            ],
        ),
        compiler_params=params(30, 0),
        cost_estimate=cost(
            2 * local * rows_each * model * (6 * hidden + 4 * tokens),
            2 * 3 * count * local * quarter * hidden + 24 * k * tokens * model,
            local * rows_each * hidden,
        ),
        name="experts",
    )(scalars, *rows_in, *grads_in, *weights)


def expert_weight_grads(row_sets, grad_sets, hidden_sets, quarter):
    groups = len(row_sets)
    local, rows, model = row_sets[0].shape
    hidden = hidden_sets[0].shape[2] // 3
    count = model // quarter
    step = min(groups, 2)
    far_sizes = [(e, [2, 4] if e == 1 else [6]) for e in range(local)]

    def body(*refs):
        d_refs, go_refs, h_refs = refs[:groups], refs[groups : 2 * groups], refs[2 * groups : 3 * groups]
        keep_refs, far_refs = refs[3 * groups : 3 * groups + 2], refs[3 * groups + 2 :]
        expert = pl.program_id(0)
        far = []
        for p in range(count):
            cols = slice(p * quarter, (p + 1) * quarter)
            sums = [None, None, None]
            for start in range(0, groups, step):
                chosen = range(start, start + step)
                left = jnp.concatenate([d_refs[g][0, :, cols] for g in chosen], axis=0)
                left_out = jnp.concatenate([go_refs[g][0, :, cols] for g in chosen], axis=0)
                right = jnp.concatenate([h_refs[g][0] for g in chosen], axis=0)
                parts = (
                    dot_tn(left, right[:, hidden : 2 * hidden]),
                    dot_tn(left, right[:, 2 * hidden :]),
                    dot_tn(left_out, right[:, :hidden]),
                )
                sums = [a if b is None else a + b for a, b in zip(parts, sums)]
            for k in range(3):
                if p < 2:
                    keep_refs[p][0, k] = sums[k]
                else:
                    far.append(sums[k].astype(BF16))
        n = 0
        for e, sizes in far_sizes:
            mine = far_refs[n : n + len(sizes)]
            n += len(sizes)

            @pl.when(expert == e)
            def _():
                at = 0
                for ref, size in zip(mine, sizes):
                    for k in range(size):
                        ref[k] = far[at + k]
                    at += size

    by_expert = lambda shape: pl.BlockSpec((1,) + shape, lambda e: (e,) + (0,) * len(shape))
    fars = [(size, quarter, hidden) for _, sizes in far_sizes for size in sizes]
    return pl.pallas_call(
        body,
        out_shape=[sds((local, 3, quarter, hidden), F32)] * 2 + [sds(f, BF16) for f in fars],
        grid=(local,),
        in_specs=[by_expert((rows, model))] * (2 * groups)
        + [by_expert((rows, 3 * hidden))] * groups,
        out_specs=[by_expert((3, quarter, hidden))] * 2 + [whole(f) for f in fars],
        compiler_params=params(56),
        cost_estimate=cost(
            6 * local * rows * groups * model * hidden,
            2 * groups * local * rows * (2 * model + 3 * hidden) + 3 * local * 3 * model * hidden,
        ),
        name="expert_weight_grads",
    )(*row_sets, *grad_sets, *hidden_sets)


def middle_grad(scalars, parts, residual, grad_out, gains):
    tokens, model = grad_out.shape
    half = tokens // 2
    count = len(parts)

    def body(sc, *refs):
        part_refs = refs[:count]
        res_ref, go_ref, gain_ref, rg_ref, branch_ref, sum_ref = refs[count:]
        total = part_refs[0][...].astype(F32)
        for k in range(1, count):
            total = total + part_refs[k][...].astype(F32)
        residual = res_ref[...]
        start = pl.multiple_of(sc[2] * half, half)
        inverse = lax.rsqrt(jnp.mean(residual * residual, axis=-1, keepdims=True) + EPS)
        scaled = gain_ref[1:2, :] * total
        shift = jnp.mean(scaled * residual, axis=-1, keepdims=True)
        grad = (
            go_ref[pl.ds(start, half)].astype(F32)
            + inverse * scaled
            - residual * (inverse * inverse * inverse * shift)
        )
        rg_ref[...] = grad
        branch_ref[...] = grad.astype(BF16)
        sum_ref[...] = jnp.broadcast_to(
            jnp.sum(total * residual * inverse, axis=0, keepdims=True), (8, model)
        )

    return pl.pallas_call(
        body,
        out_shape=[sds((half, model), F32), sds((half, model), BF16), sds((8, model), F32)],
        grid_spec=pltpu.PrefetchScalarGridSpec(
            num_scalar_prefetch=1,
            grid=(1,),
            in_specs=[whole((half, model))] * (count + 1)
            + [whole((tokens, model)), whole((8, model))],
            out_specs=[whole((half, model)), whole((half, model)), whole((8, model))],
        ),
        compiler_params=params(12),
        cost_estimate=cost(20 * half * model, 24 * half * model),
        name="middle_grad",
    )(scalars, *parts, residual, grad_out, gains)


def attend_grad(scalars, branch, queries, kv_all, lse, out_pieces, cos_table, sin_table, piece_count):
    tokens, q_width = queries.shape
    length, kv2 = kv_all.shape
    kv_width = kv2 // 2
    kv_heads = kv_width // HEAD_DIM
    heads = q_width + kv2
    pair_blocks = kv_width // LANES
    count = len(out_pieces)
    quarter = out_pieces[0].shape[0]
    model = quarter * count
    half = tokens // 2

    def body(sc, b0_ref, b1_ref, q_ref, k_ref, v_ref, lse_ref, cos_ref, sin_ref, *rest):
        own = rows_at(sc[1], tokens)
        out_refs = rest[:count]
        dq_ref, dkv_ref, mg_ref, bias_ref = rest[count:]
        c = pl.program_id(0)

        @pl.when(c == 0)
        def _():
            cols = lax.broadcasted_iota(jnp.int32, (length, tokens), 0)
            rows = lax.broadcasted_iota(jnp.int32, (length, tokens), 1)
            query_pos = token_position(sc, rows, sc[1], tokens)
            key_pos = token_position(sc, cols % tokens, cols // tokens, tokens)
            bias_ref[...] = seen_bias(sc, query_pos, key_pos, piece_count)
            total = None
            for p in range(count):
                col = columns(sc, p, quarter)
                block = jnp.concatenate([b0_ref[:, col], b1_ref[:, col]], axis=0)
                part = dot_nn(block, out_refs[p][...])
                total = part if total is None else total + part
            mg_ref[...] = total.astype(BF16)

        low = lax.broadcasted_iota(jnp.int32, (1, LANES), 1) < HEAD_DIM
        mine = low == (c % 2 == 0)
        keys = k_ref[...].astype(F32)
        keys = jnp.where(mine, keys, pltpu.roll(keys, HEAD_DIM, 1)).astype(BF16)
        vals = v_ref[...].astype(F32)
        vals = jnp.where(mine, vals, pltpu.roll(vals, HEAD_DIM, 1)).astype(BF16)
        query = q_ref[...]
        grad = mg_ref[:, pl.ds(pl.multiple_of(c * LANES, LANES), LANES)]
        zero = jnp.zeros_like(query)
        lse_t = lse_ref[...].T
        dqs = []
        dk = dv = None
        for g in range(2):
            query_g = jnp.where(low, query, zero) if g == 0 else jnp.where(low, zero, query)
            grad_g = jnp.where(low, grad, zero) if g == 0 else jnp.where(low, zero, grad)
            scores = dot_nt(keys, query_g) + bias_ref[...]
            probs = jnp.exp(scores - lse_t[g * HEAD_DIM : g * HEAD_DIM + 1])
            prob_grad = dot_nt(vals, grad_g)
            delta = jnp.sum(probs * prob_grad, axis=0, keepdims=True)
            score_grad = (probs * (prob_grad - delta)).astype(BF16)
            dqs.append(dot_tn(score_grad, keys))
            dk_g = dot_nn(score_grad, query_g)
            dv_g = dot_nn(probs.astype(BF16), grad_g)
            dk = dk_g if dk is None else dk + dk_g
            dv = dv_g if dv is None else dv + dv_g
        dq = jnp.where(low, dqs[0], dqs[1]) * HEAD_DIM**-0.5
        dq_ref[...] = turn(dq, cos_ref[own], -sin_ref[own]).astype(BF16)
        dk = turn(dk, cos_ref[...], -sin_ref[...])
        for k, value in ((0, dk), (pair_blocks, dv)):
            value = (value + pltpu.roll(value, HEAD_DIM, 1)).astype(BF16)
            where = pl.ds(pl.multiple_of((k + c // 2) * LANES, LANES), LANES)
            dkv_ref[:, where] = jnp.where(mine, value, dkv_ref[:, where])

    return pl.pallas_call(
        body,
        out_shape=[sds((tokens, q_width), BF16), sds((length, kv2), BF16)],
        grid_spec=pltpu.PrefetchScalarGridSpec(
            num_scalar_prefetch=1,
            grid=(kv_heads,),
            in_specs=[
                whole((half, model)),
                whole((half, model)),
                pl.BlockSpec((tokens, LANES), lambda c, sc: (0, c)),
                pl.BlockSpec((length, LANES), lambda c, sc: (0, c // 2)),
                pl.BlockSpec((length, LANES), lambda c, sc: (0, pair_blocks + c // 2)),
                pl.BlockSpec((tokens, LANES), lambda c, sc: (0, c)),
                whole((length, LANES)),
                whole((length, LANES)),
            ]
            + [pl.BlockSpec((quarter, q_width), lambda c, sc: (0, heads // q_width))] * count,
            out_specs=[
                pl.BlockSpec((tokens, LANES), lambda c, sc: (0, c)),
                whole((length, kv2)),
            ],
            scratch_shapes=[
                pltpu.VMEM((tokens, q_width), BF16),
                pltpu.VMEM((length, tokens), F32),
            ],
        ),
        compiler_params=params(24, length),
        cost_estimate=cost(
            40 * tokens * length * LANES + 2 * tokens * q_width * model,
            6 * length * kv2 + 8 * tokens * model,
            2 * kv_heads * tokens * length,
        ),
        name="attend_grad",
    )(scalars, *branch, queries, kv_all, kv_all, lse, cos_table, sin_table, *out_pieces)


def store_pieces(p, value, kept_refs, send_ref):
    if p % 2 == 0:
        kept_refs[p // 2][...] = value
    else:
        send_ref[p // 2] = value.astype(BF16)


def piece_shapes(quarter, width):
    return [((quarter, width), F32), ((quarter, width), F32), ((2, quarter, width), BF16)]


def out_grads(scalars, branch, mixed, extra, quarter):
    tokens, width = mixed.shape
    model = branch[0].shape[1]
    count = model // quarter
    outs = piece_shapes(quarter, width + LANES)

    def body(sc, b0_ref, b1_ref, mixed_ref, extra_ref, own_ref, far_ref, send_ref):
        values = mixed_ref[...]
        rows = lax.broadcasted_iota(jnp.int32, (quarter, quarter), 0)
        diagonal = rows == lax.broadcasted_iota(jnp.int32, (quarter, quarter), 1)
        for p in range(count):
            cols = columns(sc, p, quarter)
            block = jnp.concatenate([b0_ref[:, cols], b1_ref[:, cols]], axis=0)
            column = jnp.sum(jnp.where(diagonal, extra_ref[0:1, cols], 0.0), axis=1, keepdims=True)
            value = jnp.concatenate(
                [dot_tn(block, values), jnp.broadcast_to(column, (quarter, LANES))], axis=1
            )
            store_pieces(p, value, (own_ref, far_ref), send_ref)

    arrays = (*branch, mixed, extra)
    return pl.pallas_call(
        body,
        out_shape=[sds(*o) for o in outs],
        grid_spec=pltpu.PrefetchScalarGridSpec(
            num_scalar_prefetch=1,
            grid=(1,),
            in_specs=[whole(a.shape) for a in arrays],
            out_specs=[whole(o[0]) for o in outs],
        ),
        compiler_params=params(16),
        cost_estimate=cost(
            2 * tokens * model * width, 2 * tokens * (model + width) + 3 * model * width
        ),
        name="out_grads",
    )(scalars, *arrays)


def qkv_grads(scalars, normed, dq, dkv, quarter):
    length, model = normed.shape
    tokens, q_width = dq.shape
    width = q_width + dkv.shape[1]
    count = model // quarter
    outs = piece_shapes(quarter, width)

    def body(sc, xn_ref, dq_ref, dkv_ref, own_ref, far_ref, send_ref):
        own = rows_at(sc[1], tokens)
        for p in range(count):
            cols = columns(sc, p, quarter)
            value = jnp.concatenate(
                [dot_tn(xn_ref[own, cols], dq_ref[...]), dot_tn(xn_ref[:, cols], dkv_ref[...])],
                axis=1,
            )
            store_pieces(p, value, (own_ref, far_ref), send_ref)

    arrays = (normed, dq, dkv)
    return pl.pallas_call(
        body,
        out_shape=[sds(*o) for o in outs],
        grid_spec=pltpu.PrefetchScalarGridSpec(
            num_scalar_prefetch=1,
            grid=(1,),
            in_specs=[whole(a.shape) for a in arrays],
            out_specs=[whole(o[0]) for o in outs],
        ),
        compiler_params=params(20, length),
        cost_estimate=cost(
            2 * model * (tokens * q_width + length * dkv.shape[1]),
            2 * length * (model + width) + 3 * model * width,
        ),
        name="qkv_grads",
    )(scalars, *arrays)


def over_mate(parts):
    own, far, sent = parts
    got = fence(swap(sent, "shard", 1))[0]
    return own + got[0].astype(F32), (far + got[1].astype(F32)).astype(BF16)


def over_ctx(kept, got):
    total = fence((kept + got.astype(F32)).astype(BF16))[0]
    groups = lax.axis_size("ctx")
    rows = total.shape[0] // groups
    return lax.all_to_all(total.reshape(groups, rows, total.shape[1]), "ctx", 0, 0, tiled=True)


def back(scalars, dq, dkv, pieces):
    tokens, q_width = dq.shape
    groups, _, kv2 = dkv.shape
    heads = q_width + kv2
    count = len(pieces)
    quarter = pieces[0].shape[0]
    model = count * quarter
    half = tokens // 2

    def body(sc, dq_ref, dkv_ref, *rest):
        piece_refs = rest[:count]
        own_ref, send_ref = rest[count:]
        total = dkv_ref[0].astype(F32)
        for g in range(1, groups):
            total = total + dkv_ref[g].astype(F32)
        dl_kv = total.astype(BF16)
        dl_q = dq_ref[...]
        for p in range(count):
            cols = columns(sc, p, quarter)
            part = dot_nt(dl_q, piece_refs[p][:, :q_width]) + dot_nt(
                dl_kv, piece_refs[p][:, q_width:heads]
            )
            own_ref[:, cols] = part[:half]
            send_ref[:, cols] = part[half:].astype(BF16)

    arrays = (dq, dkv, *pieces)
    return pl.pallas_call(
        body,
        out_shape=[sds((half, model), F32), sds((half, model), BF16)],
        grid_spec=pltpu.PrefetchScalarGridSpec(
            num_scalar_prefetch=1,
            grid=(1,),
            in_specs=[whole(dq.shape), whole(dkv.shape)] + [whole((quarter, heads))] * count,
            out_specs=[whole((half, model))] * 2,
        ),
        compiler_params=params(16, groups * tokens),
        cost_estimate=cost(2 * tokens * model * heads, 2 * model * (heads + 2 * tokens)),
        name="back",
    )(scalars, *arrays)


def last_grad(scalars, layer_input, own, received, residual_grad, gains):
    tokens, model = layer_input.shape
    half = tokens // 2

    def body(sc, x_ref, own_ref, rec_ref, rg_ref, gain_ref, out_ref):
        start = pl.multiple_of(sc[2] * half, half)
        values = x_ref[pl.ds(start, half)].astype(F32)
        inverse = lax.rsqrt(jnp.mean(values * values, axis=-1, keepdims=True) + EPS)
        scaled = gain_ref[0:1, :] * (own_ref[...] + rec_ref[...].astype(F32))
        shift = jnp.mean(scaled * values, axis=-1, keepdims=True)
        out_ref[...] = (
            rg_ref[...] + inverse * scaled - values * (inverse * inverse * inverse * shift)
        ).astype(BF16)

    return pl.pallas_call(
        body,
        out_shape=sds((half, model), BF16),
        grid_spec=pltpu.PrefetchScalarGridSpec(
            num_scalar_prefetch=1,
            grid=(1,),
            in_specs=[
                whole((tokens, model)),
                whole((half, model)),
                whole((half, model)),
                whole((half, model)),
                whole((8, model)),
            ],
            out_specs=whole((half, model)),
        ),
        compiler_params=params(8),
        cost_estimate=cost(12 * half * model, 14 * half * model),
        name="last_grad",
    )(scalars, layer_input, own, received, residual_grad, gains)


def local(
    layer_input,
    attn_norm,
    w_query,
    w_key,
    w_value,
    w_out,
    moe_norm,
    expert_weights,
    expert_ids,
    slot_ids,
    gate_values,
    piece_starts,
    grad_out,
):
    _, tokens, model = layer_input.shape
    half = tokens // 2
    groups = lax.axis_size("ctx")
    shard = lax.axis_index("shard")
    group = lax.axis_index("ctx")
    side = lax.axis_index("tp")
    piece_count = piece_starts.shape[1]
    scalars = jnp.concatenate(
        [jnp.stack([shard, group, side]).astype(jnp.int32), piece_starts[0]]
    )
    flat_input = layer_input[0]
    flat_grad = grad_out[0]
    q_width, kv_width = w_query.shape[1], w_key.shape[1]
    rows_here = w_query.shape[0]
    quarter = rows_here * groups

    weight_block = jnp.concatenate(
        [
            w_query,
            w_key,
            w_value,
            w_out.T,
            attn_norm[:, None],
            moe_norm[:, None],
            jnp.zeros((rows_here, LANES - 2), BF16),
        ],
        axis=1,
    )
    own_input = lax.dynamic_slice_in_dim(flat_input, side * half, half, 0)
    local_experts = expert_weights.shape[0] // 2
    core = shard % 2


    def experts_of(which, m):
        start = (which * local_experts, m, 0, 0)
        size = (local_experts, 1) + expert_weights.shape[2:]
        return lax.dynamic_slice(expert_weights, start, size)[:, 0]

    mine = [experts_of(core, m) for m in range(3)]
    given = [experts_of(1 - core, m) for m in range(3)]

    index = jnp.arange(groups * tokens, dtype=jnp.int32)
    positions = (index ^ (side * half).astype(jnp.int32)).astype(F32)
    lane = jnp.arange(LANES, dtype=jnp.int32)
    step = (lane % (HEAD_DIM // 2)).astype(F32)
    angles = positions[:, None] * (1.0 / 10000.0 ** (step * 2.0 / HEAD_DIM))[None, :]
    cos_table = jnp.cos(angles)
    sin_table = jnp.sin(angles) * jnp.where(lane % HEAD_DIM < HEAD_DIM // 2, -1.0, 1.0)[None, :]

    gate_high = gate_values[0].astype(BF16)
    gate_low = (gate_values[0] - gate_high.astype(F32)).astype(BF16)
    grad_block = jnp.concatenate(
        [
            flat_grad,
            expert_ids[0].astype(BF16),
            slot_ids[0].astype(BF16),
            gate_high,
            gate_low,
            jnp.zeros((tokens, LANES - 4 * TOPK), BF16),
        ],
        axis=1,
    )
    grad_block = jnp.where(
        side == 0, grad_block, jnp.concatenate([grad_block[half:], grad_block[:half]], axis=0)
    )
    grad_block = jnp.broadcast_to(grad_block[None], (groups,) + grad_block.shape)

    near = [1, 3] if groups == 4 else [1]
    rest = [b for b in range(1, groups) if b not in near]
    block_0, own_input, cos_table, sin_table, grad_block, far_0, *kept = fence(
        spread(weight_block, "ctx").reshape(quarter, -1),
        own_input,
        cos_table,
        sin_table,
        grad_block,
        swap(mine[0], "shard", 2),
        *mine,
        *given,
        *[swap(own_input, "ctx", b) for b in near],
    )
    mine, given = kept[:3], kept[3:6]
    input_at = dict(zip(near, kept[6:]))
    block_0, block_2, *kept = fence(
        block_0,
        swap(block_0, "shard", 2),
        *[swap(input_at[b], "tp", 1) for b in near],
        *[swap(own_input, "ctx", b) for b in rest],
    )
    crossed = dict(zip(near, kept[: len(near)]))
    input_at.update(dict(zip(rest, kept[len(near) :])))
    grads_own = lax.all_to_all(after(grad_block, block_2), "ctx", 0, 0, tiled=True)
    block_0, block_1, block_2, block_3, far_1, taken_0, *kept = fence(
        block_0,
        swap(block_0, "shard", 1),
        block_2,
        swap(block_2, "shard", 1),
        swap(after(mine[1], block_2), "shard", 2),
        swap(after(given[0], block_2), "shard", 1),
        *[swap(input_at[b], "tp", 1) for b in rest],
    )
    crossed.update(dict(zip(rest, kept)))
    pieces = [block_0, block_1, block_2, block_3]
    others = [v for b in range(1, groups) for v in (input_at[b], crossed[b])]

    normed_all, queries, kv_all, gains = front(
        scalars, flat_input, others, pieces, cos_table, sin_table, (q_width, kv_width)
    )
    mixed, lse, attention_own, attention_send = attend(
        scalars, queries, kv_all, pieces, piece_count
    )
    attention_send, far_2, far_3, taken_1 = fence(
        attention_send,
        swap(after(mine[2], block_1), "shard", 2),
        swap(after(taken_0, block_1), "shard", 2),
        swap(after(given[1], block_1), "shard", 1),
    )
    residual, normed_two = second_norm(
        scalars, flat_input, attention_own, swap(attention_send, "tp", 1), gains
    )

    pairs = [[0, 2], [1, 3]] if groups == 4 else [[b, b + 1] for b in range(0, groups, 2)]
    soon = [0, pairs[0][1], pairs[1][0]]
    normed_two, crossed_0, far_4, taken_2, *arrived = fence(
        normed_two,
        swap(normed_two, "tp", 1),
        swap(after(taken_1, attention_send), "shard", 2),
        swap(after(given[2], attention_send), "shard", 1),
        *[swap(normed_two, "ctx", b) for b in soon[1:]],
    )
    tokens_at = dict(zip(soon, [normed_two, *arrived]))
    late = [b for b in range(groups) if b not in soon]
    grads_own, far_5, *arrived = fence(
        grads_own,
        swap(taken_2, "shard", 2),
        *[swap(tokens_at[b], "tp", 1) for b in soon[1:]],
        *[swap(normed_two, "ctx", b) for b in late],
    )
    crossed_at = dict(zip(soon, [crossed_0, *arrived[:2]]))
    tokens_at.update(dict(zip(late, arrived[2:])))
    crossed_1 = crossed_at[soon[1]]
    arrived_1 = tokens_at[soon[1]]
    grads_in = [grads_own, swap(grads_own, "shard", 1)]
    taken = [taken_0, taken_1, taken_2]
    expert_pieces = [*mine, *taken, far_0, far_1, far_2, far_3, far_4, far_5]
    rows_own = jnp.stack(
        [jnp.stack([normed_two, crossed_0]), jnp.stack([arrived_1, crossed_1])]
    )
    rows_in = [rows_own, swap(rows_own, "shard", 1)]

    def summed(own, got, part):
        return own[:, part].astype(F32) + got[:, part].astype(F32)

    low, high = slice(0, half), slice(half, tokens)
    row_sets, grad_sets, hidden_sets = [], [], []
    norm_parts, out_parts, out_sets = {}, {}, []
    waiting = None
    order = scalars
    for n, pair in enumerate(pairs):
        own, mate, out_own, out_mate, hiddens, rows, grads = experts(
            order, pair, rows_in, grads_in, expert_pieces
        )
        row_sets.append(rows)
        grad_sets.append(grads)
        hidden_sets.append(hiddens)
        out_sets.append((pair, out_own, out_mate))
        last = n + 1 == len(pairs)
        if not last:
            later = pairs[n + 1]
            wanted = [b for b in later if b not in crossed_at]
            own, mate, *arrived = fence(own, mate, *[swap(tokens_at[b], "tp", 1) for b in wanted])
            crossed_at.update(dict(zip(wanted, arrived)))
        if waiting is not None:
            own, mate, crossed = fence(own, mate, waiting[3])
            old_pair, kept_own, got, _ = waiting
            kept = summed(kept_own, got, low) + crossed.astype(F32)
            for i, b in enumerate(old_pair):
                norm_parts[b] = kept[i] if b == 0 else swap(kept[i].astype(BF16), "ctx", b)
        if not last:
            rows_own = jnp.stack([jnp.stack([tokens_at[b], crossed_at[b]]) for b in later])
            rows_in = [rows_own, swap(rows_own, "shard", 1)]
        got = swap(mate, "shard", 1)
        sent = summed(own, got, high).astype(BF16)
        waiting = (pair, own, got, swap(sent, "tp", 1))
        order = after(scalars, sent)

    hidden_sets[-1] = after(hidden_sets[-1], sent)
    pair, own, got, crossed = waiting
    early = [b for b in norm_parts if b > 0]
    mates = [swap(after(s[2], sent), "shard", 1) for s in out_sets[:-1]]
    keep_0, keep_1, *arrived = fence(
        *expert_weight_grads(row_sets, grad_sets, hidden_sets, quarter),
        crossed,
        *[norm_parts[b] for b in early],
        *mates,
    )
    fars = len(arrived) - 1 - len(early) - len(mates)
    far_sent, crossed, arrived = arrived[:fars], arrived[fars], arrived[fars + 1 :]
    far_got = []

    def send_far(count, *ready):
        start = len(far_got)
        got = [swap(after(v, *ready), "shard", 2) for v in far_sent[start : start + count]]
        far_got.extend(got)
        return got

    def keep_far(got):
        far_got[len(far_got) - len(got) :] = got

    norm_parts.update(dict(zip(early, arrived)))
    mates = arrived[len(early) :]
    kept = summed(own, got, low) + crossed.astype(F32)
    for i, b in enumerate(pair):
        norm_parts[b] = swap(kept[i].astype(BF16), "ctx", b)

    outs = [(s[0], after(s[1], kept), m) for s, m in zip(out_sets, mates)]
    out_crossed = [swap(summed(own, got, high).astype(BF16), "tp", 1) for _, own, got in outs]
    out_last = swap(after(out_sets[-1][2], kept), "shard", 1)
    sending = send_far(1, crossed)
    residual, out_last, *arrived = fence(
        residual, out_last, *[norm_parts[b] for b in range(groups)], *sending, *out_crossed
    )
    keep_far(arrived[groups : groups + len(sending)])
    out_crossed = arrived[groups + len(sending) :]
    arrived = arrived[:groups]
    residual_grad, branch_own, gain_row = middle_grad(
        scalars, arrived, residual, flat_grad, gains
    )
    sending = send_far(1, out_last)
    branch_own, branch_crossed, *sending = fence(branch_own, swap(branch_own, "tp", 1), *sending)
    keep_far(sending)
    branch = [branch_own, branch_crossed]
    for (pair, own, got), crossed in zip(outs, out_crossed):
        kept = summed(after(own, branch_own), got, low) + crossed.astype(F32)
        for i, b in enumerate(pair):
            value = kept[i]
            out_parts[b] = value if b == 0 else swap(fence(value.astype(BF16))[0], "ctx", b)
    pair, own, _ = out_sets[-1]
    own = after(own, branch_own)
    out_crossed = swap(summed(own, out_last, high).astype(BF16), "tp", 1)

    def natural(own):
        other = swap(own, "tp", 1)
        return jnp.where(
            side == 0,
            jnp.concatenate([own, other], axis=0),
            jnp.concatenate([other, own], axis=0),
        )[None]

    dq, dkv_parts = attend_grad(
        scalars, branch, queries, kv_all, lse, pieces, cos_table, sin_table, piece_count
    )
    sending = send_far(1, branch_crossed)
    dq, dkv_parts, out_crossed, *sending = fence(dq, dkv_parts, out_crossed, *sending)
    keep_far(sending)

    kept = summed(own, out_last, low) + out_crossed.astype(F32)
    for i, b in enumerate(pair):
        out_parts[b] = swap(fence(kept[i].astype(BF16))[0], "ctx", b)
    weight_parts = qkv_grads(scalars, normed_all, dq, dkv_parts, quarter)
    out_grad_parts = out_grads(scalars, branch, after(mixed, weight_parts[0]), gain_row, quarter)
    weight_kept, weight_passed = over_mate(weight_parts)
    out_kept, out_passed = over_mate(out_grad_parts)
    sending = send_far(1, dq)
    moved = [b for b in range(1, groups)]
    dkv, weight_kept, weight_got, out_kept, out_passed, *arrived = fence(
        lax.all_to_all(
            dkv_parts.reshape(groups, tokens, 2 * kv_width), "ctx", 0, 0, tiled=True
        ),
        weight_kept,
        swap(weight_passed, "shard", 2),
        out_kept,
        out_passed,
        *[out_parts[b] for b in moved],
        *sending,
    )
    out_parts.update(dict(zip(moved, arrived)))
    keep_far(arrived[len(moved) :])

    normed_own, normed_send = back(scalars, dq, dkv, pieces)
    input_half = last_grad(
        scalars, flat_input, normed_own, swap(normed_send, "tp", 1), residual_grad, gains
    )
    sending = send_far(len(far_sent), dkv)
    weight_grad, out_got, input_half, out_kept, *sending = fence(
        over_ctx(weight_kept, weight_got),
        swap(out_passed, "shard", 2),
        input_half,
        out_kept,
        *sending,
    )
    keep_far(sending)
    input_grad = natural(input_half)
    out_sum = after(residual, dkv)
    for b in range(groups):
        out_sum = out_sum + out_parts[b].astype(F32)
    output = natural(out_sum.astype(BF16))
    weight_grad = jnp.sum(weight_grad.astype(F32), axis=0)
    query_grad = weight_grad[:, :q_width]
    key_grad = weight_grad[:, q_width : q_width + kv_width]
    value_grad = weight_grad[:, q_width + kv_width :]
    out_grad = jnp.sum(over_ctx(out_kept, out_got).astype(F32), axis=0)
    moe_sum = out_grad[:, q_width]
    moe_norm_grad = moe_sum + swap(moe_sum, "tp", 1)
    out_grad = out_grad[:, :q_width].T

    got = [v[k] for v in far_got for k in range(v.shape[0])]
    grads_0, grads_1 = [], []
    for e in range(local_experts):
        blocks = [v.astype(F32) for v in got[6 * e : 6 * e + 6]]
        grads_0.append(keep_0[e] + jnp.stack(blocks[:3]))
        grads_1.append((keep_1[e] + jnp.stack(blocks[3:])).astype(BF16))
    grad_0 = jnp.stack(grads_0)
    grad_1 = swap(jnp.stack(grads_1), "shard", 1).astype(F32)
    expert_grad = jnp.where(
        core == 0,
        jnp.concatenate([grad_0, grad_1], axis=0),
        jnp.concatenate([grad_1, grad_0], axis=0),
    )
    attn_sum = (
        jnp.sum(w_query.astype(F32) * query_grad, axis=1)
        + jnp.sum(w_key.astype(F32) * key_grad, axis=1)
        + jnp.sum(w_value.astype(F32) * value_grad, axis=1)
    )
    attn_norm_grad = (attn_sum + swap(attn_sum, "tp", 1)) / attn_norm.astype(F32)
    return (
        output,
        input_grad,
        attn_norm_grad,
        query_grad,
        key_grad,
        value_grad,
        out_grad,
        moe_norm_grad,
        expert_grad,
    )


def solution(mesh):
    in_specs = (
        P("shard", "ctx", None),
        P(("shard", "ctx")),
        P(("shard", "ctx"), "tp"),
        P(("shard", "ctx"), "tp"),
        P(("shard", "ctx"), "tp"),
        P("tp", ("shard", "ctx")),
        P(("shard", "ctx")),
        P("ctx", None, "shard", "tp"),
        P("shard", "ctx", None),
        P("shard", "ctx", None),
        P("shard", "ctx", None),
        P("shard", None),
        P("shard", "ctx", None),
    )
    out_specs = (
        P("shard", "ctx", None),
        P("shard", "ctx", None),
        P(("shard", "ctx")),
        P(("shard", "ctx"), "tp"),
        P(("shard", "ctx"), "tp"),
        P(("shard", "ctx"), "tp"),
        P("tp", ("shard", "ctx")),
        P(("shard", "ctx")),
        P("ctx", None, "shard", "tp"),
    )
    return jax.shard_map(local, mesh=mesh, in_specs=in_specs, out_specs=out_specs, check_vma=False)
```

```python
import functools

import jax
import jax.numpy as jnp
from jax import lax
from jax.experimental import pallas as pl
from jax.experimental.pallas import tpu as pltpu
from jax.sharding import PartitionSpec as P

HEAD_DIM = 64
EXPERTS = 32
TOPK = 8
PIECE = 256
CAP = 96
EPS = 1e-06
MASKED = -1e30
LANES = 128
F32 = jnp.float32
BF16 = jnp.bfloat16


def swap(value, axis, distance):
    size = lax.axis_size(axis)
    return lax.ppermute(value, axis, [(i, i ^ distance) for i in range(size)])


def spread(value, axis):
    size = lax.axis_size(axis)
    copies = jnp.broadcast_to(value[None], (size,) + value.shape)
    return lax.all_to_all(copies, axis, 0, 0, tiled=True)


def after(value, *others):
    return lax.optimization_barrier((value,) + others)[0]


def fence(*values):
    return lax.optimization_barrier(values)


def dot_nn(a, b):
    return lax.dot_general(a, b, (((1,), (0,)), ((), ())), preferred_element_type=F32)


def dot_nt(a, b):
    return lax.dot_general(a, b, (((1,), (1,)), ((), ())), preferred_element_type=F32)


def dot_tn(a, b):
    return lax.dot_general(a, b, (((0,), (0,)), ((), ())), preferred_element_type=F32)


def cost(flops, moved, special=0):
    return pl.CostEstimate(flops=int(flops), bytes_accessed=int(moved), transcendentals=int(special))


def params(megabytes, length=0):
    megabytes = 58 if length > 1024 else megabytes
    return pltpu.CompilerParams(vmem_limit_bytes=megabytes * 1024 * 1024)


def sds(shape, dtype):
    return jax.ShapeDtypeStruct(shape, dtype)


def whole(shape):
    return pl.BlockSpec(shape, lambda *_: (0,) * len(shape))


def turn(value, cosine, sine):
    lane = lax.broadcasted_iota(jnp.int32, (value.shape[0], LANES), 1) % HEAD_DIM
    first = lane < HEAD_DIM // 2
    parts = []
    for j in range(value.shape[1] // LANES):
        chunk = value[:, j * LANES : (j + 1) * LANES]
        partner = jnp.where(
            first,
            pltpu.roll(chunk, LANES - HEAD_DIM // 2, 1),
            pltpu.roll(chunk, HEAD_DIM // 2, 1),
        )
        parts.append(chunk * cosine + partner * sine)
    return parts[0] if len(parts) == 1 else jnp.concatenate(parts, axis=1)


def rows_at(index, size):
    return pl.ds(pl.multiple_of(index * size, size), size)


def columns(scalars, p, width):
    return pl.ds(pl.multiple_of((scalars[0] ^ p) * width, width), width)


def spread_grads(scalars, grads, routing, groups):
    tokens, model = grads.shape
    half = tokens // 2
    out = (groups, tokens, model + LANES)

    def body(sc, grads_ref, routing_ref, out_ref):
        for h in range(2):
            here = rows_at(sc[2] ^ h, half)
            out_ref[0, h * half : (h + 1) * half, :model] = grads_ref[here]
            out_ref[0, h * half : (h + 1) * half, model:] = routing_ref[here]

    return pl.pallas_call(
        body,
        out_shape=sds(out, BF16),
        grid_spec=pltpu.PrefetchScalarGridSpec(
            num_scalar_prefetch=1,
            grid=(groups,),
            in_specs=[whole(grads.shape), whole(routing.shape)],
            out_specs=pl.BlockSpec((1,) + out[1:], lambda g, sc: (g, 0, 0)),
        ),
        compiler_params=params(12),
        cost_estimate=cost(0, 2 * (groups + 1) * tokens * (model + LANES)),
        name="spread_grads",
    )(scalars, grads, routing)


def front(scalars, layer_input, others, pieces, cos_table, sin_table, widths):
    tokens, model = layer_input.shape
    quarter = pieces[0].shape[0]
    q_width, kv_width = widths
    heads = q_width + 2 * kv_width
    gain_column = pieces[0].shape[1] - LANES
    half = tokens // 2
    count = len(pieces)
    groups = 1 + len(others) // 2
    length = groups * tokens

    def body(sc, x_ref, *rest):
        other_refs, rest = rest[: len(others)], rest[len(others) :]
        piece_refs = rest[:count]
        cos_ref, sin_ref, xn_ref, q_ref, kv_ref, gain_ref = rest[count:]
        rows = lax.broadcasted_iota(jnp.int32, (quarter, quarter), 0)
        diagonal = rows == lax.broadcasted_iota(jnp.int32, (quarter, quarter), 1)
        for p in range(count):
            gains = piece_refs[p][:, gain_column : gain_column + LANES].astype(F32)
            for k in range(2):
                row = jnp.sum(jnp.where(diagonal, gains[:, k : k + 1], 0.0), axis=0, keepdims=True)
                gain_ref[k : k + 1, columns(sc, p, quarter)] = row
        gain = gain_ref[0:1, :]
        for b in range(groups):
            for h in range(2):
                if b == 0:
                    values = x_ref[rows_at(sc[2] ^ h, half)].astype(F32)
                else:
                    values = other_refs[2 * (b - 1) + h][...].astype(F32)
                inverse = lax.rsqrt(jnp.mean(values * values, axis=-1, keepdims=True) + EPS)
                xn_ref[rows_at(2 * (sc[1] ^ b) + h, half)] = (values * inverse * gain).astype(BF16)

        own = rows_at(sc[1], tokens)
        total = None
        for p in range(count):
            part = dot_nn(xn_ref[own, columns(sc, p, quarter)], piece_refs[p][:, :q_width])
            total = part if total is None else total + part
        total = turn(total, cos_ref[own], sin_ref[own]).astype(BF16)
        q_ref[...] = (total * HEAD_DIM**-0.5).astype(BF16)

        @pl.loop(0, groups)
        def _(g):
            here = rows_at(g, tokens)
            total = None
            for p in range(count):
                part = dot_nn(xn_ref[here, columns(sc, p, quarter)], piece_refs[p][:, q_width:heads])
                total = part if total is None else total + part
            kv_ref[here, :kv_width] = turn(total[:, :kv_width], cos_ref[here], sin_ref[here]).astype(
                BF16
            )
            kv_ref[here, kv_width:] = total[:, kv_width:].astype(BF16)

    outs = [
        ((length, model), BF16),
        ((tokens, q_width), BF16),
        ((length, 2 * kv_width), BF16),
        ((8, model), F32),
    ]
    arrays = (layer_input, *others, *pieces, cos_table, sin_table)
    return pl.pallas_call(
        body,
        out_shape=[sds(*o) for o in outs],
        grid_spec=pltpu.PrefetchScalarGridSpec(
            num_scalar_prefetch=1,
            grid=(1,),
            in_specs=[whole(a.shape) for a in arrays],
            out_specs=[whole(o[0]) for o in outs],
        ),
        compiler_params=params(58),
        cost_estimate=cost(
            2 * model * (tokens * q_width + length * 2 * kv_width),
            2 * model * (2 * length + heads) + 2 * length * (kv_width + 2 * LANES),
        ),
        name="front",
    )(scalars, *arrays)


def inside_piece(position, start):
    return (position >= start) & (position < start + PIECE)


def seen_bias(sc, query_pos, key_pos, piece_count):
    seen = key_pos <= query_pos
    for k in range(piece_count):
        start = sc[3 + k]
        seen = seen | (inside_piece(query_pos, start) & inside_piece(key_pos, start))
    return jnp.where(seen, 0.0, MASKED)


def token_position(sc, index, group, tokens):
    return group * tokens + (index ^ (sc[2] * (tokens // 2)))


def attend(scalars, queries, kv_all, out_pieces, piece_count):
    tokens, q_width = queries.shape
    length, kv2 = kv_all.shape
    kv_width = kv2 // 2
    kv_heads = kv_width // HEAD_DIM
    heads = q_width + kv2
    pair_blocks = kv_width // LANES
    count = len(out_pieces)
    quarter = out_pieces[0].shape[0]
    model = quarter * count
    half = tokens // 2

    def body(sc, q_ref, k_ref, v_ref, *rest):
        out_refs = rest[:count]
        mixed_ref, lse_ref, own_ref, send_ref, bias_ref = rest[count:]
        c = pl.program_id(0)

        @pl.when(c == 0)
        def _():
            rows = lax.broadcasted_iota(jnp.int32, (tokens, length), 0)
            cols = lax.broadcasted_iota(jnp.int32, (tokens, length), 1)
            query_pos = token_position(sc, rows, sc[1], tokens)
            key_pos = token_position(sc, cols % tokens, cols // tokens, tokens)
            bias_ref[...] = seen_bias(sc, query_pos, key_pos, piece_count)

        low = lax.broadcasted_iota(jnp.int32, (1, LANES), 1) < HEAD_DIM
        mine = low == (c % 2 == 0)
        keys = k_ref[...].astype(F32)
        keys = jnp.where(mine, keys, pltpu.roll(keys, HEAD_DIM, 1)).astype(BF16)
        vals = v_ref[...].astype(F32)
        vals = jnp.where(mine, vals, pltpu.roll(vals, HEAD_DIM, 1)).astype(BF16)
        query = q_ref[...]
        zero = jnp.zeros_like(query)
        outs, lses = [], []
        for part in (jnp.where(low, query, zero), jnp.where(low, zero, query)):
            scores = dot_nt(part, keys) + bias_ref[...]
            top = jnp.max(scores, axis=-1, keepdims=True)
            expo = jnp.exp(scores - top)
            total = jnp.sum(expo, axis=-1, keepdims=True)
            probs = expo * (1.0 / total)
            outs.append(dot_nn(probs.astype(BF16), vals))
            lses.append(top + jnp.log(total))
        mixed_ref[:, pl.ds(pl.multiple_of(c * LANES, LANES), LANES)] = jnp.where(
            low, outs[0], outs[1]
        ).astype(BF16)
        lse_ref[...] = jnp.where(low, lses[0], lses[1])

        @pl.when(c == kv_heads - 1)
        def _():
            mixed = mixed_ref[...]
            for p in range(count):
                part = dot_nt(mixed, out_refs[p][...])
                own_ref[:, columns(sc, p, quarter)] = part[:half]
                send_ref[:, columns(sc, p, quarter)] = part[half:].astype(BF16)

    return pl.pallas_call(
        body,
        out_shape=[
            sds((tokens, q_width), BF16),
            sds((tokens, kv_heads * LANES), F32),
            sds((half, model), F32),
            sds((half, model), BF16),
        ],
        grid_spec=pltpu.PrefetchScalarGridSpec(
            num_scalar_prefetch=1,
            grid=(kv_heads,),
            in_specs=[
                pl.BlockSpec((tokens, LANES), lambda c, sc: (0, c)),
                pl.BlockSpec((length, LANES), lambda c, sc: (0, c // 2)),
                pl.BlockSpec((length, LANES), lambda c, sc: (0, pair_blocks + c // 2)),
            ]
            + [pl.BlockSpec((quarter, q_width), lambda c, sc: (0, heads // q_width))] * count,
            out_specs=[
                whole((tokens, q_width)),
                pl.BlockSpec((tokens, LANES), lambda c, sc: (0, c)),
                whole((half, model)),
                whole((half, model)),
            ],
            scratch_shapes=[pltpu.VMEM((tokens, length), F32)],
        ),
        compiler_params=params(58),
        cost_estimate=cost(
            16 * tokens * length * LANES + 2 * tokens * q_width * model,
            4 * length * kv2 + 8 * tokens * model,
            2 * kv_heads * tokens * length,
        ),
        name="attend",
    )(scalars, queries, kv_all, kv_all, *out_pieces)


def second_norm(scalars, layer_input, own, received, gains):
    tokens, model = layer_input.shape
    half = tokens // 2

    def body(sc, x_ref, own_ref, rec_ref, gain_ref, res_ref, norm_ref):
        start = pl.multiple_of(sc[2] * half, half)
        residual = (
            x_ref[pl.ds(start, half)].astype(F32) + own_ref[...] + rec_ref[...].astype(F32)
        )
        inverse = lax.rsqrt(jnp.mean(residual * residual, axis=-1, keepdims=True) + EPS)
        res_ref[...] = residual
        norm_ref[...] = (residual * inverse * gain_ref[1:2, :]).astype(BF16)

    return pl.pallas_call(
        body,
        out_shape=[sds((half, model), F32), sds((half, model), BF16)],
        grid_spec=pltpu.PrefetchScalarGridSpec(
            num_scalar_prefetch=1,
            grid=(1,),
            in_specs=[
                whole((tokens, model)),
                whole((half, model)),
                whole((half, model)),
                whole((8, model)),
            ],
            out_specs=[whole((half, model)), whole((half, model))],
        ),
        compiler_params=params(8),
        cost_estimate=cost(10 * half * model, 16 * half * model),
        name="second_norm",
    )(scalars, layer_input, own, received, gains)


def experts(scalars, fars, rows_in, grads_in, weights):
    k = len(fars)
    half, model = rows_in[0].shape
    tokens = 2 * half
    local, quarter, hidden = weights[0].shape
    count = model // quarter
    per_group = 2 * local
    blocks = [(side, g) for side in range(2) for g in range(k)]
    rows_each = len(blocks) * CAP

    def body(sc, *refs):
        x_ins, refs = refs[: 4 * k], refs[4 * k :]
        g_refs, refs = refs[:2], refs[2:]
        w_refs, refs = refs[: len(weights)], refs[len(weights) :]
        na_out, nb_out, ya_out, yb_out, h_out, d_out, go_out = refs[:7]
        st_ref, gate_ref, ns_ref, ys_ref, h_ref, d_ref, go_ref, g_held, w_held, x_held, sum_ref, sems = refs[7:]

        def weight(p, e, m):
            return w_held[3 * p + m, e]

        copies = (
            pltpu.make_async_copy(d_ref, d_out, sems.at[0]),
            pltpu.make_async_copy(go_ref, go_out, sems.at[1]),
        )
        hidden_copy = pltpu.make_async_copy(h_ref, h_out, sems.at[2])
        grad_copies = [
            pltpu.make_async_copy(g_refs[side].at[sc[1] ^ fars[g]], g_held.at[n], sems.at[3 + n])
            for n, (side, g) in enumerate(blocks)
        ]
        first_sem = 3 + len(blocks) + len(weights)
        row_copies = [
            pltpu.make_async_copy(x_ins[n], x_held.at[n], sems.at[first_sem + n])
            for n in range(4 * k)
        ]
        sum_copies = [
            pltpu.make_async_copy(sum_ref.at[n], out, sems.at[first_sem + 4 * k + n])
            for n, out in enumerate((na_out, nb_out, ya_out, yb_out))
        ]
        weight_copies = [
            pltpu.make_async_copy(w_refs[n], w_held.at[n], sems.at[3 + len(blocks) + n])
            for n in range(len(weights))
        ]
        for n in range(len(blocks)):
            for copy in (grad_copies[n], row_copies[2 * n], row_copies[2 * n + 1]):
                copy.start()
        for copy in weight_copies:
            copy.start()
        base = sc[1] * per_group + (sc[0] % 2) * local
        slot_row = lax.broadcasted_iota(jnp.int32, (CAP, tokens), 0).astype(F32)
        for n, (side, g) in enumerate(blocks):
            rows = slice(n * CAP, (n + 1) * CAP)
            grad_copies[n].wait()
            table = g_held[n, :, model : model + LANES].astype(F32).T
            ids, slots = table[:TOPK], table[TOPK : 2 * TOPK] - CAP
            gates = table[2 * TOPK : 3 * TOPK] + table[3 * TOPK : 4 * TOPK]
            picks = []
            for e in range(local):
                hit = ids == (base + e).astype(F32)
                slot = jnp.sum(jnp.where(hit, slots, 0.0), axis=0, keepdims=True) + CAP
                gate = jnp.sum(jnp.where(hit, gates, 0.0), axis=0, keepdims=True)
                pick = slot_row == slot
                value = jnp.sum(jnp.where(pick, gate, 0.0), axis=1, keepdims=True)
                gate_ref[e, rows, :] = jnp.broadcast_to(value, (CAP, LANES))
                picks.append(jnp.where(pick, 1.0, 0.0))
            row_copies[2 * n].wait()
            row_copies[2 * n + 1].wait()
            pick = jnp.concatenate(picks, axis=0)
            st_ref[n] = pick.T.astype(BF16)
            pick = pick.astype(BF16)
            for p in range(count):
                cols = columns(sc, p, quarter)
                values = jnp.concatenate(
                    [x_held[2 * n, :, cols], x_held[2 * n + 1, :, cols]], axis=0
                )
                got = dot_nn(pick, values).astype(BF16)
                grad = dot_nn(pick, g_held[n, :, cols])
                for e in range(local):
                    here = slice(e * CAP, (e + 1) * CAP)
                    d_ref[e, rows, p * quarter : (p + 1) * quarter] = got[here]
                    go_ref[e, rows, p * quarter : (p + 1) * quarter] = (
                        grad[here] * gate_ref[e, rows, 0:1]
                    ).astype(BF16)
        for copy in copies:
            copy.start()
        for copy in weight_copies:
            copy.wait()

        @pl.loop(0, local)
        def _(e):
            gate = up = act_grad = None
            for p in range(count):
                cols = slice(p * quarter, (p + 1) * quarter)
                rows = d_ref[e, :, cols]
                a = dot_nn(rows, weight(p, e, 0))
                b = dot_nn(rows, weight(p, e, 1))
                c = dot_nn(go_ref[e, :, cols], weight(p, e, 2))
                gate = a if gate is None else gate + a
                up = b if up is None else up + b
                act_grad = c if act_grad is None else act_grad + c
            sig = jax.nn.sigmoid(gate)
            silu = gate * sig
            act = (silu * up).astype(BF16)
            up_grad = (act_grad * silu).astype(BF16)
            gate_grad = (act_grad * up * sig * (1.0 + gate * (1.0 - sig))).astype(BF16)
            h_ref[e, :, :hidden] = act
            h_ref[e, :, hidden : 2 * hidden] = gate_grad
            h_ref[e, :, 2 * hidden :] = up_grad
            scale = gate_ref[e, :, 0:1]
            for p in range(count):
                cols = slice(p * quarter, (p + 1) * quarter)
                ns_ref[e, :, cols] = (
                    dot_nt(gate_grad, weight(p, e, 0)) + dot_nt(up_grad, weight(p, e, 1))
                ).astype(BF16)
                ys_ref[e, :, cols] = (dot_nt(act, weight(p, e, 2)) * scale).astype(BF16)

        hidden_copy.start()
        for at, source in ((0, ns_ref), (2, ys_ref)):
            for n, (side, g) in enumerate(blocks):
                rows = slice(n * CAP, (n + 1) * CAP)
                for p in range(count):
                    cols = slice(p * quarter, (p + 1) * quarter)
                    stacked = jnp.concatenate([source[e, rows, cols] for e in range(local)], axis=0)
                    sum_ref[at + side, g, :, columns(sc, p, quarter)] = dot_nn(
                        st_ref[n], stacked
                    ).astype(BF16)
                if g == k - 1:
                    sum_copies[at + side].start()
        for copy in (*copies, hidden_copy, *sum_copies):
            copy.wait()

    outside = pl.BlockSpec(memory_space=pltpu.HBM)
    sums = sds((k, tokens, model), BF16)
    rows = sds((local, rows_each, model), BF16)
    return pl.pallas_call(
        body,
        out_shape=[sums] * 4 + [sds((local, rows_each, 3 * hidden), BF16), rows, rows],
        grid_spec=pltpu.PrefetchScalarGridSpec(
            num_scalar_prefetch=1,
            grid=(1,),
            in_specs=[outside] * (4 * k + 2 + len(weights)),
            out_specs=[outside] * 7,
            scratch_shapes=[
                pltpu.VMEM((len(blocks), tokens, local * CAP), BF16),
                pltpu.VMEM((local, rows_each, LANES), F32),
                pltpu.VMEM((local, rows_each, model), BF16),
                pltpu.VMEM((local, rows_each, model), BF16),
                pltpu.VMEM((local, rows_each, 3 * hidden), BF16),
                pltpu.VMEM((local, rows_each, model), BF16),
                pltpu.VMEM((local, rows_each, model), BF16),
                pltpu.VMEM((len(blocks), tokens, model + LANES), BF16),
                pltpu.VMEM((len(weights), local, quarter, hidden), BF16),
                pltpu.VMEM((4 * k, half, model), BF16),
                pltpu.VMEM((4, k, tokens, model), BF16),
                pltpu.SemaphoreType.DMA((3 + len(blocks) + len(weights) + 4 * k + 4,)),
            ],
        ),
        compiler_params=params(58),
        cost_estimate=cost(
            2 * local * rows_each * model * (6 * hidden + 4 * tokens),
            2 * 3 * count * local * quarter * hidden + 24 * k * tokens * model,
            local * rows_each * hidden,
        ),
        name="experts",
    )(scalars, *rows_in, *grads_in, *weights)


def far_sets(local):
    mate = [(1, e) for e in range(local)]
    own = [(0, e) for e in range(local)]
    if local != 4:
        return [[v] for v in (*mate, *own)]
    return [mate[:1], mate[1:2], mate[2:] + own[:1], own[1:2], own[2:]]


def expert_weight_grads(row_sets, grad_sets, hidden_sets, quarter):
    groups = len(row_sets)
    local, _, model = row_sets[0].shape
    sets = far_sets(local)
    hidden = hidden_sets[0].shape[2] // 3
    count = model // quarter
    chunks, rows = [[]], 0
    for g in range(groups):
        if sum(row_sets[k].shape[1] for k in chunks[-1]) >= 8 * CAP:
            chunks.append([])
        chunks[-1].append(g)
        rows += row_sets[g].shape[1]

    def body(*refs):
        d_refs, go_refs, h_refs = refs[:groups], refs[groups : 2 * groups], refs[2 * groups : 3 * groups]
        keep_refs, far_refs = refs[3 * groups : 3 * groups + 2], refs[3 * groups + 2 :]
        expert = pl.program_id(0)
        far = []
        for p in range(count):
            cols = slice(p * quarter, (p + 1) * quarter)
            sums = [None, None, None]
            for chosen in chunks:
                left = jnp.concatenate([d_refs[g][0, :, cols] for g in chosen], axis=0)
                left_out = jnp.concatenate([go_refs[g][0, :, cols] for g in chosen], axis=0)
                right = jnp.concatenate([h_refs[g][0] for g in chosen], axis=0)
                parts = (
                    dot_tn(left, right[:, hidden : 2 * hidden]),
                    dot_tn(left, right[:, 2 * hidden :]),
                    dot_tn(left_out, right[:, :hidden]),
                )
                sums = [a if b is None else a + b for a, b in zip(parts, sums)]
            for k in range(3):
                if p < 2:
                    keep_refs[p][0, k] = sums[k]
                else:
                    far.append(sums[k].astype(BF16))
        for ref, chosen in zip(far_refs, sets):
            for n, (which, e) in enumerate(chosen):

                @pl.when(expert == e)
                def _():
                    for k in range(3):
                        ref[3 * n + k] = far[3 * which + k]

    by_expert = lambda shape: pl.BlockSpec((1,) + shape, lambda e: (e,) + (0,) * len(shape))
    fars = [(3 * len(chosen), quarter, hidden) for chosen in sets]
    return pl.pallas_call(
        body,
        out_shape=[sds((local, 3, quarter, hidden), F32)] * 2 + [sds(f, BF16) for f in fars],
        grid=(local,),
        in_specs=[by_expert(a.shape[1:]) for a in (*row_sets, *grad_sets, *hidden_sets)],
        out_specs=[by_expert((3, quarter, hidden))] * 2 + [whole(f) for f in fars],
        compiler_params=params(56),
        cost_estimate=cost(
            6 * local * rows * model * hidden,
            2 * local * rows * (2 * model + 3 * hidden) + 3 * local * 3 * model * hidden,
        ),
        name="expert_weight_grads",
    )(*row_sets, *grad_sets, *hidden_sets)


def middle_grad(scalars, parts, residual, grad_out, gains):
    tokens, model = grad_out.shape
    half = tokens // 2
    count = len(parts)

    def body(sc, *refs):
        part_refs = refs[:count]
        res_ref, go_ref, gain_ref, rg_ref, branch_ref, sum_ref = refs[count:]
        total = part_refs[0][...].astype(F32)
        for k in range(1, count):
            total = total + part_refs[k][...].astype(F32)
        residual = res_ref[...]
        start = pl.multiple_of(sc[2] * half, half)
        inverse = lax.rsqrt(jnp.mean(residual * residual, axis=-1, keepdims=True) + EPS)
        scaled = gain_ref[1:2, :] * total
        shift = jnp.mean(scaled * residual, axis=-1, keepdims=True)
        grad = (
            go_ref[pl.ds(start, half)].astype(F32)
            + inverse * scaled
            - residual * (inverse * inverse * inverse * shift)
        )
        rg_ref[...] = grad
        branch_ref[...] = grad.astype(BF16)
        sum_ref[...] = jnp.broadcast_to(
            jnp.sum(total * residual * inverse, axis=0, keepdims=True), (8, model)
        )

    return pl.pallas_call(
        body,
        out_shape=[sds((half, model), F32), sds((half, model), BF16), sds((8, model), F32)],
        grid_spec=pltpu.PrefetchScalarGridSpec(
            num_scalar_prefetch=1,
            grid=(1,),
            in_specs=[whole((half, model))] * (count + 1)
            + [whole((tokens, model)), whole((8, model))],
            out_specs=[whole((half, model)), whole((half, model)), whole((8, model))],
        ),
        compiler_params=params(12),
        cost_estimate=cost(20 * half * model, 24 * half * model),
        name="middle_grad",
    )(scalars, *parts, residual, grad_out, gains)


def attend_grad(scalars, branch, queries, kv_all, lse, out_pieces, cos_table, sin_table, piece_count):
    tokens, q_width = queries.shape
    length, kv2 = kv_all.shape
    kv_width = kv2 // 2
    kv_heads = kv_width // HEAD_DIM
    heads = q_width + kv2
    pair_blocks = kv_width // LANES
    count = len(out_pieces)
    quarter = out_pieces[0].shape[0]
    model = quarter * count
    half = tokens // 2

    def body(sc, b0_ref, b1_ref, q_ref, k_ref, v_ref, lse_ref, cos_ref, sin_ref, *rest):
        own = rows_at(sc[1], tokens)
        out_refs = rest[:count]
        dq_ref, dkv_ref, mg_ref, bias_ref = rest[count:]
        c = pl.program_id(0)

        @pl.when(c == 0)
        def _():
            cols = lax.broadcasted_iota(jnp.int32, (length, tokens), 0)
            rows = lax.broadcasted_iota(jnp.int32, (length, tokens), 1)
            query_pos = token_position(sc, rows, sc[1], tokens)
            key_pos = token_position(sc, cols % tokens, cols // tokens, tokens)
            bias_ref[...] = seen_bias(sc, query_pos, key_pos, piece_count)
            total = None
            for p in range(count):
                col = columns(sc, p, quarter)
                block = jnp.concatenate([b0_ref[:, col], b1_ref[:, col]], axis=0)
                part = dot_nn(block, out_refs[p][...])
                total = part if total is None else total + part
            mg_ref[...] = total.astype(BF16)

        low = lax.broadcasted_iota(jnp.int32, (1, LANES), 1) < HEAD_DIM
        mine = low == (c % 2 == 0)
        keys = k_ref[...].astype(F32)
        keys = jnp.where(mine, keys, pltpu.roll(keys, HEAD_DIM, 1)).astype(BF16)
        vals = v_ref[...].astype(F32)
        vals = jnp.where(mine, vals, pltpu.roll(vals, HEAD_DIM, 1)).astype(BF16)
        query = q_ref[...]
        grad = mg_ref[:, pl.ds(pl.multiple_of(c * LANES, LANES), LANES)]
        zero = jnp.zeros_like(query)
        lse_t = lse_ref[...].T
        dqs = []
        dk = dv = None
        for g in range(2):
            query_g = jnp.where(low, query, zero) if g == 0 else jnp.where(low, zero, query)
            grad_g = jnp.where(low, grad, zero) if g == 0 else jnp.where(low, zero, grad)
            scores = dot_nt(keys, query_g) + bias_ref[...]
            probs = jnp.exp(scores - lse_t[g * HEAD_DIM : g * HEAD_DIM + 1])
            prob_grad = dot_nt(vals, grad_g)
            delta = jnp.sum(probs * prob_grad, axis=0, keepdims=True)
            score_grad = (probs * (prob_grad - delta)).astype(BF16)
            dqs.append(dot_tn(score_grad, keys))
            dk_g = dot_nn(score_grad, query_g)
            dv_g = dot_nn(probs.astype(BF16), grad_g)
            dk = dk_g if dk is None else dk + dk_g
            dv = dv_g if dv is None else dv + dv_g
        dq = jnp.where(low, dqs[0], dqs[1]) * HEAD_DIM**-0.5
        dq_ref[...] = turn(dq, cos_ref[own], -sin_ref[own]).astype(BF16)
        dk = turn(dk, cos_ref[...], -sin_ref[...])
        for k, value in ((0, dk), (pair_blocks, dv)):
            value = (value + pltpu.roll(value, HEAD_DIM, 1)).astype(BF16)
            where = pl.ds(pl.multiple_of((k + c // 2) * LANES, LANES), LANES)
            dkv_ref[:, where] = jnp.where(mine, value, dkv_ref[:, where])

    return pl.pallas_call(
        body,
        out_shape=[sds((tokens, q_width), BF16), sds((length, kv2), BF16)],
        grid_spec=pltpu.PrefetchScalarGridSpec(
            num_scalar_prefetch=1,
            grid=(kv_heads,),
            in_specs=[
                whole((half, model)),
                whole((half, model)),
                pl.BlockSpec((tokens, LANES), lambda c, sc: (0, c)),
                pl.BlockSpec((length, LANES), lambda c, sc: (0, c // 2)),
                pl.BlockSpec((length, LANES), lambda c, sc: (0, pair_blocks + c // 2)),
                pl.BlockSpec((tokens, LANES), lambda c, sc: (0, c)),
                whole((length, LANES)),
                whole((length, LANES)),
            ]
            + [pl.BlockSpec((quarter, q_width), lambda c, sc: (0, heads // q_width))] * count,
            out_specs=[
                pl.BlockSpec((tokens, LANES), lambda c, sc: (0, c)),
                whole((length, kv2)),
            ],
            scratch_shapes=[
                pltpu.VMEM((tokens, q_width), BF16),
                pltpu.VMEM((length, tokens), F32),
            ],
        ),
        compiler_params=params(58),
        cost_estimate=cost(
            40 * tokens * length * LANES + 2 * tokens * q_width * model,
            6 * length * kv2 + 8 * tokens * model,
            2 * kv_heads * tokens * length,
        ),
        name="attend_grad",
    )(scalars, *branch, queries, kv_all, kv_all, lse, cos_table, sin_table, *out_pieces)


def weight_grads(scalars, normed, dq, dkv, branch, mixed, extra, quarter):
    length, model = normed.shape
    tokens, q_width = dq.shape
    kv2 = dkv.shape[1]
    width = q_width + kv2 + mixed.shape[1]
    count = model // quarter
    outs = [((quarter, width + LANES), F32)] * 2 + [((2, quarter, width + LANES), BF16)]

    def body(sc, xn_ref, dq_ref, dkv_ref, b0_ref, b1_ref, mixed_ref, extra_ref, *out_refs):
        own = rows_at(sc[1], tokens)
        rows = lax.broadcasted_iota(jnp.int32, (quarter, quarter), 0)
        diagonal = rows == lax.broadcasted_iota(jnp.int32, (quarter, quarter), 1)
        for p in range(count):
            cols = columns(sc, p, quarter)
            ref = (out_refs[0], None, out_refs[1], None)[p]
            block = jnp.concatenate([b0_ref[:, cols], b1_ref[:, cols]], axis=0)
            column = jnp.sum(jnp.where(diagonal, extra_ref[0:1, cols], 0.0), axis=1, keepdims=True)
            at = 0
            for value in (
                dot_tn(xn_ref[own, cols], dq_ref[...]),
                dot_tn(xn_ref[:, cols], dkv_ref[...]),
                dot_tn(block, mixed_ref[...]),
                jnp.broadcast_to(column, (quarter, LANES)),
            ):
                here = slice(at, at + value.shape[1])
                at += value.shape[1]
                if ref is not None:
                    ref[:, here] = value
                else:
                    out_refs[2][p // 2, :, here] = value.astype(BF16)

    arrays = (normed, dq, dkv, *branch, mixed, extra)
    return pl.pallas_call(
        body,
        out_shape=[sds(*o) for o in outs],
        grid_spec=pltpu.PrefetchScalarGridSpec(
            num_scalar_prefetch=1,
            grid=(1,),
            in_specs=[whole(a.shape) for a in arrays],
            out_specs=[whole(o[0]) for o in outs],
        ),
        compiler_params=params(58),
        cost_estimate=cost(
            2 * model * (tokens * (q_width + mixed.shape[1]) + length * kv2),
            2 * length * (model + kv2) + 3 * model * width,
        ),
        name="weight_grads",
    )(scalars, *arrays)


def gather_expert_grads(scalars, keep, far, mates, sent):
    local, _, quarter, hidden = keep.shape
    sets = far_sets(local)
    chosen = range(len(sets) - len(far), len(sets)) if sent is not None else range(len(far))
    places = [
        (i, 3 * k, v[1])
        for i, n in enumerate(chosen)
        for k, v in enumerate(sets[n])
        if v[0] == 0
    ]
    used = sorted({i for i, _, _ in places})
    experts_here = [e for _, _, e in places]
    lowest = min(experts_here) if experts_here else 0
    count = len(experts_here)
    held = [] if sent is None else [sent]
    mates_here = [] if mates is None else [mates]
    steps = count + (local if mates_here else 0)

    def place(step, sc):
        core = sc[0] % 2
        mine = core * local + lowest + step
        return jnp.where(step < count, mine, (1 - core) * local + step - count)

    def body(sc, keep_ref, *rest):
        far_refs, out_ref = dict(zip(used, rest)), rest[-1]
        step = pl.program_id(0)
        for i, start, expert in places:

            @pl.when(step == expert - lowest)
            def _():
                out_ref[0] = keep_ref[0] + far_refs[i][start : start + 3].astype(F32)

        if mates_here:

            @pl.when(step >= count)
            def _():
                out_ref[0] = rest[len(used)][0].astype(F32)

    block = (1, 3, quarter, hidden)
    own = lambda step, sc: (lowest + jnp.minimum(step, max(count - 1, 0)), 0, 0, 0)
    other = lambda step, sc: (jnp.maximum(step - count, 0), 0, 0, 0)
    arrays = [keep, *[far[i] for i in used], *mates_here, *held]
    return pl.pallas_call(
        body,
        out_shape=sds((2 * local, 3, quarter, hidden), F32),
        grid_spec=pltpu.PrefetchScalarGridSpec(
            num_scalar_prefetch=1,
            grid=(steps,),
            in_specs=[pl.BlockSpec(block, own)]
            + [whole(far[i].shape) for i in used]
            + [pl.BlockSpec(block, other)] * len(mates_here)
            + [pl.BlockSpec(memory_space=pl.ANY)] * len(held),
            out_specs=pl.BlockSpec(block, lambda step, sc: (place(step, sc), 0, 0, 0)),
        ),
        input_output_aliases={len(arrays): 0} if held else {},
        compiler_params=params(24),
        cost_estimate=cost(3 * steps * quarter * hidden, 3 * 10 * steps * quarter * hidden),
        name="gather_expert_grads",
    )(scalars, *arrays)


def back(scalars, dq, dkv, pieces):
    tokens, q_width = dq.shape
    groups, _, kv2 = dkv.shape
    heads = q_width + kv2
    count = len(pieces)
    quarter = pieces[0].shape[0]
    model = count * quarter
    half = tokens // 2

    def body(sc, dq_ref, dkv_ref, *rest):
        piece_refs = rest[:count]
        own_ref, send_ref = rest[count:]
        total = dkv_ref[0].astype(F32)
        for g in range(1, groups):
            total = total + dkv_ref[g].astype(F32)
        dl_kv = total.astype(BF16)
        dl_q = dq_ref[...]
        for p in range(count):
            cols = columns(sc, p, quarter)
            part = dot_nt(dl_q, piece_refs[p][:, :q_width]) + dot_nt(
                dl_kv, piece_refs[p][:, q_width:heads]
            )
            own_ref[:, cols] = part[:half]
            send_ref[:, cols] = part[half:].astype(BF16)

    arrays = (dq, dkv, *pieces)
    return pl.pallas_call(
        body,
        out_shape=[sds((half, model), F32), sds((half, model), BF16)],
        grid_spec=pltpu.PrefetchScalarGridSpec(
            num_scalar_prefetch=1,
            grid=(1,),
            in_specs=[whole(dq.shape), whole(dkv.shape)] + [whole((quarter, heads))] * count,
            out_specs=[whole((half, model))] * 2,
        ),
        compiler_params=params(58),
        cost_estimate=cost(2 * tokens * model * heads, 2 * model * (heads + 2 * tokens)),
        name="back",
    )(scalars, *arrays)


def last_grad(scalars, layer_input, own, received, residual_grad, gains):
    tokens, model = layer_input.shape
    half = tokens // 2

    def body(sc, x_ref, own_ref, rec_ref, rg_ref, gain_ref, out_ref):
        start = pl.multiple_of(sc[2] * half, half)
        values = x_ref[pl.ds(start, half)].astype(F32)
        inverse = lax.rsqrt(jnp.mean(values * values, axis=-1, keepdims=True) + EPS)
        scaled = gain_ref[0:1, :] * (own_ref[...] + rec_ref[...].astype(F32))
        shift = jnp.mean(scaled * values, axis=-1, keepdims=True)
        out_ref[...] = (
            rg_ref[...] + inverse * scaled - values * (inverse * inverse * inverse * shift)
        ).astype(BF16)

    return pl.pallas_call(
        body,
        out_shape=sds((half, model), BF16),
        grid_spec=pltpu.PrefetchScalarGridSpec(
            num_scalar_prefetch=1,
            grid=(1,),
            in_specs=[
                whole((tokens, model)),
                whole((half, model)),
                whole((half, model)),
                whole((half, model)),
                whole((8, model)),
            ],
            out_specs=whole((half, model)),
        ),
        compiler_params=params(8),
        cost_estimate=cost(12 * half * model, 14 * half * model),
        name="last_grad",
    )(scalars, layer_input, own, received, residual_grad, gains)


def local(
    layer_input,
    attn_norm,
    w_query,
    w_key,
    w_value,
    w_out,
    moe_norm,
    expert_weights,
    expert_ids,
    slot_ids,
    gate_values,
    piece_starts,
    grad_out,
):
    _, tokens, model = layer_input.shape
    half = tokens // 2
    groups = lax.axis_size("ctx")
    shard = lax.axis_index("shard")
    group = lax.axis_index("ctx")
    side = lax.axis_index("tp")
    piece_count = piece_starts.shape[1]
    scalars = jnp.concatenate(
        [jnp.stack([shard, group, side]).astype(jnp.int32), piece_starts[0]]
    )
    flat_input = layer_input[0]
    flat_grad = grad_out[0]
    q_width, kv_width = w_query.shape[1], w_key.shape[1]
    rows_here = w_query.shape[0]
    quarter = rows_here * groups

    weight_block = jnp.concatenate(
        [
            w_query,
            w_key,
            w_value,
            w_out.T,
            attn_norm[:, None],
            moe_norm[:, None],
            jnp.zeros((rows_here, LANES - 2), BF16),
        ],
        axis=1,
    )
    own_input = jnp.where(side == 0, flat_input[:half], flat_input[half:])
    local_experts = expert_weights.shape[0] // 2
    core = shard % 2


    def experts_of(which, m):
        start = (which * local_experts, m, 0, 0)
        size = (local_experts, 1) + expert_weights.shape[2:]
        return lax.dynamic_slice(expert_weights, start, size)[:, 0]

    mine = [experts_of(core, m) for m in range(3)]
    given = [experts_of(1 - core, m) for m in range(3)]

    index = jnp.arange(groups * tokens, dtype=jnp.int32)
    positions = (index ^ (side * half).astype(jnp.int32)).astype(F32)
    lane = jnp.arange(LANES, dtype=jnp.int32)
    step = (lane % (HEAD_DIM // 2)).astype(F32)
    angles = positions[:, None] * (1.0 / 10000.0 ** (step * 2.0 / HEAD_DIM))[None, :]
    cos_table = jnp.cos(angles)
    sin_table = jnp.sin(angles) * jnp.where(lane % HEAD_DIM < HEAD_DIM // 2, -1.0, 1.0)[None, :]

    gate_high = gate_values[0].astype(BF16)
    gate_low = (gate_values[0] - gate_high.astype(F32)).astype(BF16)
    routing = jnp.concatenate(
        [
            expert_ids[0].astype(BF16),
            slot_ids[0].astype(BF16),
            gate_high,
            gate_low,
            jnp.zeros((tokens, LANES - 4 * TOPK), BF16),
        ],
        axis=1,
    )
    grad_block = spread_grads(scalars, flat_grad, routing, groups)

    near = [1, 3] if groups == 4 else [1]
    rest = [b for b in range(1, groups) if b not in near]
    block_0, own_input, cos_table, sin_table, grad_block, far_0, *kept = fence(
        spread(weight_block, "ctx").reshape(quarter, -1),
        own_input,
        cos_table,
        sin_table,
        grad_block,
        swap(mine[0], "shard", 2),
        *mine,
        *given,
        *[swap(own_input, "ctx", b) for b in near],
    )
    mine, given = kept[:3], kept[3:6]
    input_at = dict(zip(near, kept[6:]))
    block_0, block_2, *kept = fence(
        block_0,
        swap(block_0, "shard", 2),
        *[swap(input_at[b], "tp", 1) for b in near],
        *[swap(own_input, "ctx", b) for b in rest],
    )
    crossed = dict(zip(near, kept[: len(near)]))
    input_at.update(dict(zip(rest, kept[len(near) :])))
    grads_own = lax.all_to_all(after(grad_block, block_2), "ctx", 0, 0, tiled=True)
    block_0, block_1, block_2, block_3, taken_0, far_1, *kept = fence(
        block_0,
        swap(block_0, "shard", 1),
        block_2,
        swap(block_2, "shard", 1),
        swap(after(given[0], block_2), "shard", 1),
        swap(after(mine[1], block_2), "shard", 2),
        *[swap(input_at[b], "tp", 1) for b in rest],
    )
    crossed.update(dict(zip(rest, kept)))
    pieces = [block_0, block_1, block_2, block_3]
    others = [v for b in range(1, groups) for v in (input_at[b], crossed[b])]

    normed_all, queries, kv_all, gains = front(
        scalars, flat_input, others, pieces, cos_table, sin_table, (q_width, kv_width)
    )
    mixed, lse, attention_own, attention_send = attend(
        scalars, queries, kv_all, pieces, piece_count
    )
    attention_send, far_2, far_3, taken_2, taken_1 = fence(
        attention_send,
        swap(after(mine[2], block_1), "shard", 2),
        swap(after(taken_0, block_1), "shard", 2),
        swap(after(given[2], block_1), "shard", 1),
        swap(after(given[1], block_1), "shard", 1),
    )
    attention_got, far_4 = fence(
        swap(attention_send, "tp", 1), swap(after(taken_1, attention_send), "shard", 2)
    )
    residual, normed_two = second_norm(
        scalars, flat_input, attention_own, attention_got, gains
    )

    calls = [[0], *[[b, b + 1] for b in range(1, groups - 1, 2)], [groups - 1]]
    far_5 = swap(after(taken_2, far_4), "shard", 2)
    grads_own = after(grads_own, residual)
    normed_two, crossed, grads_own, grads_mate, far_5, *arrived = fence(
        normed_two,
        swap(normed_two, "tp", 1),
        grads_own,
        swap(grads_own, "shard", 1),
        far_5,
        *[swap(normed_two, "ctx", b) for b in calls[1]],
    )
    tokens_at = {0: normed_two, **dict(zip(calls[1], arrived))}
    grads_in = [grads_own, grads_mate]
    taken = [taken_0, taken_1, taken_2]
    expert_pieces = [*mine, *taken, far_0, far_1, far_2, far_3, far_4, far_5]
    rows_in = [normed_two, crossed, swap(normed_two, "shard", 1), swap(crossed, "shard", 1)]

    def summed(own, got, part):
        return own[:, part].astype(F32) + got[:, part].astype(F32)

    low, high = slice(0, half), slice(half, tokens)
    row_sets, grad_sets, hidden_sets = [], [], []
    norm_parts, out_parts, out_sets = {}, {}, []
    waiting = None
    order = scalars
    for n, call in enumerate(calls):
        own, mate, out_own, out_mate, hiddens, rows, grads = experts(
            order, call, rows_in, grads_in, expert_pieces
        )
        row_sets.append(rows)
        grad_sets.append(grads)
        hidden_sets.append(hiddens)
        out_sets.append((call, out_own, out_mate))
        later = calls[n + 1] if n + 1 < len(calls) else []
        latest = calls[n + 2] if n + 2 < len(calls) else []
        own, mate, *arrived = fence(
            own,
            mate,
            *[swap(tokens_at[b], "tp", 1) for b in later],
            *[swap(tokens_at[b], "shard", 1) for b in later],
            *[swap(normed_two, "ctx", b) for b in latest],
            *([waiting[3]] if waiting is not None else []),
        )
        crossed, arrived = arrived[: len(later)], arrived[len(later) :]
        mates, arrived = arrived[: len(later)], arrived[len(later) :]
        tokens_at.update(dict(zip(latest, arrived)))
        if later:
            here = [v for b, c in zip(later, crossed) for v in (tokens_at[b], c)]
            there = [v for m, c in zip(mates, crossed) for v in (m, swap(c, "shard", 1))]
            rows_in = [*here, *there]
        got = swap(mate, "shard", 1)
        sent = summed(own, got, high).astype(BF16)
        if waiting is not None:
            old_call, kept_own, old_got, _ = waiting
            kept = summed(after(kept_own, sent), old_got, low) + arrived[-1].astype(F32)
            for i, b in enumerate(old_call):
                norm_parts[b] = kept[i] if b == 0 else swap(kept[i].astype(BF16), "ctx", b)
        waiting = (call, own, got, swap(sent, "tp", 1))
        order = after(scalars, sent)

    hidden_sets[-1] = after(hidden_sets[-1], sent)
    call, own, got, crossed = waiting
    early = [b for b in norm_parts if b > 0]
    mates = [swap(after(s[2], sent), "shard", 1) for s in out_sets[:-1]]
    keep_0, keep_1, *arrived = fence(
        *expert_weight_grads(row_sets, grad_sets, hidden_sets, quarter),
        crossed,
        *[norm_parts[b] for b in early],
        *mates,
    )
    fars = len(arrived) - 1 - len(early) - len(mates)
    far_sent, crossed, arrived = arrived[:fars], arrived[fars], arrived[fars + 1 :]
    far_got = []

    def send_far(count, *ready):
        start = len(far_got)
        got = [swap(after(v, *ready), "shard", 2) for v in far_sent[start : start + count]]
        far_got.extend(got)
        return got

    def keep_far(got):
        if got:
            far_got[len(far_got) - len(got) :] = got

    norm_parts.update(dict(zip(early, arrived)))
    mates = arrived[len(early) :]
    kept = summed(own, got, low) + crossed.astype(F32)
    for i, b in enumerate(call):
        norm_parts[b] = swap(kept[i].astype(BF16), "ctx", b)

    outs = [(s[0], after(s[1], kept), m) for s, m in zip(out_sets, mates)]
    middle, edges = outs[1:], outs[:1]
    out_crossed = [swap(summed(own, got, high).astype(BF16), "tp", 1) for _, own, got in middle]
    out_last = swap(after(out_sets[-1][2], kept), "shard", 1)
    sending = send_far(1, crossed)
    residual, out_last, *arrived = fence(
        residual, out_last, *[norm_parts[b] for b in range(groups)], *sending, *out_crossed
    )
    keep_far(arrived[groups : groups + len(sending)])
    out_crossed = arrived[groups + len(sending) :]
    arrived = arrived[:groups]
    residual_grad, branch_own, gain_row = middle_grad(
        scalars, arrived, residual, flat_grad, gains
    )
    sending = send_far(1, out_last)
    branch_own, branch_crossed, *sending = fence(branch_own, swap(branch_own, "tp", 1), *sending)
    keep_far(sending)
    branch = [branch_own, branch_crossed]
    for (call, own, got), crossed in zip(middle, out_crossed):
        kept = summed(after(own, branch_own), got, low) + crossed.astype(F32)
        for i, b in enumerate(call):
            out_parts[b] = swap(fence(kept[i].astype(BF16))[0], "ctx", b)
    moved = list(out_parts)
    edges.append((*out_sets[-1][:2], out_last))
    edges = [(call, after(own, branch_own), got) for call, own, got in edges]
    out_crossed = [swap(summed(own, got, high).astype(BF16), "tp", 1) for _, own, got in edges]

    dq, dkv_parts = attend_grad(
        scalars, branch, queries, kv_all, lse, pieces, cos_table, sin_table, piece_count
    )
    sending = send_far(1, branch_crossed)
    dq, dkv_parts, out_first, out_last, *arrived = fence(
        dq, dkv_parts, *out_crossed, *[out_parts[b] for b in moved], *sending
    )
    out_crossed = [out_first, out_last]
    out_parts.update(dict(zip(moved, arrived)))
    keep_far(arrived[len(moved) :])

    for (call, own, got), crossed in zip(edges, out_crossed):
        kept = summed(after(own, dq), got, low) + crossed.astype(F32)
        for i, b in enumerate(call):
            out_parts[b] = kept[i] if b == 0 else swap(fence(kept[i].astype(BF16))[0], "ctx", b)
    sending = send_far(1, dq)
    own_grads, far_grads, sent_grads, dkv_parts, *arrived = fence(
        *weight_grads(scalars, normed_all, dq, dkv_parts, branch, mixed, gain_row, quarter),
        dkv_parts,
        *[out_parts[b] for b in calls[-1]],
        *sending,
    )
    out_parts.update(dict(zip(calls[-1], arrived)))
    keep_far(arrived[len(calls[-1]) :])

    got_grads = fence(swap(sent_grads, "shard", 1))[0]
    passed = (far_grads + got_grads[1].astype(F32)).astype(BF16)
    dkv, passed, own_grads, got_grads = fence(
        lax.all_to_all(
            dkv_parts.reshape(groups, tokens, 2 * kv_width), "ctx", 0, 0, tiled=True
        ),
        swap(passed, "shard", 2),
        own_grads,
        got_grads,
    )

    total = fence((own_grads + got_grads[0].astype(F32) + passed.astype(F32)).astype(BF16))[0]
    normed_own, normed_send = back(scalars, dq, dkv, pieces)
    input_half = last_grad(
        scalars, flat_input, normed_own, swap(normed_send, "tp", 1), residual_grad, gains
    )
    places = {
        v[1]: (n, 3 * k)
        for n, chosen in enumerate(far_sets(local_experts))
        for k, v in enumerate(chosen)
        if v[0] == 1
    }
    mates = jnp.stack(
        [
            (keep_1[e] + far_got[n][start : start + 3].astype(F32)).astype(BF16)
            for e, (n, start) in sorted(places.items())
        ]
    )
    out_sum = after(residual, dkv)
    for b in range(groups):
        out_sum = out_sum + out_parts[b].astype(F32)
    out_half = out_sum.astype(BF16)
    def natural(own, other):
        return jnp.where(
            side == 0,
            jnp.concatenate([own, other], axis=0),
            jnp.concatenate([other, own], axis=0),
        )[None]

    early = list(far_got)
    sending = send_far(len(far_sent), dkv)
    expert_grad = gather_expert_grads(scalars, keep_0, early, swap(mates, "shard", 1), None)
    total, input_half, input_other, output, expert_grad, *sending = fence(
        lax.all_to_all(
            total.reshape(groups, rows_here, total.shape[1]), "ctx", 0, 0, tiled=True
        ),
        input_half,
        swap(input_half, "tp", 1),
        natural(out_half, swap(out_half, "tp", 1)),
        expert_grad,
        *sending,
    )
    keep_far(sending)
    input_grad = natural(input_half, input_other)
    if sending:
        expert_grad = gather_expert_grads(scalars, keep_0, sending, None, expert_grad)
    total = jnp.sum(total.astype(F32), axis=0)
    query_grad = total[:, :q_width]
    key_grad = total[:, q_width : q_width + kv_width]
    value_grad = total[:, q_width + kv_width : q_width + 2 * kv_width]
    heads = q_width + 2 * kv_width
    out_grad = total[:, heads : heads + q_width].T
    moe_sum = total[:, heads + q_width]
    attn_sum = (
        jnp.sum(w_query.astype(F32) * query_grad, axis=1)
        + jnp.sum(w_key.astype(F32) * key_grad, axis=1)
        + jnp.sum(w_value.astype(F32) * value_grad, axis=1)
    )
    sums = jnp.stack([attn_sum, moe_sum])
    attn_sum, moe_norm_grad = sums + swap(sums, "tp", 1)
    attn_norm_grad = attn_sum / attn_norm.astype(F32)
    return (
        output,
        input_grad,
        attn_norm_grad,
        query_grad,
        key_grad,
        value_grad,
        out_grad,
        moe_norm_grad,
        expert_grad,
    )


def solution(mesh):
    in_specs = (
        P("shard", "ctx", None),
        P(("shard", "ctx")),
        P(("shard", "ctx"), "tp"),
        P(("shard", "ctx"), "tp"),
        P(("shard", "ctx"), "tp"),
        P("tp", ("shard", "ctx")),
        P(("shard", "ctx")),
        P("ctx", None, "shard", "tp"),
        P("shard", "ctx", None),
        P("shard", "ctx", None),
        P("shard", "ctx", None),
        P("shard", None),
        P("shard", "ctx", None),
    )
    out_specs = (
        P("shard", "ctx", None),
        P("shard", "ctx", None),
        P(("shard", "ctx")),
        P(("shard", "ctx"), "tp"),
        P(("shard", "ctx"), "tp"),
        P(("shard", "ctx"), "tp"),
        P("tp", ("shard", "ctx")),
        P(("shard", "ctx")),
        P("ctx", None, "shard", "tp"),
    )
    return jax.shard_map(local, mesh=mesh, in_specs=in_specs, out_specs=out_specs, check_vma=False)
```

```python
import functools

import jax
import jax.numpy as jnp
from jax import lax
from jax.experimental import pallas as pl
from jax.experimental.pallas import tpu as pltpu
from jax.sharding import PartitionSpec as P

HEAD_DIM = 64
EXPERTS = 32
TOPK = 8
PIECE = 256
CAP = 96
EPS = 1e-06
MASKED = -1e30
LANES = 128
F32 = jnp.float32
BF16 = jnp.bfloat16


def swap(value, axis, distance):
    size = lax.axis_size(axis)
    return lax.ppermute(value, axis, [(i, i ^ distance) for i in range(size)])


def spread(value, axis):
    size = lax.axis_size(axis)
    copies = jnp.broadcast_to(value[None], (size,) + value.shape)
    return lax.all_to_all(copies, axis, 0, 0, tiled=True)


def after(value, *others):
    return lax.optimization_barrier((value,) + others)[0]


def fence(*values):
    return lax.optimization_barrier(values)


def dot_nn(a, b):
    return lax.dot_general(a, b, (((1,), (0,)), ((), ())), preferred_element_type=F32)


def dot_nt(a, b):
    return lax.dot_general(a, b, (((1,), (1,)), ((), ())), preferred_element_type=F32)


def dot_tn(a, b):
    return lax.dot_general(a, b, (((0,), (0,)), ((), ())), preferred_element_type=F32)


def cost(flops, moved, special=0):
    return pl.CostEstimate(flops=int(flops), bytes_accessed=int(moved), transcendentals=int(special))


def params(megabytes, length=0):
    megabytes = 58 if length > 1024 else megabytes
    return pltpu.CompilerParams(vmem_limit_bytes=megabytes * 1024 * 1024)


def sds(shape, dtype):
    return jax.ShapeDtypeStruct(shape, dtype)


def whole(shape):
    return pl.BlockSpec(shape, lambda *_: (0,) * len(shape))


def turn(value, cosine, sine):
    lane = lax.broadcasted_iota(jnp.int32, (value.shape[0], LANES), 1) % HEAD_DIM
    first = lane < HEAD_DIM // 2
    parts = []
    for j in range(value.shape[1] // LANES):
        chunk = value[:, j * LANES : (j + 1) * LANES]
        partner = jnp.where(
            first,
            pltpu.roll(chunk, LANES - HEAD_DIM // 2, 1),
            pltpu.roll(chunk, HEAD_DIM // 2, 1),
        )
        parts.append(chunk * cosine + partner * sine)
    return parts[0] if len(parts) == 1 else jnp.concatenate(parts, axis=1)


def rows_at(index, size):
    return pl.ds(pl.multiple_of(index * size, size), size)


def columns(scalars, p, width):
    return pl.ds(pl.multiple_of((scalars[0] ^ p) * width, width), width)


def spread_grads(scalars, grads, routing, groups):
    tokens, model = grads.shape
    half = tokens // 2
    out = (groups, tokens, model + LANES)

    def body(sc, grads_ref, routing_ref, out_ref):
        for h in range(2):
            here = rows_at(sc[2] ^ h, half)
            out_ref[0, h * half : (h + 1) * half, :model] = grads_ref[here]
            out_ref[0, h * half : (h + 1) * half, model:] = routing_ref[here]

    return pl.pallas_call(
        body,
        out_shape=sds(out, BF16),
        grid_spec=pltpu.PrefetchScalarGridSpec(
            num_scalar_prefetch=1,
            grid=(groups,),
            in_specs=[whole(grads.shape), whole(routing.shape)],
            out_specs=pl.BlockSpec((1,) + out[1:], lambda g, sc: (g, 0, 0)),
        ),
        compiler_params=params(12),
        cost_estimate=cost(0, 2 * (groups + 1) * tokens * (model + LANES)),
        name="spread_grads",
    )(scalars, grads, routing)


def front(scalars, layer_input, others, pieces, cos_table, sin_table, widths):
    tokens, model = layer_input.shape
    quarter = pieces[0].shape[0]
    q_width, kv_width = widths
    heads = q_width + 2 * kv_width
    gain_column = pieces[0].shape[1] - LANES
    half = tokens // 2
    count = len(pieces)
    groups = 1 + len(others) // 2
    length = groups * tokens

    def body(sc, x_ref, *rest):
        other_refs, rest = rest[: len(others)], rest[len(others) :]
        piece_refs = rest[:count]
        cos_ref, sin_ref, xn_ref, q_ref, kv_ref, gain_ref = rest[count:]
        rows = lax.broadcasted_iota(jnp.int32, (quarter, quarter), 0)
        diagonal = rows == lax.broadcasted_iota(jnp.int32, (quarter, quarter), 1)
        for p in range(count):
            gains = piece_refs[p][:, gain_column : gain_column + LANES].astype(F32)
            for k in range(2):
                row = jnp.sum(jnp.where(diagonal, gains[:, k : k + 1], 0.0), axis=0, keepdims=True)
                gain_ref[k : k + 1, columns(sc, p, quarter)] = row
        gain = gain_ref[0:1, :]
        for b in range(groups):
            for h in range(2):
                if b == 0:
                    values = x_ref[rows_at(sc[2] ^ h, half)].astype(F32)
                else:
                    values = other_refs[2 * (b - 1) + h][...].astype(F32)
                inverse = lax.rsqrt(jnp.mean(values * values, axis=-1, keepdims=True) + EPS)
                xn_ref[rows_at(2 * (sc[1] ^ b) + h, half)] = (values * inverse * gain).astype(BF16)

        own = rows_at(sc[1], tokens)
        total = None
        for p in range(count):
            part = dot_nn(xn_ref[own, columns(sc, p, quarter)], piece_refs[p][:, :q_width])
            total = part if total is None else total + part
        total = turn(total, cos_ref[own], sin_ref[own]).astype(BF16)
        q_ref[...] = (total * HEAD_DIM**-0.5).astype(BF16)

        @pl.loop(0, groups)
        def _(g):
            here = rows_at(g, tokens)
            total = None
            for p in range(count):
                part = dot_nn(xn_ref[here, columns(sc, p, quarter)], piece_refs[p][:, q_width:heads])
                total = part if total is None else total + part
            kv_ref[here, :kv_width] = turn(total[:, :kv_width], cos_ref[here], sin_ref[here]).astype(
                BF16
            )
            kv_ref[here, kv_width:] = total[:, kv_width:].astype(BF16)

    outs = [
        ((length, model), BF16),
        ((tokens, q_width), BF16),
        ((length, 2 * kv_width), BF16),
        ((8, model), F32),
    ]
    arrays = (layer_input, *others, *pieces, cos_table, sin_table)
    return pl.pallas_call(
        body,
        out_shape=[sds(*o) for o in outs],
        grid_spec=pltpu.PrefetchScalarGridSpec(
            num_scalar_prefetch=1,
            grid=(1,),
            in_specs=[whole(a.shape) for a in arrays],
            out_specs=[whole(o[0]) for o in outs],
        ),
        compiler_params=params(58),
        cost_estimate=cost(
            2 * model * (tokens * q_width + length * 2 * kv_width),
            2 * model * (2 * length + heads) + 2 * length * (kv_width + 2 * LANES),
        ),
        name="front",
    )(scalars, *arrays)


def inside_piece(position, start):
    return (position >= start) & (position < start + PIECE)


def seen_bias(sc, query_pos, key_pos, piece_count):
    seen = key_pos <= query_pos
    for k in range(piece_count):
        start = sc[3 + k]
        seen = seen | (inside_piece(query_pos, start) & inside_piece(key_pos, start))
    return jnp.where(seen, 0.0, MASKED)


def token_position(sc, index, group, tokens):
    return group * tokens + (index ^ (sc[2] * (tokens // 2)))


def attend(scalars, queries, kv_all, out_pieces, piece_count):
    tokens, q_width = queries.shape
    length, kv2 = kv_all.shape
    kv_width = kv2 // 2
    kv_heads = kv_width // HEAD_DIM
    heads = q_width + kv2
    pair_blocks = kv_width // LANES
    count = len(out_pieces)
    quarter = out_pieces[0].shape[0]
    model = quarter * count
    half = tokens // 2

    def body(sc, q_ref, k_ref, v_ref, *rest):
        out_refs = rest[:count]
        mixed_ref, lse_ref, own_ref, send_ref, bias_ref = rest[count:]
        c = pl.program_id(0)

        @pl.when(c == 0)
        def _():
            rows = lax.broadcasted_iota(jnp.int32, (tokens, length), 0)
            cols = lax.broadcasted_iota(jnp.int32, (tokens, length), 1)
            query_pos = token_position(sc, rows, sc[1], tokens)
            key_pos = token_position(sc, cols % tokens, cols // tokens, tokens)
            bias_ref[...] = seen_bias(sc, query_pos, key_pos, piece_count)

        low = lax.broadcasted_iota(jnp.int32, (1, LANES), 1) < HEAD_DIM
        mine = low == (c % 2 == 0)
        keys = k_ref[...].astype(F32)
        keys = jnp.where(mine, keys, pltpu.roll(keys, HEAD_DIM, 1)).astype(BF16)
        vals = v_ref[...].astype(F32)
        vals = jnp.where(mine, vals, pltpu.roll(vals, HEAD_DIM, 1)).astype(BF16)
        query = q_ref[...]
        zero = jnp.zeros_like(query)
        outs, lses = [], []
        for part in (jnp.where(low, query, zero), jnp.where(low, zero, query)):
            scores = dot_nt(part, keys) + bias_ref[...]
            top = jnp.max(scores, axis=-1, keepdims=True)
            expo = jnp.exp(scores - top)
            total = jnp.sum(expo, axis=-1, keepdims=True)
            probs = expo * (1.0 / total)
            outs.append(dot_nn(probs.astype(BF16), vals))
            lses.append(top + jnp.log(total))
        mixed_ref[:, pl.ds(pl.multiple_of(c * LANES, LANES), LANES)] = jnp.where(
            low, outs[0], outs[1]
        ).astype(BF16)
        lse_ref[...] = jnp.where(low, lses[0], lses[1])

        @pl.when(c == kv_heads - 1)
        def _():
            mixed = mixed_ref[...]
            for p in range(count):
                part = dot_nt(mixed, out_refs[p][...])
                own_ref[:, columns(sc, p, quarter)] = part[:half]
                send_ref[:, columns(sc, p, quarter)] = part[half:].astype(BF16)

    return pl.pallas_call(
        body,
        out_shape=[
            sds((tokens, q_width), BF16),
            sds((tokens, kv_heads * LANES), F32),
            sds((half, model), F32),
            sds((half, model), BF16),
        ],
        grid_spec=pltpu.PrefetchScalarGridSpec(
            num_scalar_prefetch=1,
            grid=(kv_heads,),
            in_specs=[
                pl.BlockSpec((tokens, LANES), lambda c, sc: (0, c)),
                pl.BlockSpec((length, LANES), lambda c, sc: (0, c // 2)),
                pl.BlockSpec((length, LANES), lambda c, sc: (0, pair_blocks + c // 2)),
            ]
            + [pl.BlockSpec((quarter, q_width), lambda c, sc: (0, heads // q_width))] * count,
            out_specs=[
                whole((tokens, q_width)),
                pl.BlockSpec((tokens, LANES), lambda c, sc: (0, c)),
                whole((half, model)),
                whole((half, model)),
            ],
            scratch_shapes=[pltpu.VMEM((tokens, length), F32)],
        ),
        compiler_params=params(58),
        cost_estimate=cost(
            16 * tokens * length * LANES + 2 * tokens * q_width * model,
            4 * length * kv2 + 8 * tokens * model,
            2 * kv_heads * tokens * length,
        ),
        name="attend",
    )(scalars, queries, kv_all, kv_all, *out_pieces)


def second_norm(scalars, layer_input, own, received, gains):
    tokens, model = layer_input.shape
    half = tokens // 2

    def body(sc, x_ref, own_ref, rec_ref, gain_ref, res_ref, norm_ref):
        start = pl.multiple_of(sc[2] * half, half)
        residual = (
            x_ref[pl.ds(start, half)].astype(F32) + own_ref[...] + rec_ref[...].astype(F32)
        )
        inverse = lax.rsqrt(jnp.mean(residual * residual, axis=-1, keepdims=True) + EPS)
        res_ref[...] = residual
        norm_ref[...] = (residual * inverse * gain_ref[1:2, :]).astype(BF16)

    return pl.pallas_call(
        body,
        out_shape=[sds((half, model), F32), sds((half, model), BF16)],
        grid_spec=pltpu.PrefetchScalarGridSpec(
            num_scalar_prefetch=1,
            grid=(1,),
            in_specs=[
                whole((tokens, model)),
                whole((half, model)),
                whole((half, model)),
                whole((8, model)),
            ],
            out_specs=[whole((half, model)), whole((half, model))],
        ),
        compiler_params=params(8),
        cost_estimate=cost(10 * half * model, 16 * half * model),
        name="second_norm",
    )(scalars, layer_input, own, received, gains)


def experts(scalars, fars, rows_in, grads_in, weights):
    k = len(fars)
    half, model = rows_in[0].shape
    tokens = 2 * half
    local, quarter, hidden = weights[0].shape
    count = model // quarter
    per_group = 2 * local
    blocks = [(side, g) for side in range(2) for g in range(k)]
    rows_each = len(blocks) * CAP

    def body(sc, *refs):
        x_ins, refs = refs[: 4 * k], refs[4 * k :]
        g_refs, refs = refs[:2], refs[2:]
        w_refs, refs = refs[: len(weights)], refs[len(weights) :]
        na_out, nb_out, ya_out, yb_out, h_out, d_out, go_out = refs[:7]
        st_ref, gate_ref, ns_ref, ys_ref, h_ref, d_ref, go_ref, g_held, w_held, x_held, sum_ref, sems = refs[7:]

        def weight(p, e, m):
            return w_held[3 * p + m, e]

        copies = (
            pltpu.make_async_copy(d_ref, d_out, sems.at[0]),
            pltpu.make_async_copy(go_ref, go_out, sems.at[1]),
        )
        hidden_copy = pltpu.make_async_copy(h_ref, h_out, sems.at[2])
        grad_copies = [
            pltpu.make_async_copy(g_refs[side].at[sc[1] ^ fars[g]], g_held.at[n], sems.at[3 + n])
            for n, (side, g) in enumerate(blocks)
        ]
        first_sem = 3 + len(blocks) + len(weights)
        row_copies = [
            pltpu.make_async_copy(x_ins[n], x_held.at[n], sems.at[first_sem + n])
            for n in range(4 * k)
        ]
        sum_copies = [
            pltpu.make_async_copy(sum_ref.at[n], out, sems.at[first_sem + 4 * k + n])
            for n, out in enumerate((na_out, nb_out, ya_out, yb_out))
        ]
        weight_copies = [
            pltpu.make_async_copy(w_refs[n], w_held.at[n], sems.at[3 + len(blocks) + n])
            for n in range(len(weights))
        ]
        for n in range(len(blocks)):
            for copy in (grad_copies[n], row_copies[2 * n], row_copies[2 * n + 1]):
                copy.start()
        for copy in weight_copies:
            copy.start()
        base = sc[1] * per_group + (sc[0] % 2) * local
        slot_row = lax.broadcasted_iota(jnp.int32, (CAP, tokens), 0).astype(F32)
        for n, (side, g) in enumerate(blocks):
            rows = slice(n * CAP, (n + 1) * CAP)
            grad_copies[n].wait()
            table = g_held[n, :, model : model + LANES].astype(F32).T
            ids, slots = table[:TOPK], table[TOPK : 2 * TOPK] - CAP
            gates = table[2 * TOPK : 3 * TOPK] + table[3 * TOPK : 4 * TOPK]
            picks = []
            for e in range(local):
                hit = ids == (base + e).astype(F32)
                slot = jnp.sum(jnp.where(hit, slots, 0.0), axis=0, keepdims=True) + CAP
                gate = jnp.sum(jnp.where(hit, gates, 0.0), axis=0, keepdims=True)
                pick = slot_row == slot
                value = jnp.sum(jnp.where(pick, gate, 0.0), axis=1, keepdims=True)
                gate_ref[e, rows, :] = jnp.broadcast_to(value, (CAP, LANES))
                picks.append(jnp.where(pick, 1.0, 0.0))
            row_copies[2 * n].wait()
            row_copies[2 * n + 1].wait()
            pick = jnp.concatenate(picks, axis=0)
            st_ref[n] = pick.T.astype(BF16)
            pick = pick.astype(BF16)
            for p in range(count):
                cols = columns(sc, p, quarter)
                values = jnp.concatenate(
                    [x_held[2 * n, :, cols], x_held[2 * n + 1, :, cols]], axis=0
                )
                got = dot_nn(pick, values).astype(BF16)
                grad = dot_nn(pick, g_held[n, :, cols])
                for e in range(local):
                    here = slice(e * CAP, (e + 1) * CAP)
                    d_ref[e, rows, p * quarter : (p + 1) * quarter] = got[here]
                    go_ref[e, rows, p * quarter : (p + 1) * quarter] = (
                        grad[here] * gate_ref[e, rows, 0:1]
                    ).astype(BF16)
        for copy in copies:
            copy.start()
        for copy in weight_copies:
            copy.wait()

        @pl.loop(0, local)
        def _(e):
            gate = up = act_grad = None
            for p in range(count):
                cols = slice(p * quarter, (p + 1) * quarter)
                rows = d_ref[e, :, cols]
                a = dot_nn(rows, weight(p, e, 0))
                b = dot_nn(rows, weight(p, e, 1))
                c = dot_nn(go_ref[e, :, cols], weight(p, e, 2))
                gate = a if gate is None else gate + a
                up = b if up is None else up + b
                act_grad = c if act_grad is None else act_grad + c
            sig = jax.nn.sigmoid(gate)
            silu = gate * sig
            act = (silu * up).astype(BF16)
            up_grad = (act_grad * silu).astype(BF16)
            gate_grad = (act_grad * up * sig * (1.0 + gate * (1.0 - sig))).astype(BF16)
            h_ref[e, :, :hidden] = act
            h_ref[e, :, hidden : 2 * hidden] = gate_grad
            h_ref[e, :, 2 * hidden :] = up_grad
            scale = gate_ref[e, :, 0:1]
            for p in range(count):
                cols = slice(p * quarter, (p + 1) * quarter)
                ns_ref[e, :, cols] = (
                    dot_nt(gate_grad, weight(p, e, 0)) + dot_nt(up_grad, weight(p, e, 1))
                ).astype(BF16)
                ys_ref[e, :, cols] = (dot_nt(act, weight(p, e, 2)) * scale).astype(BF16)

        hidden_copy.start()
        for at, source in ((0, ns_ref), (2, ys_ref)):
            for n, (side, g) in enumerate(blocks):
                rows = slice(n * CAP, (n + 1) * CAP)
                for p in range(count):
                    cols = slice(p * quarter, (p + 1) * quarter)
                    stacked = jnp.concatenate([source[e, rows, cols] for e in range(local)], axis=0)
                    sum_ref[at + side, g, :, columns(sc, p, quarter)] = dot_nn(
                        st_ref[n], stacked
                    ).astype(BF16)
                if g == k - 1:
                    sum_copies[at + side].start()
        for copy in (*copies, hidden_copy, *sum_copies):
            copy.wait()

    outside = pl.BlockSpec(memory_space=pltpu.HBM)
    sums = sds((k, tokens, model), BF16)
    rows = sds((local, rows_each, model), BF16)
    return pl.pallas_call(
        body,
        out_shape=[sums] * 4 + [sds((local, rows_each, 3 * hidden), BF16), rows, rows],
        grid_spec=pltpu.PrefetchScalarGridSpec(
            num_scalar_prefetch=1,
            grid=(1,),
            in_specs=[outside] * (4 * k + 2 + len(weights)),
            out_specs=[outside] * 7,
            scratch_shapes=[
                pltpu.VMEM((len(blocks), tokens, local * CAP), BF16),
                pltpu.VMEM((local, rows_each, LANES), F32),
                pltpu.VMEM((local, rows_each, model), BF16),
                pltpu.VMEM((local, rows_each, model), BF16),
                pltpu.VMEM((local, rows_each, 3 * hidden), BF16),
                pltpu.VMEM((local, rows_each, model), BF16),
                pltpu.VMEM((local, rows_each, model), BF16),
                pltpu.VMEM((len(blocks), tokens, model + LANES), BF16),
                pltpu.VMEM((len(weights), local, quarter, hidden), BF16),
                pltpu.VMEM((4 * k, half, model), BF16),
                pltpu.VMEM((4, k, tokens, model), BF16),
                pltpu.SemaphoreType.DMA((3 + len(blocks) + len(weights) + 4 * k + 4,)),
            ],
        ),
        compiler_params=params(58),
        cost_estimate=cost(
            2 * local * rows_each * model * (6 * hidden + 4 * tokens),
            2 * 3 * count * local * quarter * hidden + 24 * k * tokens * model,
            local * rows_each * hidden,
        ),
        name="experts",
    )(scalars, *rows_in, *grads_in, *weights)


def far_sets(local):
    mate = [(1, e) for e in range(local)]
    own = [(0, e) for e in range(local)]
    if local != 4:
        return [[v] for v in (*mate, *own)]
    return [mate[:1], mate[1:2], mate[2:] + own[:1], own[1:2], own[2:]]


def expert_weight_grads(row_sets, grad_sets, hidden_sets, quarter):
    groups = len(row_sets)
    local, _, model = row_sets[0].shape
    sets = far_sets(local)
    hidden = hidden_sets[0].shape[2] // 3
    count = model // quarter
    chunks, rows = [[]], 0
    for g in range(groups):
        if sum(row_sets[k].shape[1] for k in chunks[-1]) >= 8 * CAP:
            chunks.append([])
        chunks[-1].append(g)
        rows += row_sets[g].shape[1]

    def body(*refs):
        d_refs, go_refs, h_refs = refs[:groups], refs[groups : 2 * groups], refs[2 * groups : 3 * groups]
        keep_refs, far_refs = refs[3 * groups : 3 * groups + 2], refs[3 * groups + 2 :]
        expert = pl.program_id(0)
        far = []
        for p in range(count):
            cols = slice(p * quarter, (p + 1) * quarter)
            sums = [None, None, None]
            for chosen in chunks:
                left = jnp.concatenate([d_refs[g][0, :, cols] for g in chosen], axis=0)
                left_out = jnp.concatenate([go_refs[g][0, :, cols] for g in chosen], axis=0)
                right = jnp.concatenate([h_refs[g][0] for g in chosen], axis=0)
                parts = (
                    dot_tn(left, right[:, hidden : 2 * hidden]),
                    dot_tn(left, right[:, 2 * hidden :]),
                    dot_tn(left_out, right[:, :hidden]),
                )
                sums = [a if b is None else a + b for a, b in zip(parts, sums)]
            for k in range(3):
                if p < 2:
                    keep_refs[p][0, k] = sums[k].astype(BF16)
                else:
                    far.append(sums[k].astype(BF16))
        for ref, chosen in zip(far_refs, sets):
            for n, (which, e) in enumerate(chosen):

                @pl.when(expert == e)
                def _():
                    for k in range(3):
                        ref[3 * n + k] = far[3 * which + k]

    by_expert = lambda shape: pl.BlockSpec((1,) + shape, lambda e: (e,) + (0,) * len(shape))
    fars = [(3 * len(chosen), quarter, hidden) for chosen in sets]
    return pl.pallas_call(
        body,
        out_shape=[sds((local, 3, quarter, hidden), BF16)] * 2 + [sds(f, BF16) for f in fars],
        grid=(local,),
        in_specs=[by_expert(a.shape[1:]) for a in (*row_sets, *grad_sets, *hidden_sets)],
        out_specs=[by_expert((3, quarter, hidden))] * 2 + [whole(f) for f in fars],
        compiler_params=params(56),
        cost_estimate=cost(
            6 * local * rows * model * hidden,
            2 * local * rows * (2 * model + 3 * hidden) + 3 * local * 3 * model * hidden,
        ),
        name="expert_weight_grads",
    )(*row_sets, *grad_sets, *hidden_sets)


def middle_grad(scalars, parts, residual, grad_out, gains):
    tokens, model = grad_out.shape
    half = tokens // 2
    count = len(parts)

    def body(sc, *refs):
        part_refs = refs[:count]
        res_ref, go_ref, gain_ref, rg_ref, branch_ref, sum_ref = refs[count:]
        total = part_refs[0][...].astype(F32)
        for k in range(1, count):
            total = total + part_refs[k][...].astype(F32)
        residual = res_ref[...]
        start = pl.multiple_of(sc[2] * half, half)
        inverse = lax.rsqrt(jnp.mean(residual * residual, axis=-1, keepdims=True) + EPS)
        scaled = gain_ref[1:2, :] * total
        shift = jnp.mean(scaled * residual, axis=-1, keepdims=True)
        grad = (
            go_ref[pl.ds(start, half)].astype(F32)
            + inverse * scaled
            - residual * (inverse * inverse * inverse * shift)
        )
        rg_ref[...] = grad
        branch_ref[...] = grad.astype(BF16)
        sum_ref[...] = jnp.broadcast_to(
            jnp.sum(total * residual * inverse, axis=0, keepdims=True), (8, model)
        )

    return pl.pallas_call(
        body,
        out_shape=[sds((half, model), F32), sds((half, model), BF16), sds((8, model), F32)],
        grid_spec=pltpu.PrefetchScalarGridSpec(
            num_scalar_prefetch=1,
            grid=(1,),
            in_specs=[whole((half, model))] * (count + 1)
            + [whole((tokens, model)), whole((8, model))],
            out_specs=[whole((half, model)), whole((half, model)), whole((8, model))],
        ),
        compiler_params=params(12),
        cost_estimate=cost(20 * half * model, 24 * half * model),
        name="middle_grad",
    )(scalars, *parts, residual, grad_out, gains)


def attend_grad(scalars, branch, queries, kv_all, lse, out_pieces, cos_table, sin_table, piece_count):
    tokens, q_width = queries.shape
    length, kv2 = kv_all.shape
    kv_width = kv2 // 2
    kv_heads = kv_width // HEAD_DIM
    heads = q_width + kv2
    pair_blocks = kv_width // LANES
    count = len(out_pieces)
    quarter = out_pieces[0].shape[0]
    model = quarter * count
    half = tokens // 2

    def body(sc, b0_ref, b1_ref, q_ref, k_ref, v_ref, lse_ref, cos_ref, sin_ref, *rest):
        own = rows_at(sc[1], tokens)
        out_refs = rest[:count]
        dq_ref, dkv_ref, mg_ref, bias_ref = rest[count:]
        c = pl.program_id(0)

        @pl.when(c == 0)
        def _():
            cols = lax.broadcasted_iota(jnp.int32, (length, tokens), 0)
            rows = lax.broadcasted_iota(jnp.int32, (length, tokens), 1)
            query_pos = token_position(sc, rows, sc[1], tokens)
            key_pos = token_position(sc, cols % tokens, cols // tokens, tokens)
            bias_ref[...] = seen_bias(sc, query_pos, key_pos, piece_count)
            total = None
            for p in range(count):
                col = columns(sc, p, quarter)
                block = jnp.concatenate([b0_ref[:, col], b1_ref[:, col]], axis=0)
                part = dot_nn(block, out_refs[p][...])
                total = part if total is None else total + part
            mg_ref[...] = total.astype(BF16)

        low = lax.broadcasted_iota(jnp.int32, (1, LANES), 1) < HEAD_DIM
        mine = low == (c % 2 == 0)
        keys = k_ref[...].astype(F32)
        keys = jnp.where(mine, keys, pltpu.roll(keys, HEAD_DIM, 1)).astype(BF16)
        vals = v_ref[...].astype(F32)
        vals = jnp.where(mine, vals, pltpu.roll(vals, HEAD_DIM, 1)).astype(BF16)
        query = q_ref[...]
        grad = mg_ref[:, pl.ds(pl.multiple_of(c * LANES, LANES), LANES)]
        zero = jnp.zeros_like(query)
        lse_t = lse_ref[...].T
        dqs = []
        dk = dv = None
        for g in range(2):
            query_g = jnp.where(low, query, zero) if g == 0 else jnp.where(low, zero, query)
            grad_g = jnp.where(low, grad, zero) if g == 0 else jnp.where(low, zero, grad)
            scores = dot_nt(keys, query_g) + bias_ref[...]
            probs = jnp.exp(scores - lse_t[g * HEAD_DIM : g * HEAD_DIM + 1])
            prob_grad = dot_nt(vals, grad_g)
            delta = jnp.sum(probs * prob_grad, axis=0, keepdims=True)
            score_grad = (probs * (prob_grad - delta)).astype(BF16)
            dqs.append(dot_tn(score_grad, keys))
            dk_g = dot_nn(score_grad, query_g)
            dv_g = dot_nn(probs.astype(BF16), grad_g)
            dk = dk_g if dk is None else dk + dk_g
            dv = dv_g if dv is None else dv + dv_g
        dq = jnp.where(low, dqs[0], dqs[1]) * HEAD_DIM**-0.5
        dq_ref[...] = turn(dq, cos_ref[own], -sin_ref[own]).astype(BF16)
        dk = turn(dk, cos_ref[...], -sin_ref[...])
        for k, value in ((0, dk), (pair_blocks, dv)):
            value = (value + pltpu.roll(value, HEAD_DIM, 1)).astype(BF16)
            where = pl.ds(pl.multiple_of((k + c // 2) * LANES, LANES), LANES)
            dkv_ref[:, where] = jnp.where(mine, value, dkv_ref[:, where])

    return pl.pallas_call(
        body,
        out_shape=[sds((tokens, q_width), BF16), sds((length, kv2), BF16)],
        grid_spec=pltpu.PrefetchScalarGridSpec(
            num_scalar_prefetch=1,
            grid=(kv_heads,),
            in_specs=[
                whole((half, model)),
                whole((half, model)),
                pl.BlockSpec((tokens, LANES), lambda c, sc: (0, c)),
                pl.BlockSpec((length, LANES), lambda c, sc: (0, c // 2)),
                pl.BlockSpec((length, LANES), lambda c, sc: (0, pair_blocks + c // 2)),
                pl.BlockSpec((tokens, LANES), lambda c, sc: (0, c)),
                whole((length, LANES)),
                whole((length, LANES)),
            ]
            + [pl.BlockSpec((quarter, q_width), lambda c, sc: (0, heads // q_width))] * count,
            out_specs=[
                pl.BlockSpec((tokens, LANES), lambda c, sc: (0, c)),
                whole((length, kv2)),
            ],
            scratch_shapes=[
                pltpu.VMEM((tokens, q_width), BF16),
                pltpu.VMEM((length, tokens), F32),
            ],
        ),
        compiler_params=params(58),
        cost_estimate=cost(
            40 * tokens * length * LANES + 2 * tokens * q_width * model,
            6 * length * kv2 + 8 * tokens * model,
            2 * kv_heads * tokens * length,
        ),
        name="attend_grad",
    )(scalars, *branch, queries, kv_all, kv_all, lse, cos_table, sin_table, *out_pieces)


def weight_grads(scalars, normed, dq, dkv, branch, mixed, extra, quarter):
    length, model = normed.shape
    tokens, q_width = dq.shape
    kv2 = dkv.shape[1]
    width = q_width + kv2 + mixed.shape[1]
    count = model // quarter
    outs = [((quarter, width + LANES), BF16)] * 2 + [((2, quarter, width + LANES), BF16)]

    def body(sc, xn_ref, dq_ref, dkv_ref, b0_ref, b1_ref, mixed_ref, extra_ref, *out_refs):
        own = rows_at(sc[1], tokens)
        rows = lax.broadcasted_iota(jnp.int32, (quarter, quarter), 0)
        diagonal = rows == lax.broadcasted_iota(jnp.int32, (quarter, quarter), 1)
        for p in range(count):
            cols = columns(sc, p, quarter)
            ref = (out_refs[0], None, out_refs[1], None)[p]
            block = jnp.concatenate([b0_ref[:, cols], b1_ref[:, cols]], axis=0)
            column = jnp.sum(jnp.where(diagonal, extra_ref[0:1, cols], 0.0), axis=1, keepdims=True)
            at = 0
            for value in (
                dot_tn(xn_ref[own, cols], dq_ref[...]),
                dot_tn(xn_ref[:, cols], dkv_ref[...]),
                dot_tn(block, mixed_ref[...]),
                jnp.broadcast_to(column, (quarter, LANES)),
            ):
                here = slice(at, at + value.shape[1])
                at += value.shape[1]
                if ref is not None:
                    ref[:, here] = value.astype(BF16)
                else:
                    out_refs[2][p // 2, :, here] = value.astype(BF16)

    arrays = (normed, dq, dkv, *branch, mixed, extra)
    return pl.pallas_call(
        body,
        out_shape=[sds(*o) for o in outs],
        grid_spec=pltpu.PrefetchScalarGridSpec(
            num_scalar_prefetch=1,
            grid=(1,),
            in_specs=[whole(a.shape) for a in arrays],
            out_specs=[whole(o[0]) for o in outs],
        ),
        compiler_params=params(58),
        cost_estimate=cost(
            2 * model * (tokens * (q_width + mixed.shape[1]) + length * kv2),
            2 * length * (model + kv2) + 3 * model * width,
        ),
        name="weight_grads",
    )(scalars, *arrays)


def gather_expert_grads(scalars, keep, far, mates, sent):
    local, _, quarter, hidden = keep.shape
    sets = far_sets(local)
    chosen = range(len(sets) - len(far), len(sets)) if sent is not None else range(len(far))
    places = [
        (i, 3 * k, v[1])
        for i, n in enumerate(chosen)
        for k, v in enumerate(sets[n])
        if v[0] == 0
    ]
    used = sorted({i for i, _, _ in places})
    experts_here = [e for _, _, e in places]
    lowest = min(experts_here) if experts_here else 0
    count = len(experts_here)
    held = [] if sent is None else [sent]
    mates_here = [] if mates is None else [mates]
    steps = count + (local if mates_here else 0)

    def place(step, sc):
        core = sc[0] % 2
        mine = core * local + lowest + step
        return jnp.where(step < count, mine, (1 - core) * local + step - count)

    def body(sc, keep_ref, *rest):
        far_refs, out_ref = dict(zip(used, rest)), rest[-1]
        step = pl.program_id(0)
        for i, start, expert in places:

            @pl.when(step == expert - lowest)
            def _():
                out_ref[0] = keep_ref[0].astype(F32) + far_refs[i][start : start + 3].astype(F32)

        if mates_here:

            @pl.when(step >= count)
            def _():
                out_ref[0] = rest[len(used)][0].astype(F32)

    block = (1, 3, quarter, hidden)
    own = lambda step, sc: (lowest + jnp.minimum(step, max(count - 1, 0)), 0, 0, 0)
    other = lambda step, sc: (jnp.maximum(step - count, 0), 0, 0, 0)
    arrays = [keep, *[far[i] for i in used], *mates_here, *held]
    return pl.pallas_call(
        body,
        out_shape=sds((2 * local, 3, quarter, hidden), F32),
        grid_spec=pltpu.PrefetchScalarGridSpec(
            num_scalar_prefetch=1,
            grid=(steps,),
            in_specs=[pl.BlockSpec(block, own)]
            + [whole(far[i].shape) for i in used]
            + [pl.BlockSpec(block, other)] * len(mates_here)
            + [pl.BlockSpec(memory_space=pl.ANY)] * len(held),
            out_specs=pl.BlockSpec(block, lambda step, sc: (place(step, sc), 0, 0, 0)),
        ),
        input_output_aliases={len(arrays): 0} if held else {},
        compiler_params=params(24),
        cost_estimate=cost(3 * steps * quarter * hidden, 3 * 10 * steps * quarter * hidden),
        name="gather_expert_grads",
    )(scalars, *arrays)


def back(scalars, dq, dkv, pieces):
    tokens, q_width = dq.shape
    groups, _, kv2 = dkv.shape
    heads = q_width + kv2
    count = len(pieces)
    quarter = pieces[0].shape[0]
    model = count * quarter
    half = tokens // 2

    def body(sc, dq_ref, dkv_ref, *rest):
        piece_refs = rest[:count]
        own_ref, send_ref = rest[count:]
        total = dkv_ref[0].astype(F32)
        for g in range(1, groups):
            total = total + dkv_ref[g].astype(F32)
        dl_kv = total.astype(BF16)
        dl_q = dq_ref[...]
        for p in range(count):
            cols = columns(sc, p, quarter)
            part = dot_nt(dl_q, piece_refs[p][:, :q_width]) + dot_nt(
                dl_kv, piece_refs[p][:, q_width:heads]
            )
            own_ref[:, cols] = part[:half]
            send_ref[:, cols] = part[half:].astype(BF16)

    arrays = (dq, dkv, *pieces)
    return pl.pallas_call(
        body,
        out_shape=[sds((half, model), F32), sds((half, model), BF16)],
        grid_spec=pltpu.PrefetchScalarGridSpec(
            num_scalar_prefetch=1,
            grid=(1,),
            in_specs=[whole(dq.shape), whole(dkv.shape)] + [whole((quarter, heads))] * count,
            out_specs=[whole((half, model))] * 2,
        ),
        compiler_params=params(58),
        cost_estimate=cost(2 * tokens * model * heads, 2 * model * (heads + 2 * tokens)),
        name="back",
    )(scalars, *arrays)


def last_grad(scalars, layer_input, own, received, residual_grad, gains):
    tokens, model = layer_input.shape
    half = tokens // 2

    def body(sc, x_ref, own_ref, rec_ref, rg_ref, gain_ref, out_ref):
        start = pl.multiple_of(sc[2] * half, half)
        values = x_ref[pl.ds(start, half)].astype(F32)
        inverse = lax.rsqrt(jnp.mean(values * values, axis=-1, keepdims=True) + EPS)
        scaled = gain_ref[0:1, :] * (own_ref[...] + rec_ref[...].astype(F32))
        shift = jnp.mean(scaled * values, axis=-1, keepdims=True)
        out_ref[...] = (
            rg_ref[...] + inverse * scaled - values * (inverse * inverse * inverse * shift)
        ).astype(BF16)

    return pl.pallas_call(
        body,
        out_shape=sds((half, model), BF16),
        grid_spec=pltpu.PrefetchScalarGridSpec(
            num_scalar_prefetch=1,
            grid=(1,),
            in_specs=[
                whole((tokens, model)),
                whole((half, model)),
                whole((half, model)),
                whole((half, model)),
                whole((8, model)),
            ],
            out_specs=whole((half, model)),
        ),
        compiler_params=params(8),
        cost_estimate=cost(12 * half * model, 14 * half * model),
        name="last_grad",
    )(scalars, layer_input, own, received, residual_grad, gains)


def local(
    layer_input,
    attn_norm,
    w_query,
    w_key,
    w_value,
    w_out,
    moe_norm,
    expert_weights,
    expert_ids,
    slot_ids,
    gate_values,
    piece_starts,
    grad_out,
):
    _, tokens, model = layer_input.shape
    half = tokens // 2
    groups = lax.axis_size("ctx")
    shard = lax.axis_index("shard")
    group = lax.axis_index("ctx")
    side = lax.axis_index("tp")
    piece_count = piece_starts.shape[1]
    scalars = jnp.concatenate(
        [jnp.stack([shard, group, side]).astype(jnp.int32), piece_starts[0]]
    )
    flat_input = layer_input[0]
    flat_grad = grad_out[0]
    q_width, kv_width = w_query.shape[1], w_key.shape[1]
    rows_here = w_query.shape[0]
    quarter = rows_here * groups

    own_input = jnp.where(side == 0, flat_input[:half], flat_input[half:])
    local_experts = expert_weights.shape[0] // 2
    core = shard % 2


    def experts_of(which, m):
        start = (which * local_experts, m, 0, 0)
        size = (local_experts, 1) + expert_weights.shape[2:]
        return lax.dynamic_slice(expert_weights, start, size)[:, 0]

    mine = [experts_of(core, m) for m in range(3)]
    given = [experts_of(1 - core, m) for m in range(3)]
    weight_block = jnp.concatenate(
        [
            after(w_query, *mine),
            w_key,
            w_value,
            w_out.T,
            attn_norm[:, None],
            moe_norm[:, None],
            jnp.zeros((rows_here, LANES - 2), BF16),
        ],
        axis=1,
    )

    index = jnp.arange(groups * tokens, dtype=jnp.int32)
    positions = (index ^ (side * half).astype(jnp.int32)).astype(F32)
    lane = jnp.arange(LANES, dtype=jnp.int32)
    step = (lane % (HEAD_DIM // 2)).astype(F32)
    angles = positions[:, None] * (1.0 / 10000.0 ** (step * 2.0 / HEAD_DIM))[None, :]
    cos_table = jnp.cos(angles)
    sin_table = jnp.sin(angles) * jnp.where(lane % HEAD_DIM < HEAD_DIM // 2, -1.0, 1.0)[None, :]

    gate_high = gate_values[0].astype(BF16)
    gate_low = (gate_values[0] - gate_high.astype(F32)).astype(BF16)
    routing = jnp.concatenate(
        [
            expert_ids[0].astype(BF16),
            slot_ids[0].astype(BF16),
            gate_high,
            gate_low,
            jnp.zeros((tokens, LANES - 4 * TOPK), BF16),
        ],
        axis=1,
    )
    grad_block = spread_grads(scalars, flat_grad, routing, groups)

    near = [1, 3] if groups == 4 else [1]
    rest = [b for b in range(1, groups) if b not in near]
    block_0, own_input, cos_table, sin_table, grad_block, far_0, far_1, *kept = fence(
        spread(weight_block, "ctx").reshape(quarter, -1),
        own_input,
        cos_table,
        sin_table,
        grad_block,
        swap(mine[0], "shard", 2),
        swap(mine[1], "shard", 2),
        *mine,
        *given,
        *[swap(own_input, "ctx", b) for b in near],
    )
    mine, given = kept[:3], kept[3:6]
    input_at = dict(zip(near, kept[6:]))
    halves = [swap(input_at[b], "tp", 1) for b in near]
    block_0, block_2, *kept = fence(
        block_0,
        swap(block_0, "shard", 2),
        *halves,
        *[swap(own_input, "ctx", b) for b in rest],
    )
    crossed = dict(zip(near, kept[: len(near)]))
    input_at.update(dict(zip(rest, kept[len(near) :])))
    grads_own = lax.all_to_all(after(grad_block, block_2), "ctx", 0, 0, tiled=True)
    block_0, block_1, block_2, block_3, taken_0, *kept = fence(
        block_0,
        swap(block_0, "shard", 1),
        block_2,
        swap(block_2, "shard", 1),
        swap(after(given[0], block_2), "shard", 1),
        *[swap(input_at[b], "tp", 1) for b in rest],
    )
    crossed.update(dict(zip(rest, kept)))
    pieces = [block_0, block_1, block_2, block_3]
    others = [v for b in range(1, groups) for v in (input_at[b], crossed[b])]

    normed_all, queries, kv_all, gains = front(
        scalars, flat_input, others, pieces, cos_table, sin_table, (q_width, kv_width)
    )
    mixed, lse, attention_own, attention_send = attend(
        scalars, queries, kv_all, pieces, piece_count
    )
    attention_send, far_2, far_3, taken_2, taken_1 = fence(
        attention_send,
        swap(after(mine[2], block_1), "shard", 2),
        swap(after(taken_0, block_1), "shard", 2),
        swap(after(given[2], block_1), "shard", 1),
        swap(after(given[1], block_1), "shard", 1),
    )
    attention_got, far_4 = fence(
        swap(attention_send, "tp", 1), swap(after(taken_1, attention_send), "shard", 2)
    )
    residual, normed_two = second_norm(
        scalars, flat_input, attention_own, attention_got, gains
    )

    calls = [[0], *[[b, b + 1] for b in range(1, groups - 1, 2)], [groups - 1]]
    far_5 = swap(after(taken_2, far_4), "shard", 2)
    grads_own = after(grads_own, residual)
    normed_two, crossed, grads_own, grads_mate, far_5, *arrived = fence(
        normed_two,
        swap(normed_two, "tp", 1),
        grads_own,
        swap(grads_own, "shard", 1),
        far_5,
        *[swap(normed_two, "ctx", b) for b in calls[1]],
    )
    tokens_at = {0: normed_two, **dict(zip(calls[1], arrived))}
    grads_in = [grads_own, grads_mate]
    taken = [taken_0, taken_1, taken_2]
    expert_pieces = [*mine, *taken, far_0, far_1, far_2, far_3, far_4, far_5]
    rows_in = [normed_two, crossed, swap(normed_two, "shard", 1), swap(crossed, "shard", 1)]

    def summed(own, got, part):
        return own[:, part].astype(F32) + got[:, part].astype(F32)

    low, high = slice(0, half), slice(half, tokens)
    row_sets, grad_sets, hidden_sets = [], [], []
    norm_parts, out_parts, out_sets = {}, {}, []
    waiting = None
    order = scalars
    for n, call in enumerate(calls):
        own, mate, out_own, out_mate, hiddens, rows, grads = experts(
            order, call, rows_in, grads_in, expert_pieces
        )
        row_sets.append(rows)
        grad_sets.append(grads)
        hidden_sets.append(hiddens)
        out_sets.append((call, out_own, out_mate))
        later = calls[n + 1] if n + 1 < len(calls) else []
        latest = calls[n + 2] if n + 2 < len(calls) else []
        own, mate, *arrived = fence(
            own,
            mate,
            *[swap(tokens_at[b], "tp", 1) for b in later],
            *[swap(tokens_at[b], "shard", 1) for b in later],
            *[swap(normed_two, "ctx", b) for b in latest],
            *([waiting[3]] if waiting is not None else []),
        )
        crossed, arrived = arrived[: len(later)], arrived[len(later) :]
        mates, arrived = arrived[: len(later)], arrived[len(later) :]
        tokens_at.update(dict(zip(latest, arrived)))
        if later:
            here = [v for b, c in zip(later, crossed) for v in (tokens_at[b], c)]
            there = [v for m, c in zip(mates, crossed) for v in (m, swap(c, "shard", 1))]
            rows_in = [*here, *there]
        got = swap(mate, "shard", 1)
        sent = summed(own, got, high).astype(BF16)
        if waiting is not None:
            old_call, kept_own, old_got, _ = waiting
            kept = summed(after(kept_own, sent), old_got, low) + arrived[-1].astype(F32)
            for i, b in enumerate(old_call):
                norm_parts[b] = kept[i] if b == 0 else swap(kept[i].astype(BF16), "ctx", b)
        waiting = (call, own, got, swap(sent, "tp", 1))
        order = after(scalars, sent)

    hidden_sets[-1] = after(hidden_sets[-1], sent)
    call, own, got, crossed = waiting
    early = [b for b in norm_parts if b > 0]
    mates = [swap(after(s[2], sent), "shard", 1) for s in out_sets[:-1]]
    keep_0, keep_1, *arrived = fence(
        *expert_weight_grads(row_sets, grad_sets, hidden_sets, quarter),
        crossed,
        *[norm_parts[b] for b in early],
        *mates,
    )
    fars = len(arrived) - 1 - len(early) - len(mates)
    far_sent, crossed, arrived = arrived[:fars], arrived[fars], arrived[fars + 1 :]
    far_got = []

    def send_far(count, *ready):
        start = len(far_got)
        got = [swap(after(v, *ready), "shard", 2) for v in far_sent[start : start + count]]
        far_got.extend(got)
        return got

    def keep_far(got):
        if got:
            far_got[len(far_got) - len(got) :] = got

    norm_parts.update(dict(zip(early, arrived)))
    mates = arrived[len(early) :]
    kept = summed(own, got, low) + crossed.astype(F32)
    for i, b in enumerate(call):
        norm_parts[b] = swap(kept[i].astype(BF16), "ctx", b)

    outs = [(s[0], after(s[1], kept), m) for s, m in zip(out_sets, mates)]
    middle, edges = outs[1:], outs[:1]
    out_crossed = [swap(summed(own, got, high).astype(BF16), "tp", 1) for _, own, got in middle]
    out_last = swap(after(out_sets[-1][2], kept), "shard", 1)
    sending = send_far(1, crossed)
    residual, out_last, *arrived = fence(
        residual, out_last, *[norm_parts[b] for b in range(groups)], *sending, *out_crossed
    )
    keep_far(arrived[groups : groups + len(sending)])
    out_crossed = arrived[groups + len(sending) :]
    arrived = arrived[:groups]
    residual_grad, branch_own, gain_row = middle_grad(
        scalars, arrived, residual, flat_grad, gains
    )
    sending = send_far(1, out_last)
    branch_own, branch_crossed, *sending = fence(branch_own, swap(branch_own, "tp", 1), *sending)
    keep_far(sending)
    branch = [branch_own, branch_crossed]
    for (call, own, got), crossed in zip(middle, out_crossed):
        kept = summed(after(own, branch_own), got, low) + crossed.astype(F32)
        for i, b in enumerate(call):
            out_parts[b] = swap(fence(kept[i].astype(BF16))[0], "ctx", b)
    moved = list(out_parts)
    edges.append((*out_sets[-1][:2], out_last))
    edges = [(call, after(own, branch_own), got) for call, own, got in edges]
    out_crossed = [swap(summed(own, got, high).astype(BF16), "tp", 1) for _, own, got in edges]

    dq, dkv_parts = attend_grad(
        scalars, branch, queries, kv_all, lse, pieces, cos_table, sin_table, piece_count
    )
    sending = send_far(1, branch_crossed)
    dq, dkv_parts, out_first, out_last, *arrived = fence(
        dq, dkv_parts, *out_crossed, *[out_parts[b] for b in moved], *sending
    )
    out_crossed = [out_first, out_last]
    out_parts.update(dict(zip(moved, arrived)))
    keep_far(arrived[len(moved) :])

    for (call, own, got), crossed in zip(edges, out_crossed):
        kept = summed(after(own, dq), got, low) + crossed.astype(F32)
        for i, b in enumerate(call):
            out_parts[b] = kept[i] if b == 0 else swap(fence(kept[i].astype(BF16))[0], "ctx", b)
    sending = send_far(1, dq)
    own_grads, far_grads, sent_grads, dkv_parts, *arrived = fence(
        *weight_grads(scalars, normed_all, dq, dkv_parts, branch, mixed, gain_row, quarter),
        dkv_parts,
        *[out_parts[b] for b in calls[-1]],
        *sending,
    )
    out_parts.update(dict(zip(calls[-1], arrived)))
    keep_far(arrived[len(calls[-1]) :])

    got_grads = fence(swap(sent_grads, "shard", 1))[0]
    passed = (far_grads.astype(F32) + got_grads[1].astype(F32)).astype(BF16)
    places = {
        v[1]: (n, 3 * k)
        for n, chosen in enumerate(far_sets(local_experts))
        for k, v in enumerate(chosen)
        if v[0] == 1
    }
    mates = jnp.stack(
        [
            (keep_1[e].astype(F32) + far_got[n][start : start + 3].astype(F32)).astype(BF16)
            for e, (n, start) in sorted(places.items())
        ]
    )
    kept_grads = (after(own_grads, mates).astype(F32) + got_grads[0].astype(F32)).astype(BF16)
    def natural(own, other):
        return jnp.where(
            side == 0,
            jnp.concatenate([own, other], axis=0),
            jnp.concatenate([other, own], axis=0),
        )[None]

    out_sum = after(residual, kept_grads)
    for b in range(groups):
        out_sum = out_sum + out_parts[b].astype(F32)
    out_half = out_sum.astype(BF16)
    output = natural(out_half, swap(out_half, "tp", 1))
    dkv, passed, kept_grads, output, mates = fence(
        lax.all_to_all(
            dkv_parts.reshape(groups, tokens, 2 * kv_width), "ctx", 0, 0, tiled=True
        ),
        swap(passed, "shard", 2),
        kept_grads,
        output,
        swap(mates, "shard", 1),
    )

    total = fence((kept_grads.astype(F32) + passed.astype(F32)).astype(BF16))[0]
    normed_own, normed_send = back(scalars, dq, dkv, pieces)
    input_half = last_grad(
        scalars, flat_input, normed_own, swap(normed_send, "tp", 1), residual_grad, gains
    )
    early = list(far_got)
    sending = send_far(len(far_sent), dkv)
    expert_grad = gather_expert_grads(scalars, keep_0, early, mates, None)
    total, input_half, input_other, expert_grad, *sending = fence(
        lax.all_to_all(
            total.reshape(groups, rows_here, total.shape[1]), "ctx", 0, 0, tiled=True
        ),
        input_half,
        swap(input_half, "tp", 1),
        expert_grad,
        *sending,
    )
    keep_far(sending)
    input_grad = natural(input_half, input_other)
    if sending:
        expert_grad = gather_expert_grads(scalars, keep_0, sending, None, expert_grad)
    total = jnp.sum(total.astype(F32), axis=0)
    query_grad = total[:, :q_width]
    key_grad = total[:, q_width : q_width + kv_width]
    value_grad = total[:, q_width + kv_width : q_width + 2 * kv_width]
    heads = q_width + 2 * kv_width
    out_grad = total[:, heads : heads + q_width].T
    moe_sum = total[:, heads + q_width]
    attn_sum = (
        jnp.sum(w_query.astype(F32) * query_grad, axis=1)
        + jnp.sum(w_key.astype(F32) * key_grad, axis=1)
        + jnp.sum(w_value.astype(F32) * value_grad, axis=1)
    )
    sums = jnp.stack([attn_sum, moe_sum])
    attn_sum, moe_norm_grad = sums + swap(sums, "tp", 1)
    attn_norm_grad = attn_sum / attn_norm.astype(F32)
    return (
        output,
        input_grad,
        attn_norm_grad,
        query_grad,
        key_grad,
        value_grad,
        out_grad,
        moe_norm_grad,
        expert_grad,
    )


def solution(mesh):
    in_specs = (
        P("shard", "ctx", None),
        P(("shard", "ctx")),
        P(("shard", "ctx"), "tp"),
        P(("shard", "ctx"), "tp"),
        P(("shard", "ctx"), "tp"),
        P("tp", ("shard", "ctx")),
        P(("shard", "ctx")),
        P("ctx", None, "shard", "tp"),
        P("shard", "ctx", None),
        P("shard", "ctx", None),
        P("shard", "ctx", None),
        P("shard", None),
        P("shard", "ctx", None),
    )
    out_specs = (
        P("shard", "ctx", None),
        P("shard", "ctx", None),
        P(("shard", "ctx")),
        P(("shard", "ctx"), "tp"),
        P(("shard", "ctx"), "tp"),
        P(("shard", "ctx"), "tp"),
        P("tp", ("shard", "ctx")),
        P(("shard", "ctx")),
        P("ctx", None, "shard", "tp"),
    )
    return jax.shard_map(local, mesh=mesh, in_specs=in_specs, out_specs=out_specs, check_vma=False)
```

```python
import functools

import jax
import jax.numpy as jnp
from jax import lax
from jax.experimental import pallas as pl
from jax.experimental.pallas import tpu as pltpu
from jax.sharding import PartitionSpec as P

HEAD_DIM = 64
EXPERTS = 32
TOPK = 8
PIECE = 256
CAP = 96
EPS = 1e-06
MASKED = -1e30
LANES = 128
F32 = jnp.float32
BF16 = jnp.bfloat16


def swap(value, axis, distance):
    size = lax.axis_size(axis)
    return lax.ppermute(value, axis, [(i, i ^ distance) for i in range(size)])


def spread(value, axis):
    size = lax.axis_size(axis)
    copies = jnp.broadcast_to(value[None], (size,) + value.shape)
    return lax.all_to_all(copies, axis, 0, 0, tiled=True)


def after(value, *others):
    return lax.optimization_barrier((value,) + others)[0]


def fence(*values):
    return lax.optimization_barrier(values)


def dot_nn(a, b):
    return lax.dot_general(a, b, (((1,), (0,)), ((), ())), preferred_element_type=F32)


def dot_nt(a, b):
    return lax.dot_general(a, b, (((1,), (1,)), ((), ())), preferred_element_type=F32)


def dot_tn(a, b):
    return lax.dot_general(a, b, (((0,), (0,)), ((), ())), preferred_element_type=F32)


def cost(flops, moved, special=0):
    return pl.CostEstimate(flops=int(flops), bytes_accessed=int(moved), transcendentals=int(special))


def params(megabytes, length=0):
    megabytes = 58 if length > 1024 else megabytes
    return pltpu.CompilerParams(vmem_limit_bytes=megabytes * 1024 * 1024)


def sds(shape, dtype):
    return jax.ShapeDtypeStruct(shape, dtype)


def whole(shape):
    return pl.BlockSpec(shape, lambda *_: (0,) * len(shape))


def turn(value, cosine, sine):
    lane = lax.broadcasted_iota(jnp.int32, (value.shape[0], LANES), 1) % HEAD_DIM
    first = lane < HEAD_DIM // 2
    parts = []
    for j in range(value.shape[1] // LANES):
        chunk = value[:, j * LANES : (j + 1) * LANES]
        partner = jnp.where(
            first,
            pltpu.roll(chunk, LANES - HEAD_DIM // 2, 1),
            pltpu.roll(chunk, HEAD_DIM // 2, 1),
        )
        parts.append(chunk * cosine + partner * sine)
    return parts[0] if len(parts) == 1 else jnp.concatenate(parts, axis=1)


def rows_at(index, size):
    return pl.ds(pl.multiple_of(index * size, size), size)


def columns(scalars, p, width):
    return pl.ds(pl.multiple_of((scalars[0] ^ p) * width, width), width)


def spread_grads(scalars, grads, routing, groups):
    tokens, model = grads.shape
    half = tokens // 2
    out = (groups, tokens, model + LANES)

    def body(sc, grads_ref, routing_ref, out_ref):
        for h in range(2):
            here = rows_at(sc[2] ^ h, half)
            out_ref[0, h * half : (h + 1) * half, :model] = grads_ref[here]
            out_ref[0, h * half : (h + 1) * half, model:] = routing_ref[here]

    return pl.pallas_call(
        body,
        out_shape=sds(out, BF16),
        grid_spec=pltpu.PrefetchScalarGridSpec(
            num_scalar_prefetch=1,
            grid=(groups,),
            in_specs=[whole(grads.shape), whole(routing.shape)],
            out_specs=pl.BlockSpec((1,) + out[1:], lambda g, sc: (g, 0, 0)),
        ),
        compiler_params=params(12),
        cost_estimate=cost(0, 2 * (groups + 1) * tokens * (model + LANES)),
        name="spread_grads",
    )(scalars, grads, routing)


def front(scalars, layer_input, others, pieces, cos_table, sin_table, widths):
    tokens, model = layer_input.shape
    quarter = pieces[0].shape[0]
    q_width, kv_width = widths
    heads = q_width + 2 * kv_width
    gain_column = pieces[0].shape[1] - LANES
    half = tokens // 2
    count = len(pieces)
    groups = 1 + len(others) // 2
    length = groups * tokens

    def body(sc, x_ref, *rest):
        other_refs, rest = rest[: len(others)], rest[len(others) :]
        piece_refs = rest[:count]
        cos_ref, sin_ref, xn_ref, q_ref, kv_ref, gain_ref = rest[count:]
        rows = lax.broadcasted_iota(jnp.int32, (quarter, quarter), 0)
        diagonal = rows == lax.broadcasted_iota(jnp.int32, (quarter, quarter), 1)
        for p in range(count):
            gains = piece_refs[p][:, gain_column : gain_column + LANES].astype(F32)
            for k in range(2):
                row = jnp.sum(jnp.where(diagonal, gains[:, k : k + 1], 0.0), axis=0, keepdims=True)
                gain_ref[k : k + 1, columns(sc, p, quarter)] = row
        gain = gain_ref[0:1, :]
        for b in range(groups):
            for h in range(2):
                if b == 0:
                    values = x_ref[rows_at(sc[2] ^ h, half)].astype(F32)
                else:
                    values = other_refs[2 * (b - 1) + h][...].astype(F32)
                inverse = lax.rsqrt(jnp.mean(values * values, axis=-1, keepdims=True) + EPS)
                xn_ref[rows_at(2 * (sc[1] ^ b) + h, half)] = (values * inverse * gain).astype(BF16)

        own = rows_at(sc[1], tokens)
        total = None
        for p in range(count):
            part = dot_nn(xn_ref[own, columns(sc, p, quarter)], piece_refs[p][:, :q_width])
            total = part if total is None else total + part
        total = turn(total, cos_ref[own], sin_ref[own]).astype(BF16)
        q_ref[...] = (total * HEAD_DIM**-0.5).astype(BF16)

        @pl.loop(0, groups)
        def _(g):
            here = rows_at(g, tokens)
            total = None
            for p in range(count):
                part = dot_nn(xn_ref[here, columns(sc, p, quarter)], piece_refs[p][:, q_width:heads])
                total = part if total is None else total + part
            kv_ref[here, :kv_width] = turn(total[:, :kv_width], cos_ref[here], sin_ref[here]).astype(
                BF16
            )
            kv_ref[here, kv_width:] = total[:, kv_width:].astype(BF16)

    outs = [
        ((length, model), BF16),
        ((tokens, q_width), BF16),
        ((length, 2 * kv_width), BF16),
        ((8, model), F32),
    ]
    arrays = (layer_input, *others, *pieces, cos_table, sin_table)
    return pl.pallas_call(
        body,
        out_shape=[sds(*o) for o in outs],
        grid_spec=pltpu.PrefetchScalarGridSpec(
            num_scalar_prefetch=1,
            grid=(1,),
            in_specs=[whole(a.shape) for a in arrays],
            out_specs=[whole(o[0]) for o in outs],
        ),
        compiler_params=params(58),
        cost_estimate=cost(
            2 * model * (tokens * q_width + length * 2 * kv_width),
            2 * model * (2 * length + heads) + 2 * length * (kv_width + 2 * LANES),
        ),
        name="front",
    )(scalars, *arrays)


def inside_piece(position, start):
    return (position >= start) & (position < start + PIECE)


def seen_bias(sc, query_pos, key_pos, piece_count):
    seen = key_pos <= query_pos
    for k in range(piece_count):
        start = sc[3 + k]
        seen = seen | (inside_piece(query_pos, start) & inside_piece(key_pos, start))
    return jnp.where(seen, 0.0, MASKED)


def token_position(sc, index, group, tokens):
    return group * tokens + (index ^ (sc[2] * (tokens // 2)))


def attend(scalars, queries, kv_all, out_pieces, piece_count):
    tokens, q_width = queries.shape
    length, kv2 = kv_all.shape
    kv_width = kv2 // 2
    kv_heads = kv_width // HEAD_DIM
    heads = q_width + kv2
    pair_blocks = kv_width // LANES
    count = len(out_pieces)
    quarter = out_pieces[0].shape[0]
    model = quarter * count
    half = tokens // 2

    def body(sc, q_ref, k_ref, v_ref, *rest):
        out_refs = rest[:count]
        mixed_ref, lse_ref, own_ref, send_ref, bias_ref = rest[count:]
        c = pl.program_id(0)

        @pl.when(c == 0)
        def _():
            rows = lax.broadcasted_iota(jnp.int32, (tokens, length), 0)
            cols = lax.broadcasted_iota(jnp.int32, (tokens, length), 1)
            query_pos = token_position(sc, rows, sc[1], tokens)
            key_pos = token_position(sc, cols % tokens, cols // tokens, tokens)
            bias_ref[...] = seen_bias(sc, query_pos, key_pos, piece_count)

        low = lax.broadcasted_iota(jnp.int32, (1, LANES), 1) < HEAD_DIM
        mine = low == (c % 2 == 0)
        keys = k_ref[...].astype(F32)
        keys = jnp.where(mine, keys, pltpu.roll(keys, HEAD_DIM, 1)).astype(BF16)
        vals = v_ref[...].astype(F32)
        vals = jnp.where(mine, vals, pltpu.roll(vals, HEAD_DIM, 1)).astype(BF16)
        query = q_ref[...]
        zero = jnp.zeros_like(query)
        outs, lses = [], []
        for part in (jnp.where(low, query, zero), jnp.where(low, zero, query)):
            scores = dot_nt(part, keys) + bias_ref[...]
            top = jnp.max(scores, axis=-1, keepdims=True)
            expo = jnp.exp(scores - top)
            total = jnp.sum(expo, axis=-1, keepdims=True)
            probs = expo * (1.0 / total)
            outs.append(dot_nn(probs.astype(BF16), vals))
            lses.append(top + jnp.log(total))
        mixed_ref[:, pl.ds(pl.multiple_of(c * LANES, LANES), LANES)] = jnp.where(
            low, outs[0], outs[1]
        ).astype(BF16)
        lse_ref[...] = jnp.where(low, lses[0], lses[1])

        @pl.when(c == kv_heads - 1)
        def _():
            mixed = mixed_ref[...]
            for p in range(count):
                part = dot_nt(mixed, out_refs[p][...])
                own_ref[:, columns(sc, p, quarter)] = part[:half]
                send_ref[:, columns(sc, p, quarter)] = part[half:].astype(BF16)

    return pl.pallas_call(
        body,
        out_shape=[
            sds((tokens, q_width), BF16),
            sds((tokens, kv_heads * LANES), F32),
            sds((half, model), F32),
            sds((half, model), BF16),
        ],
        grid_spec=pltpu.PrefetchScalarGridSpec(
            num_scalar_prefetch=1,
            grid=(kv_heads,),
            in_specs=[
                pl.BlockSpec((tokens, LANES), lambda c, sc: (0, c)),
                pl.BlockSpec((length, LANES), lambda c, sc: (0, c // 2)),
                pl.BlockSpec((length, LANES), lambda c, sc: (0, pair_blocks + c // 2)),
            ]
            + [pl.BlockSpec((quarter, q_width), lambda c, sc: (0, heads // q_width))] * count,
            out_specs=[
                whole((tokens, q_width)),
                pl.BlockSpec((tokens, LANES), lambda c, sc: (0, c)),
                whole((half, model)),
                whole((half, model)),
            ],
            scratch_shapes=[pltpu.VMEM((tokens, length), F32)],
        ),
        compiler_params=params(58),
        cost_estimate=cost(
            16 * tokens * length * LANES + 2 * tokens * q_width * model,
            4 * length * kv2 + 8 * tokens * model,
            2 * kv_heads * tokens * length,
        ),
        name="attend",
    )(scalars, queries, kv_all, kv_all, *out_pieces)


def second_norm(scalars, layer_input, own, received, gains):
    tokens, model = layer_input.shape
    half = tokens // 2

    def body(sc, x_ref, own_ref, rec_ref, gain_ref, res_ref, norm_ref):
        start = pl.multiple_of(sc[2] * half, half)
        residual = (
            x_ref[pl.ds(start, half)].astype(F32) + own_ref[...] + rec_ref[...].astype(F32)
        )
        inverse = lax.rsqrt(jnp.mean(residual * residual, axis=-1, keepdims=True) + EPS)
        res_ref[...] = residual
        norm_ref[...] = (residual * inverse * gain_ref[1:2, :]).astype(BF16)

    return pl.pallas_call(
        body,
        out_shape=[sds((half, model), F32), sds((half, model), BF16)],
        grid_spec=pltpu.PrefetchScalarGridSpec(
            num_scalar_prefetch=1,
            grid=(1,),
            in_specs=[
                whole((tokens, model)),
                whole((half, model)),
                whole((half, model)),
                whole((8, model)),
            ],
            out_specs=[whole((half, model)), whole((half, model))],
        ),
        compiler_params=params(8),
        cost_estimate=cost(10 * half * model, 16 * half * model),
        name="second_norm",
    )(scalars, layer_input, own, received, gains)


def experts(scalars, fars, rows_in, grads_in, weights):
    k = len(fars)
    half, model = rows_in[0].shape
    tokens = 2 * half
    local, quarter, hidden = weights[0].shape
    count = model // quarter
    per_group = 2 * local
    blocks = [(side, g) for side in range(2) for g in range(k)]
    rows_each = len(blocks) * CAP

    def body(sc, *refs):
        x_ins, refs = refs[: 4 * k], refs[4 * k :]
        g_refs, refs = refs[:2], refs[2:]
        w_refs, refs = refs[: len(weights)], refs[len(weights) :]
        na_out, nb_out, ya_out, yb_out, h_out, d_out, go_out = refs[:7]
        st_ref, gate_ref, ns_ref, ys_ref, h_ref, d_ref, go_ref, g_held, w_held, x_held, sum_ref, sems = refs[7:]

        def weight(p, e, m):
            return w_held[3 * p + m, e]

        copies = (
            pltpu.make_async_copy(d_ref, d_out, sems.at[0]),
            pltpu.make_async_copy(go_ref, go_out, sems.at[1]),
        )
        hidden_copy = pltpu.make_async_copy(h_ref, h_out, sems.at[2])
        grad_copies = [
            pltpu.make_async_copy(g_refs[side].at[sc[1] ^ fars[g]], g_held.at[n], sems.at[3 + n])
            for n, (side, g) in enumerate(blocks)
        ]
        first_sem = 3 + len(blocks) + len(weights)
        row_copies = [
            pltpu.make_async_copy(x_ins[n], x_held.at[n], sems.at[first_sem + n])
            for n in range(4 * k)
        ]
        sum_copies = [
            pltpu.make_async_copy(sum_ref.at[n], out, sems.at[first_sem + 4 * k + n])
            for n, out in enumerate((na_out, nb_out, ya_out, yb_out))
        ]
        weight_copies = [
            pltpu.make_async_copy(w_refs[n], w_held.at[n], sems.at[3 + len(blocks) + n])
            for n in range(len(weights))
        ]
        for n in range(len(blocks)):
            for copy in (grad_copies[n], row_copies[2 * n], row_copies[2 * n + 1]):
                copy.start()
        for copy in weight_copies:
            copy.start()
        base = sc[1] * per_group + (sc[0] % 2) * local
        slot_row = lax.broadcasted_iota(jnp.int32, (CAP, tokens), 0).astype(F32)
        for n, (side, g) in enumerate(blocks):
            rows = slice(n * CAP, (n + 1) * CAP)
            grad_copies[n].wait()
            table = g_held[n, :, model : model + LANES].astype(F32).T
            ids, slots = table[:TOPK], table[TOPK : 2 * TOPK] - CAP
            gates = table[2 * TOPK : 3 * TOPK] + table[3 * TOPK : 4 * TOPK]
            picks = []
            for e in range(local):
                hit = ids == (base + e).astype(F32)
                slot = jnp.sum(jnp.where(hit, slots, 0.0), axis=0, keepdims=True) + CAP
                gate = jnp.sum(jnp.where(hit, gates, 0.0), axis=0, keepdims=True)
                pick = slot_row == slot
                value = jnp.sum(jnp.where(pick, gate, 0.0), axis=1, keepdims=True)
                gate_ref[e, rows, :] = jnp.broadcast_to(value, (CAP, LANES))
                picks.append(jnp.where(pick, 1.0, 0.0))
            row_copies[2 * n].wait()
            row_copies[2 * n + 1].wait()
            pick = jnp.concatenate(picks, axis=0)
            st_ref[n] = pick.T.astype(BF16)
            pick = pick.astype(BF16)
            for p in range(count):
                cols = columns(sc, p, quarter)
                values = jnp.concatenate(
                    [x_held[2 * n, :, cols], x_held[2 * n + 1, :, cols]], axis=0
                )
                got = dot_nn(pick, values).astype(BF16)
                grad = dot_nn(pick, g_held[n, :, cols])
                for e in range(local):
                    here = slice(e * CAP, (e + 1) * CAP)
                    d_ref[e, rows, p * quarter : (p + 1) * quarter] = got[here]
                    go_ref[e, rows, p * quarter : (p + 1) * quarter] = (
                        grad[here] * gate_ref[e, rows, 0:1]
                    ).astype(BF16)
        for copy in copies:
            copy.start()
        for copy in weight_copies:
            copy.wait()

        @pl.loop(0, local)
        def _(e):
            gate = up = act_grad = None
            for p in range(count):
                cols = slice(p * quarter, (p + 1) * quarter)
                rows = d_ref[e, :, cols]
                a = dot_nn(rows, weight(p, e, 0))
                b = dot_nn(rows, weight(p, e, 1))
                c = dot_nn(go_ref[e, :, cols], weight(p, e, 2))
                gate = a if gate is None else gate + a
                up = b if up is None else up + b
                act_grad = c if act_grad is None else act_grad + c
            sig = jax.nn.sigmoid(gate)
            silu = gate * sig
            act = (silu * up).astype(BF16)
            up_grad = (act_grad * silu).astype(BF16)
            gate_grad = (act_grad * up * sig * (1.0 + gate * (1.0 - sig))).astype(BF16)
            h_ref[e, :, :hidden] = act
            h_ref[e, :, hidden : 2 * hidden] = gate_grad
            h_ref[e, :, 2 * hidden :] = up_grad
            scale = gate_ref[e, :, 0:1]
            for p in range(count):
                cols = slice(p * quarter, (p + 1) * quarter)
                ns_ref[e, :, cols] = (
                    dot_nt(gate_grad, weight(p, e, 0)) + dot_nt(up_grad, weight(p, e, 1))
                ).astype(BF16)
                ys_ref[e, :, cols] = (dot_nt(act, weight(p, e, 2)) * scale).astype(BF16)

        hidden_copy.start()
        for at, source in ((0, ns_ref), (2, ys_ref)):
            for n, (side, g) in enumerate(blocks):
                rows = slice(n * CAP, (n + 1) * CAP)
                for p in range(count):
                    cols = slice(p * quarter, (p + 1) * quarter)
                    stacked = jnp.concatenate([source[e, rows, cols] for e in range(local)], axis=0)
                    sum_ref[at + side, g, :, columns(sc, p, quarter)] = dot_nn(
                        st_ref[n], stacked
                    ).astype(BF16)
                if g == k - 1:
                    sum_copies[at + side].start()
        for copy in (*copies, hidden_copy, *sum_copies):
            copy.wait()

    outside = pl.BlockSpec(memory_space=pltpu.HBM)
    sums = sds((k, tokens, model), BF16)
    rows = sds((local, rows_each, model), BF16)
    return pl.pallas_call(
        body,
        out_shape=[sums] * 4 + [sds((local, rows_each, 3 * hidden), BF16), rows, rows],
        grid_spec=pltpu.PrefetchScalarGridSpec(
            num_scalar_prefetch=1,
            grid=(1,),
            in_specs=[outside] * (4 * k + 2 + len(weights)),
            out_specs=[outside] * 7,
            scratch_shapes=[
                pltpu.VMEM((len(blocks), tokens, local * CAP), BF16),
                pltpu.VMEM((local, rows_each, LANES), F32),
                pltpu.VMEM((local, rows_each, model), BF16),
                pltpu.VMEM((local, rows_each, model), BF16),
                pltpu.VMEM((local, rows_each, 3 * hidden), BF16),
                pltpu.VMEM((local, rows_each, model), BF16),
                pltpu.VMEM((local, rows_each, model), BF16),
                pltpu.VMEM((len(blocks), tokens, model + LANES), BF16),
                pltpu.VMEM((len(weights), local, quarter, hidden), BF16),
                pltpu.VMEM((4 * k, half, model), BF16),
                pltpu.VMEM((4, k, tokens, model), BF16),
                pltpu.SemaphoreType.DMA((3 + len(blocks) + len(weights) + 4 * k + 4,)),
            ],
        ),
        compiler_params=params(58),
        cost_estimate=cost(
            2 * local * rows_each * model * (6 * hidden + 4 * tokens),
            2 * 3 * count * local * quarter * hidden + 24 * k * tokens * model,
            local * rows_each * hidden,
        ),
        name="experts",
    )(scalars, *rows_in, *grads_in, *weights)


def far_sets(local):
    mate = [(1, e) for e in range(local)]
    own = [(0, e) for e in range(local)]
    if local != 4:
        return [[v] for v in (*mate, *own)]
    return [mate[:1], mate[1:2], mate[2:] + own[:1], own[1:2], own[2:]]


def expert_weight_grads(row_sets, grad_sets, hidden_sets, quarter):
    groups = len(row_sets)
    local, _, model = row_sets[0].shape
    sets = far_sets(local)
    hidden = hidden_sets[0].shape[2] // 3
    count = model // quarter
    chunks, rows = [[]], 0
    for g in range(groups):
        if sum(row_sets[k].shape[1] for k in chunks[-1]) >= 8 * CAP:
            chunks.append([])
        chunks[-1].append(g)
        rows += row_sets[g].shape[1]

    def body(*refs):
        d_refs, go_refs, h_refs = refs[:groups], refs[groups : 2 * groups], refs[2 * groups : 3 * groups]
        keep_refs, far_refs = refs[3 * groups : 3 * groups + 2], refs[3 * groups + 2 :]
        expert = pl.program_id(0)
        far = []
        for p in range(count):
            cols = slice(p * quarter, (p + 1) * quarter)
            sums = [None, None, None]
            for chosen in chunks:
                left = jnp.concatenate([d_refs[g][0, :, cols] for g in chosen], axis=0)
                left_out = jnp.concatenate([go_refs[g][0, :, cols] for g in chosen], axis=0)
                right = jnp.concatenate([h_refs[g][0] for g in chosen], axis=0)
                parts = (
                    dot_tn(left, right[:, hidden : 2 * hidden]),
                    dot_tn(left, right[:, 2 * hidden :]),
                    dot_tn(left_out, right[:, :hidden]),
                )
                sums = [a if b is None else a + b for a, b in zip(parts, sums)]
            for k in range(3):
                if p < 2:
                    keep_refs[p][0, k] = sums[k].astype(BF16)
                else:
                    far.append(sums[k].astype(BF16))
        for ref, chosen in zip(far_refs, sets):
            for n, (which, e) in enumerate(chosen):

                @pl.when(expert == e)
                def _():
                    for k in range(3):
                        ref[3 * n + k] = far[3 * which + k]

    by_expert = lambda shape: pl.BlockSpec((1,) + shape, lambda e: (e,) + (0,) * len(shape))
    fars = [(3 * len(chosen), quarter, hidden) for chosen in sets]
    return pl.pallas_call(
        body,
        out_shape=[sds((local, 3, quarter, hidden), BF16)] * 2 + [sds(f, BF16) for f in fars],
        grid=(local,),
        in_specs=[by_expert(a.shape[1:]) for a in (*row_sets, *grad_sets, *hidden_sets)],
        out_specs=[by_expert((3, quarter, hidden))] * 2 + [whole(f) for f in fars],
        compiler_params=params(56),
        cost_estimate=cost(
            6 * local * rows * model * hidden,
            2 * local * rows * (2 * model + 3 * hidden) + 3 * local * 3 * model * hidden,
        ),
        name="expert_weight_grads",
    )(*row_sets, *grad_sets, *hidden_sets)


def middle_grad(scalars, parts, residual, grad_out, gains):
    tokens, model = grad_out.shape
    half = tokens // 2
    count = len(parts)

    def body(sc, *refs):
        part_refs = refs[:count]
        res_ref, go_ref, gain_ref, rg_ref, branch_ref, sum_ref = refs[count:]
        total = part_refs[0][...].astype(F32)
        for k in range(1, count):
            total = total + part_refs[k][...].astype(F32)
        residual = res_ref[...]
        start = pl.multiple_of(sc[2] * half, half)
        inverse = lax.rsqrt(jnp.mean(residual * residual, axis=-1, keepdims=True) + EPS)
        scaled = gain_ref[1:2, :] * total
        shift = jnp.mean(scaled * residual, axis=-1, keepdims=True)
        grad = (
            go_ref[pl.ds(start, half)].astype(F32)
            + inverse * scaled
            - residual * (inverse * inverse * inverse * shift)
        )
        rg_ref[...] = grad
        branch_ref[...] = grad.astype(BF16)
        sum_ref[...] = jnp.broadcast_to(
            jnp.sum(total * residual * inverse, axis=0, keepdims=True), (8, model)
        )

    return pl.pallas_call(
        body,
        out_shape=[sds((half, model), F32), sds((half, model), BF16), sds((8, model), F32)],
        grid_spec=pltpu.PrefetchScalarGridSpec(
            num_scalar_prefetch=1,
            grid=(1,),
            in_specs=[whole((half, model))] * (count + 1)
            + [whole((tokens, model)), whole((8, model))],
            out_specs=[whole((half, model)), whole((half, model)), whole((8, model))],
        ),
        compiler_params=params(12),
        cost_estimate=cost(20 * half * model, 24 * half * model),
        name="middle_grad",
    )(scalars, *parts, residual, grad_out, gains)


def attend_grad(scalars, branch, queries, kv_all, lse, out_pieces, cos_table, sin_table, piece_count):
    tokens, q_width = queries.shape
    length, kv2 = kv_all.shape
    kv_width = kv2 // 2
    kv_heads = kv_width // HEAD_DIM
    heads = q_width + kv2
    pair_blocks = kv_width // LANES
    count = len(out_pieces)
    quarter = out_pieces[0].shape[0]
    model = quarter * count
    half = tokens // 2

    def body(sc, b0_ref, b1_ref, q_ref, k_ref, v_ref, lse_ref, cos_ref, sin_ref, *rest):
        own = rows_at(sc[1], tokens)
        out_refs = rest[:count]
        dq_ref, dkv_ref, mg_ref, bias_ref = rest[count:]
        c = pl.program_id(0)

        @pl.when(c == 0)
        def _():
            cols = lax.broadcasted_iota(jnp.int32, (length, tokens), 0)
            rows = lax.broadcasted_iota(jnp.int32, (length, tokens), 1)
            query_pos = token_position(sc, rows, sc[1], tokens)
            key_pos = token_position(sc, cols % tokens, cols // tokens, tokens)
            bias_ref[...] = seen_bias(sc, query_pos, key_pos, piece_count)
            total = None
            for p in range(count):
                col = columns(sc, p, quarter)
                block = jnp.concatenate([b0_ref[:, col], b1_ref[:, col]], axis=0)
                part = dot_nn(block, out_refs[p][...])
                total = part if total is None else total + part
            mg_ref[...] = total.astype(BF16)

        low = lax.broadcasted_iota(jnp.int32, (1, LANES), 1) < HEAD_DIM
        mine = low == (c % 2 == 0)
        keys = k_ref[...].astype(F32)
        keys = jnp.where(mine, keys, pltpu.roll(keys, HEAD_DIM, 1)).astype(BF16)
        vals = v_ref[...].astype(F32)
        vals = jnp.where(mine, vals, pltpu.roll(vals, HEAD_DIM, 1)).astype(BF16)
        query = q_ref[...]
        grad = mg_ref[:, pl.ds(pl.multiple_of(c * LANES, LANES), LANES)]
        zero = jnp.zeros_like(query)
        lse_t = lse_ref[...].T
        dqs = []
        dk = dv = None
        for g in range(2):
            query_g = jnp.where(low, query, zero) if g == 0 else jnp.where(low, zero, query)
            grad_g = jnp.where(low, grad, zero) if g == 0 else jnp.where(low, zero, grad)
            scores = dot_nt(keys, query_g) + bias_ref[...]
            probs = jnp.exp(scores - lse_t[g * HEAD_DIM : g * HEAD_DIM + 1])
            prob_grad = dot_nt(vals, grad_g)
            delta = jnp.sum(probs * prob_grad, axis=0, keepdims=True)
            score_grad = (probs * (prob_grad - delta)).astype(BF16)
            dqs.append(dot_tn(score_grad, keys))
            dk_g = dot_nn(score_grad, query_g)
            dv_g = dot_nn(probs.astype(BF16), grad_g)
            dk = dk_g if dk is None else dk + dk_g
            dv = dv_g if dv is None else dv + dv_g
        dq = jnp.where(low, dqs[0], dqs[1]) * HEAD_DIM**-0.5
        dq_ref[...] = turn(dq, cos_ref[own], -sin_ref[own]).astype(BF16)
        dk = turn(dk, cos_ref[...], -sin_ref[...])
        for k, value in ((0, dk), (pair_blocks, dv)):
            value = (value + pltpu.roll(value, HEAD_DIM, 1)).astype(BF16)
            where = pl.ds(pl.multiple_of((k + c // 2) * LANES, LANES), LANES)
            dkv_ref[:, where] = jnp.where(mine, value, dkv_ref[:, where])

    return pl.pallas_call(
        body,
        out_shape=[sds((tokens, q_width), BF16), sds((length, kv2), BF16)],
        grid_spec=pltpu.PrefetchScalarGridSpec(
            num_scalar_prefetch=1,
            grid=(kv_heads,),
            in_specs=[
                whole((half, model)),
                whole((half, model)),
                pl.BlockSpec((tokens, LANES), lambda c, sc: (0, c)),
                pl.BlockSpec((length, LANES), lambda c, sc: (0, c // 2)),
                pl.BlockSpec((length, LANES), lambda c, sc: (0, pair_blocks + c // 2)),
                pl.BlockSpec((tokens, LANES), lambda c, sc: (0, c)),
                whole((length, LANES)),
                whole((length, LANES)),
            ]
            + [pl.BlockSpec((quarter, q_width), lambda c, sc: (0, heads // q_width))] * count,
            out_specs=[
                pl.BlockSpec((tokens, LANES), lambda c, sc: (0, c)),
                whole((length, kv2)),
            ],
            scratch_shapes=[
                pltpu.VMEM((tokens, q_width), BF16),
                pltpu.VMEM((length, tokens), F32),
            ],
        ),
        compiler_params=params(58),
        cost_estimate=cost(
            40 * tokens * length * LANES + 2 * tokens * q_width * model,
            6 * length * kv2 + 8 * tokens * model,
            2 * kv_heads * tokens * length,
        ),
        name="attend_grad",
    )(scalars, *branch, queries, kv_all, kv_all, lse, cos_table, sin_table, *out_pieces)


def weight_grads(scalars, normed, dq, dkv, branch, mixed, extra, quarter):
    length, model = normed.shape
    tokens, q_width = dq.shape
    kv2 = dkv.shape[1]
    width = q_width + kv2 + mixed.shape[1]
    count = model // quarter
    outs = [((quarter, width + LANES), BF16)] * 2 + [((2, quarter, width + LANES), BF16)]

    def body(sc, xn_ref, dq_ref, dkv_ref, b0_ref, b1_ref, mixed_ref, extra_ref, *out_refs):
        own = rows_at(sc[1], tokens)
        rows = lax.broadcasted_iota(jnp.int32, (quarter, quarter), 0)
        diagonal = rows == lax.broadcasted_iota(jnp.int32, (quarter, quarter), 1)
        for p in range(count):
            cols = columns(sc, p, quarter)
            ref = (out_refs[0], None, out_refs[1], None)[p]
            block = jnp.concatenate([b0_ref[:, cols], b1_ref[:, cols]], axis=0)
            column = jnp.sum(jnp.where(diagonal, extra_ref[0:1, cols], 0.0), axis=1, keepdims=True)
            at = 0
            for value in (
                dot_tn(xn_ref[own, cols], dq_ref[...]),
                dot_tn(xn_ref[:, cols], dkv_ref[...]),
                dot_tn(block, mixed_ref[...]),
                jnp.broadcast_to(column, (quarter, LANES)),
            ):
                here = slice(at, at + value.shape[1])
                at += value.shape[1]
                if ref is not None:
                    ref[:, here] = value.astype(BF16)
                else:
                    out_refs[2][p // 2, :, here] = value.astype(BF16)

    arrays = (normed, dq, dkv, *branch, mixed, extra)
    return pl.pallas_call(
        body,
        out_shape=[sds(*o) for o in outs],
        grid_spec=pltpu.PrefetchScalarGridSpec(
            num_scalar_prefetch=1,
            grid=(1,),
            in_specs=[whole(a.shape) for a in arrays],
            out_specs=[whole(o[0]) for o in outs],
        ),
        compiler_params=params(58),
        cost_estimate=cost(
            2 * model * (tokens * (q_width + mixed.shape[1]) + length * kv2),
            2 * length * (model + kv2) + 3 * model * width,
        ),
        name="weight_grads",
    )(scalars, *arrays)


def gather_expert_grads(scalars, keep, far, mates, sent):
    local, _, quarter, hidden = keep.shape
    sets = far_sets(local)
    chosen = range(len(sets) - len(far), len(sets)) if sent is not None else range(len(far))
    places = [
        (i, 3 * k, v[1])
        for i, n in enumerate(chosen)
        for k, v in enumerate(sets[n])
        if v[0] == 0
    ]
    used = sorted({i for i, _, _ in places})
    experts_here = [e for _, _, e in places]
    lowest = min(experts_here) if experts_here else 0
    count = len(experts_here)
    held = [] if sent is None else [sent]
    mates_here = [] if mates is None else [mates]
    steps = count + (local if mates_here else 0)

    def place(step, sc):
        core = sc[0] % 2
        mine = core * local + lowest + step
        return jnp.where(step < count, mine, (1 - core) * local + step - count)

    def body(sc, keep_ref, *rest):
        far_refs, out_ref = dict(zip(used, rest)), rest[-1]
        step = pl.program_id(0)
        for i, start, expert in places:

            @pl.when(step == expert - lowest)
            def _():
                out_ref[0] = keep_ref[0].astype(F32) + far_refs[i][start : start + 3].astype(F32)

        if mates_here:

            @pl.when(step >= count)
            def _():
                out_ref[0] = rest[len(used)][0].astype(F32)

    block = (1, 3, quarter, hidden)
    own = lambda step, sc: (lowest + jnp.minimum(step, max(count - 1, 0)), 0, 0, 0)
    other = lambda step, sc: (jnp.maximum(step - count, 0), 0, 0, 0)
    arrays = [keep, *[far[i] for i in used], *mates_here, *held]
    return pl.pallas_call(
        body,
        out_shape=sds((2 * local, 3, quarter, hidden), F32),
        grid_spec=pltpu.PrefetchScalarGridSpec(
            num_scalar_prefetch=1,
            grid=(steps,),
            in_specs=[pl.BlockSpec(block, own)]
            + [whole(far[i].shape) for i in used]
            + [pl.BlockSpec(block, other)] * len(mates_here)
            + [pl.BlockSpec(memory_space=pl.ANY)] * len(held),
            out_specs=pl.BlockSpec(block, lambda step, sc: (place(step, sc), 0, 0, 0)),
        ),
        input_output_aliases={len(arrays): 0} if held else {},
        compiler_params=params(24),
        cost_estimate=cost(3 * steps * quarter * hidden, 3 * 10 * steps * quarter * hidden),
        name="gather_expert_grads",
    )(scalars, *arrays)


def back(scalars, dq, dkv, pieces):
    tokens, q_width = dq.shape
    groups, _, kv2 = dkv.shape
    heads = q_width + kv2
    count = len(pieces)
    quarter = pieces[0].shape[0]
    model = count * quarter
    half = tokens // 2

    def body(sc, dq_ref, dkv_ref, *rest):
        piece_refs = rest[:count]
        own_ref, send_ref = rest[count:]
        total = dkv_ref[0].astype(F32)
        for g in range(1, groups):
            total = total + dkv_ref[g].astype(F32)
        dl_kv = total.astype(BF16)
        dl_q = dq_ref[...]
        for p in range(count):
            cols = columns(sc, p, quarter)
            part = dot_nt(dl_q, piece_refs[p][:, :q_width]) + dot_nt(
                dl_kv, piece_refs[p][:, q_width:heads]
            )
            own_ref[:, cols] = part[:half]
            send_ref[:, cols] = part[half:].astype(BF16)

    arrays = (dq, dkv, *pieces)
    return pl.pallas_call(
        body,
        out_shape=[sds((half, model), F32), sds((half, model), BF16)],
        grid_spec=pltpu.PrefetchScalarGridSpec(
            num_scalar_prefetch=1,
            grid=(1,),
            in_specs=[whole(dq.shape), whole(dkv.shape)] + [whole((quarter, heads))] * count,
            out_specs=[whole((half, model))] * 2,
        ),
        compiler_params=params(58),
        cost_estimate=cost(2 * tokens * model * heads, 2 * model * (heads + 2 * tokens)),
        name="back",
    )(scalars, *arrays)


def last_grad(scalars, layer_input, own, received, residual_grad, gains):
    tokens, model = layer_input.shape
    half = tokens // 2

    def body(sc, x_ref, own_ref, rec_ref, rg_ref, gain_ref, out_ref):
        start = pl.multiple_of(sc[2] * half, half)
        values = x_ref[pl.ds(start, half)].astype(F32)
        inverse = lax.rsqrt(jnp.mean(values * values, axis=-1, keepdims=True) + EPS)
        scaled = gain_ref[0:1, :] * (own_ref[...] + rec_ref[...].astype(F32))
        shift = jnp.mean(scaled * values, axis=-1, keepdims=True)
        out_ref[...] = (
            rg_ref[...] + inverse * scaled - values * (inverse * inverse * inverse * shift)
        ).astype(BF16)

    return pl.pallas_call(
        body,
        out_shape=sds((half, model), BF16),
        grid_spec=pltpu.PrefetchScalarGridSpec(
            num_scalar_prefetch=1,
            grid=(1,),
            in_specs=[
                whole((tokens, model)),
                whole((half, model)),
                whole((half, model)),
                whole((half, model)),
                whole((8, model)),
            ],
            out_specs=whole((half, model)),
        ),
        compiler_params=params(8),
        cost_estimate=cost(12 * half * model, 14 * half * model),
        name="last_grad",
    )(scalars, layer_input, own, received, residual_grad, gains)


def local(
    layer_input,
    attn_norm,
    w_query,
    w_key,
    w_value,
    w_out,
    moe_norm,
    expert_weights,
    expert_ids,
    slot_ids,
    gate_values,
    piece_starts,
    grad_out,
):
    _, tokens, model = layer_input.shape
    half = tokens // 2
    groups = lax.axis_size("ctx")
    shard = lax.axis_index("shard")
    group = lax.axis_index("ctx")
    side = lax.axis_index("tp")
    piece_count = piece_starts.shape[1]
    scalars = jnp.concatenate(
        [jnp.stack([shard, group, side]).astype(jnp.int32), piece_starts[0]]
    )
    flat_input = layer_input[0]
    flat_grad = grad_out[0]
    q_width, kv_width = w_query.shape[1], w_key.shape[1]
    rows_here = w_query.shape[0]
    quarter = rows_here * groups

    own_input = jnp.where(side == 0, flat_input[:half], flat_input[half:])
    local_experts = expert_weights.shape[0] // 2
    core = shard % 2


    def experts_of(which, m):
        start = (which * local_experts, m, 0, 0)
        size = (local_experts, 1) + expert_weights.shape[2:]
        return lax.dynamic_slice(expert_weights, start, size)[:, 0]

    mine = [experts_of(core, m) for m in range(3)]
    given = [experts_of(1 - core, m) for m in range(3)]
    weight_block = jnp.concatenate(
        [
            after(w_query, *mine),
            w_key,
            w_value,
            w_out.T,
            attn_norm[:, None],
            moe_norm[:, None],
            jnp.zeros((rows_here, LANES - 2), BF16),
        ],
        axis=1,
    )

    index = jnp.arange(groups * tokens, dtype=jnp.int32)
    positions = (index ^ (side * half).astype(jnp.int32)).astype(F32)
    lane = jnp.arange(LANES, dtype=jnp.int32)
    step = (lane % (HEAD_DIM // 2)).astype(F32)
    angles = positions[:, None] * (1.0 / 10000.0 ** (step * 2.0 / HEAD_DIM))[None, :]
    cos_table = jnp.cos(angles)
    sin_table = jnp.sin(angles) * jnp.where(lane % HEAD_DIM < HEAD_DIM // 2, -1.0, 1.0)[None, :]

    gate_high = gate_values[0].astype(BF16)
    gate_low = (gate_values[0] - gate_high.astype(F32)).astype(BF16)
    routing = jnp.concatenate(
        [
            expert_ids[0].astype(BF16),
            slot_ids[0].astype(BF16),
            gate_high,
            gate_low,
            jnp.zeros((tokens, LANES - 4 * TOPK), BF16),
        ],
        axis=1,
    )
    grad_block = spread_grads(scalars, flat_grad, routing, groups)

    near = [1, 3] if groups == 4 else [1]
    rest = [b for b in range(1, groups) if b not in near]
    block_0, own_input, cos_table, sin_table, grad_block, far_0, far_1, *kept = fence(
        spread(weight_block, "ctx").reshape(quarter, -1),
        own_input,
        cos_table,
        sin_table,
        grad_block,
        swap(mine[0], "shard", 2),
        swap(mine[1], "shard", 2),
        *mine,
        *given,
        *[swap(own_input, "ctx", b) for b in near],
    )
    mine, given = kept[:3], kept[3:6]
    input_at = dict(zip(near, kept[6:]))
    halves = [swap(input_at[b], "tp", 1) for b in near]
    block_0, block_2, *kept = fence(
        block_0,
        swap(block_0, "shard", 2),
        *halves,
        *[swap(own_input, "ctx", b) for b in rest],
    )
    crossed = dict(zip(near, kept[: len(near)]))
    input_at.update(dict(zip(rest, kept[len(near) :])))
    grads_own = lax.all_to_all(after(grad_block, block_2), "ctx", 0, 0, tiled=True)
    block_0, block_1, block_2, block_3, taken_0, *kept = fence(
        block_0,
        swap(block_0, "shard", 1),
        block_2,
        swap(block_2, "shard", 1),
        swap(after(given[0], block_2), "shard", 1),
        *[swap(input_at[b], "tp", 1) for b in rest],
    )
    crossed.update(dict(zip(rest, kept)))
    pieces = [block_0, block_1, block_2, block_3]
    others = [v for b in range(1, groups) for v in (input_at[b], crossed[b])]

    normed_all, queries, kv_all, gains = front(
        scalars, flat_input, others, pieces, cos_table, sin_table, (q_width, kv_width)
    )
    mixed, lse, attention_own, attention_send = attend(
        scalars, queries, kv_all, pieces, piece_count
    )
    attention_send, far_2, far_3, taken_2, taken_1 = fence(
        attention_send,
        swap(after(mine[2], block_1), "shard", 2),
        swap(after(taken_0, block_1), "shard", 2),
        swap(after(given[2], block_1), "shard", 1),
        swap(after(given[1], block_1), "shard", 1),
    )
    attention_got, far_4 = fence(
        swap(attention_send, "tp", 1), swap(after(taken_1, attention_send), "shard", 2)
    )
    residual, normed_two = second_norm(
        scalars, flat_input, attention_own, attention_got, gains
    )

    calls = [[0], *[[b, b + 1] for b in range(1, groups - 1, 2)], [groups - 1]]
    far_5 = swap(after(taken_2, far_4), "shard", 2)
    grads_own = after(grads_own, residual)
    normed_two, crossed, grads_own, grads_mate, far_5, *arrived = fence(
        normed_two,
        swap(normed_two, "tp", 1),
        grads_own,
        swap(grads_own, "shard", 1),
        far_5,
        *[swap(normed_two, "ctx", b) for b in calls[1]],
    )
    tokens_at = {0: normed_two, **dict(zip(calls[1], arrived))}
    grads_in = [grads_own, grads_mate]
    taken = [taken_0, taken_1, taken_2]
    expert_pieces = [*mine, *taken, far_0, far_1, far_2, far_3, far_4, far_5]
    rows_in = [normed_two, crossed, swap(normed_two, "shard", 1), swap(crossed, "shard", 1)]

    def summed(own, got, part):
        return own[:, part].astype(F32) + got[:, part].astype(F32)

    low, high = slice(0, half), slice(half, tokens)
    row_sets, grad_sets, hidden_sets = [], [], []
    norm_parts, out_parts, out_sets = {}, {}, []
    waiting = None
    order = scalars
    for n, call in enumerate(calls):
        own, mate, out_own, out_mate, hiddens, rows, grads = experts(
            order, call, rows_in, grads_in, expert_pieces
        )
        row_sets.append(rows)
        grad_sets.append(grads)
        hidden_sets.append(hiddens)
        out_sets.append((call, out_own, out_mate))
        later = calls[n + 1] if n + 1 < len(calls) else []
        latest = calls[n + 2] if n + 2 < len(calls) else []
        own, mate, *arrived = fence(
            own,
            mate,
            *[swap(tokens_at[b], "tp", 1) for b in later],
            *[swap(tokens_at[b], "shard", 1) for b in later],
            *[swap(normed_two, "ctx", b) for b in latest],
            *([waiting[3]] if waiting is not None else []),
        )
        crossed, arrived = arrived[: len(later)], arrived[len(later) :]
        mates, arrived = arrived[: len(later)], arrived[len(later) :]
        tokens_at.update(dict(zip(latest, arrived)))
        if later:
            here = [v for b, c in zip(later, crossed) for v in (tokens_at[b], c)]
            there = [v for m, c in zip(mates, crossed) for v in (m, swap(c, "shard", 1))]
            rows_in = [*here, *there]
        got = swap(mate, "shard", 1)
        sent = summed(own, got, high).astype(BF16)
        if waiting is not None:
            old_call, kept_own, old_got, _ = waiting
            kept = summed(kept_own, old_got, low) + arrived[-1].astype(F32)
            for i, b in enumerate(old_call):
                norm_parts[b] = kept[i] if b == 0 else swap(kept[i].astype(BF16), "ctx", b)
        waiting = (call, own, got, swap(sent, "tp", 1))
        order = after(scalars, sent)

    hidden_sets[-1] = after(hidden_sets[-1], sent)
    call, own, got, crossed = waiting
    early = [b for b in norm_parts if b > 0]
    mates = [swap(after(s[2], sent), "shard", 1) for s in out_sets[:-1]]
    keep_0, keep_1, *arrived = fence(
        *expert_weight_grads(row_sets, grad_sets, hidden_sets, quarter),
        crossed,
        *[norm_parts[b] for b in early],
        *mates,
    )
    fars = len(arrived) - 1 - len(early) - len(mates)
    far_sent, crossed, arrived = arrived[:fars], arrived[fars], arrived[fars + 1 :]
    far_got = []

    def send_far(count, *ready):
        start = len(far_got)
        got = [swap(after(v, *ready), "shard", 2) for v in far_sent[start : start + count]]
        far_got.extend(got)
        return got

    def keep_far(got):
        if got:
            far_got[len(far_got) - len(got) :] = got

    norm_parts.update(dict(zip(early, arrived)))
    mates = arrived[len(early) :]
    kept = summed(own, got, low) + crossed.astype(F32)
    for i, b in enumerate(call):
        norm_parts[b] = swap(kept[i].astype(BF16), "ctx", b)

    outs = [(s[0], after(s[1], kept), m) for s, m in zip(out_sets, mates)]
    middle, edges = outs[1:], outs[:1]
    out_crossed = [swap(summed(own, got, high).astype(BF16), "tp", 1) for _, own, got in middle]
    out_last = swap(after(out_sets[-1][2], kept), "shard", 1)
    sending = send_far(1, crossed)
    residual, out_last, *arrived = fence(
        residual, out_last, *[norm_parts[b] for b in range(groups)], *sending, *out_crossed
    )
    keep_far(arrived[groups : groups + len(sending)])
    out_crossed = arrived[groups + len(sending) :]
    arrived = arrived[:groups]
    residual_grad, branch_own, gain_row = middle_grad(
        scalars, arrived, residual, flat_grad, gains
    )
    sending = send_far(1, out_last)
    branch_own, branch_crossed, *sending = fence(branch_own, swap(branch_own, "tp", 1), *sending)
    keep_far(sending)
    branch = [branch_own, branch_crossed]
    for (call, own, got), crossed in zip(middle, out_crossed):
        kept = summed(after(own, branch_own), got, low) + crossed.astype(F32)
        for i, b in enumerate(call):
            out_parts[b] = swap(fence(kept[i].astype(BF16))[0], "ctx", b)
    moved = list(out_parts)
    edges.append((*out_sets[-1][:2], out_last))
    edges = [(call, after(own, branch_own), got) for call, own, got in edges]
    out_crossed = [swap(summed(own, got, high).astype(BF16), "tp", 1) for _, own, got in edges]

    dq, dkv_parts = attend_grad(
        scalars, branch, queries, kv_all, lse, pieces, cos_table, sin_table, piece_count
    )
    sending = send_far(1, branch_crossed)
    dq, dkv_parts, out_first, out_last, *arrived = fence(
        dq, dkv_parts, *out_crossed, *[out_parts[b] for b in moved], *sending
    )
    out_crossed = [out_first, out_last]
    out_parts.update(dict(zip(moved, arrived)))
    keep_far(arrived[len(moved) :])

    for (call, own, got), crossed in zip(edges, out_crossed):
        kept = summed(after(own, dq), got, low) + crossed.astype(F32)
        for i, b in enumerate(call):
            out_parts[b] = kept[i] if b == 0 else swap(fence(kept[i].astype(BF16))[0], "ctx", b)
    sending = send_far(1, dq)
    own_grads, far_grads, sent_grads, dkv_parts, *arrived = fence(
        *weight_grads(scalars, normed_all, dq, dkv_parts, branch, mixed, gain_row, quarter),
        dkv_parts,
        *[out_parts[b] for b in calls[-1]],
        *sending,
    )
    out_parts.update(dict(zip(calls[-1], arrived)))
    keep_far(arrived[len(calls[-1]) :])

    got_grads = fence(swap(sent_grads, "shard", 1))[0]
    passed = (far_grads.astype(F32) + got_grads[1].astype(F32)).astype(BF16)
    places = {
        v[1]: (n, 3 * k)
        for n, chosen in enumerate(far_sets(local_experts))
        for k, v in enumerate(chosen)
        if v[0] == 1
    }
    mates = jnp.stack(
        [
            (keep_1[e].astype(F32) + far_got[n][start : start + 3].astype(F32)).astype(BF16)
            for e, (n, start) in sorted(places.items())
        ]
    )
    kept_grads = (after(own_grads, mates).astype(F32) + got_grads[0].astype(F32)).astype(BF16)
    def natural(own, other):
        return jnp.where(
            side == 0,
            jnp.concatenate([own, other], axis=0),
            jnp.concatenate([other, own], axis=0),
        )[None]

    out_sum = after(residual, kept_grads)
    for b in range(groups):
        out_sum = out_sum + out_parts[b].astype(F32)
    out_half = out_sum.astype(BF16)
    output = natural(out_half, swap(out_half, "tp", 1))
    dkv, passed, kept_grads, output, mates = fence(
        lax.all_to_all(
            dkv_parts.reshape(groups, tokens, 2 * kv_width), "ctx", 0, 0, tiled=True
        ),
        swap(passed, "shard", 2),
        kept_grads,
        output,
        swap(mates, "shard", 1),
    )

    total = fence((kept_grads.astype(F32) + passed.astype(F32)).astype(BF16))[0]
    normed_own, normed_send = back(scalars, dq, dkv, pieces)
    input_half = last_grad(
        scalars, flat_input, normed_own, swap(normed_send, "tp", 1), residual_grad, gains
    )
    early = list(far_got)
    sending = send_far(len(far_sent), dkv)
    expert_grad = gather_expert_grads(scalars, keep_0, early, mates, None)
    total, input_half, input_other, expert_grad, *sending = fence(
        lax.all_to_all(
            total.reshape(groups, rows_here, total.shape[1]), "ctx", 0, 0, tiled=True
        ),
        input_half,
        swap(input_half, "tp", 1),
        expert_grad,
        *sending,
    )
    keep_far(sending)
    input_grad = natural(input_half, input_other)
    if sending:
        expert_grad = gather_expert_grads(scalars, keep_0, sending, None, expert_grad)
    total = jnp.sum(total.astype(F32), axis=0)
    query_grad = total[:, :q_width]
    key_grad = total[:, q_width : q_width + kv_width]
    value_grad = total[:, q_width + kv_width : q_width + 2 * kv_width]
    heads = q_width + 2 * kv_width
    out_grad = total[:, heads : heads + q_width].T
    moe_sum = total[:, heads + q_width]
    attn_sum = (
        jnp.sum(w_query.astype(F32) * query_grad, axis=1)
        + jnp.sum(w_key.astype(F32) * key_grad, axis=1)
        + jnp.sum(w_value.astype(F32) * value_grad, axis=1)
    )
    sums = jnp.stack([attn_sum, moe_sum])
    attn_sum, moe_norm_grad = sums + swap(sums, "tp", 1)
    attn_norm_grad = attn_sum / attn_norm.astype(F32)
    return (
        output,
        input_grad,
        attn_norm_grad,
        query_grad,
        key_grad,
        value_grad,
        out_grad,
        moe_norm_grad,
        expert_grad,
    )


def solution(mesh):
    in_specs = (
        P("shard", "ctx", None),
        P(("shard", "ctx")),
        P(("shard", "ctx"), "tp"),
        P(("shard", "ctx"), "tp"),
        P(("shard", "ctx"), "tp"),
        P("tp", ("shard", "ctx")),
        P(("shard", "ctx")),
        P("ctx", None, "shard", "tp"),
        P("shard", "ctx", None),
        P("shard", "ctx", None),
        P("shard", "ctx", None),
        P("shard", None),
        P("shard", "ctx", None),
    )
    out_specs = (
        P("shard", "ctx", None),
        P("shard", "ctx", None),
        P(("shard", "ctx")),
        P(("shard", "ctx"), "tp"),
        P(("shard", "ctx"), "tp"),
        P(("shard", "ctx"), "tp"),
        P("tp", ("shard", "ctx")),
        P(("shard", "ctx")),
        P("ctx", None, "shard", "tp"),
    )
    return jax.shard_map(local, mesh=mesh, in_specs=in_specs, out_specs=out_specs, check_vma=False)
```

```python
import functools

import jax
import jax.numpy as jnp
from jax import lax
from jax.experimental import pallas as pl
from jax.experimental.pallas import tpu as pltpu
from jax.sharding import PartitionSpec as P

HEAD_DIM = 64
EXPERTS = 32
TOPK = 8
PIECE = 256
CAP = 96
EPS = 1e-06
MASKED = -1e30
LANES = 128
F32 = jnp.float32
BF16 = jnp.bfloat16


def swap(value, axis, distance):
    size = lax.axis_size(axis)
    return lax.ppermute(value, axis, [(i, i ^ distance) for i in range(size)])


def spread(value, axis):
    size = lax.axis_size(axis)
    copies = jnp.broadcast_to(value[None], (size,) + value.shape)
    return lax.all_to_all(copies, axis, 0, 0, tiled=True)


def after(value, *others):
    return lax.optimization_barrier((value,) + others)[0]


def fence(*values):
    return lax.optimization_barrier(values)


def dot_nn(a, b):
    return lax.dot_general(a, b, (((1,), (0,)), ((), ())), preferred_element_type=F32)


def dot_nt(a, b):
    return lax.dot_general(a, b, (((1,), (1,)), ((), ())), preferred_element_type=F32)


def dot_tn(a, b):
    return lax.dot_general(a, b, (((0,), (0,)), ((), ())), preferred_element_type=F32)


def cost(flops, moved, special=0):
    return pl.CostEstimate(flops=int(flops), bytes_accessed=int(moved), transcendentals=int(special))


def params(megabytes, length=0):
    megabytes = 58 if length > 1024 else megabytes
    return pltpu.CompilerParams(vmem_limit_bytes=megabytes * 1024 * 1024)


def sds(shape, dtype):
    return jax.ShapeDtypeStruct(shape, dtype)


def whole(shape):
    return pl.BlockSpec(shape, lambda *_: (0,) * len(shape))


def turn(value, cosine, sine):
    lane = lax.broadcasted_iota(jnp.int32, (value.shape[0], LANES), 1) % HEAD_DIM
    first = lane < HEAD_DIM // 2
    parts = []
    for j in range(value.shape[1] // LANES):
        chunk = value[:, j * LANES : (j + 1) * LANES]
        partner = jnp.where(
            first,
            pltpu.roll(chunk, LANES - HEAD_DIM // 2, 1),
            pltpu.roll(chunk, HEAD_DIM // 2, 1),
        )
        parts.append(chunk * cosine + partner * sine)
    return parts[0] if len(parts) == 1 else jnp.concatenate(parts, axis=1)


def rows_at(index, size):
    return pl.ds(pl.multiple_of(index * size, size), size)


def columns(scalars, p, width):
    return pl.ds(pl.multiple_of((scalars[0] ^ p) * width, width), width)


def spread_grads(scalars, grads, routing, groups):
    tokens, model = grads.shape
    half = tokens // 2
    out = (groups, tokens, model + LANES)

    def body(sc, grads_ref, routing_ref, out_ref):
        for h in range(2):
            here = rows_at(sc[2] ^ h, half)
            out_ref[0, h * half : (h + 1) * half, :model] = grads_ref[here]
            out_ref[0, h * half : (h + 1) * half, model:] = routing_ref[here]

    return pl.pallas_call(
        body,
        out_shape=sds(out, BF16),
        grid_spec=pltpu.PrefetchScalarGridSpec(
            num_scalar_prefetch=1,
            grid=(groups,),
            in_specs=[whole(grads.shape), whole(routing.shape)],
            out_specs=pl.BlockSpec((1,) + out[1:], lambda g, sc: (g, 0, 0)),
        ),
        compiler_params=params(12),
        cost_estimate=cost(0, 2 * (groups + 1) * tokens * (model + LANES)),
        name="spread_grads",
    )(scalars, grads, routing)


def front(scalars, layer_input, others, pieces, cos_table, sin_table, widths):
    tokens, model = layer_input.shape
    quarter = pieces[0].shape[0]
    q_width, kv_width = widths
    heads = q_width + 2 * kv_width
    gain_column = pieces[0].shape[1] - LANES
    half = tokens // 2
    count = len(pieces)
    groups = 1 + len(others) // 2
    length = groups * tokens

    def body(sc, x_ref, *rest):
        other_refs, rest = rest[: len(others)], rest[len(others) :]
        piece_refs = rest[:count]
        cos_ref, sin_ref, xn_ref, q_ref, kv_ref, gain_ref = rest[count:]
        rows = lax.broadcasted_iota(jnp.int32, (quarter, quarter), 0)
        diagonal = rows == lax.broadcasted_iota(jnp.int32, (quarter, quarter), 1)
        for p in range(count):
            gains = piece_refs[p][:, gain_column : gain_column + LANES].astype(F32)
            for k in range(2):
                row = jnp.sum(jnp.where(diagonal, gains[:, k : k + 1], 0.0), axis=0, keepdims=True)
                gain_ref[k : k + 1, columns(sc, p, quarter)] = row
        gain = gain_ref[0:1, :]
        for b in range(groups):
            for h in range(2):
                if b == 0:
                    values = x_ref[rows_at(sc[2] ^ h, half)].astype(F32)
                else:
                    values = other_refs[2 * (b - 1) + h][...].astype(F32)
                inverse = lax.rsqrt(jnp.mean(values * values, axis=-1, keepdims=True) + EPS)
                xn_ref[rows_at(2 * (sc[1] ^ b) + h, half)] = (values * inverse * gain).astype(BF16)

        own = rows_at(sc[1], tokens)
        total = None
        for p in range(count):
            part = dot_nn(xn_ref[own, columns(sc, p, quarter)], piece_refs[p][:, :q_width])
            total = part if total is None else total + part
        total = turn(total, cos_ref[own], sin_ref[own]).astype(BF16)
        q_ref[...] = (total * HEAD_DIM**-0.5).astype(BF16)

        @pl.loop(0, groups)
        def _(g):
            here = rows_at(g, tokens)
            total = None
            for p in range(count):
                part = dot_nn(xn_ref[here, columns(sc, p, quarter)], piece_refs[p][:, q_width:heads])
                total = part if total is None else total + part
            kv_ref[here, :kv_width] = turn(total[:, :kv_width], cos_ref[here], sin_ref[here]).astype(
                BF16
            )
            kv_ref[here, kv_width:] = total[:, kv_width:].astype(BF16)

    outs = [
        ((length, model), BF16),
        ((tokens, q_width), BF16),
        ((length, 2 * kv_width), BF16),
        ((8, model), F32),
    ]
    arrays = (layer_input, *others, *pieces, cos_table, sin_table)
    return pl.pallas_call(
        body,
        out_shape=[sds(*o) for o in outs],
        grid_spec=pltpu.PrefetchScalarGridSpec(
            num_scalar_prefetch=1,
            grid=(1,),
            in_specs=[whole(a.shape) for a in arrays],
            out_specs=[whole(o[0]) for o in outs],
        ),
        compiler_params=params(58),
        cost_estimate=cost(
            2 * model * (tokens * q_width + length * 2 * kv_width),
            2 * model * (2 * length + heads) + 2 * length * (kv_width + 2 * LANES),
        ),
        name="front",
    )(scalars, *arrays)


def inside_piece(position, start):
    return (position >= start) & (position < start + PIECE)


def seen_bias(sc, query_pos, key_pos, piece_count):
    seen = key_pos <= query_pos
    for k in range(piece_count):
        start = sc[3 + k]
        seen = seen | (inside_piece(query_pos, start) & inside_piece(key_pos, start))
    return jnp.where(seen, 0.0, MASKED)


def token_position(sc, index, group, tokens):
    return group * tokens + (index ^ (sc[2] * (tokens // 2)))


def attend(scalars, queries, kv_all, out_pieces, piece_count):
    tokens, q_width = queries.shape
    length, kv2 = kv_all.shape
    kv_width = kv2 // 2
    kv_heads = kv_width // HEAD_DIM
    heads = q_width + kv2
    pair_blocks = kv_width // LANES
    count = len(out_pieces)
    quarter = out_pieces[0].shape[0]
    model = quarter * count
    half = tokens // 2

    def body(sc, q_ref, k_ref, v_ref, *rest):
        out_refs = rest[:count]
        mixed_ref, lse_ref, own_ref, send_ref, bias_ref = rest[count:]
        c = pl.program_id(0)

        @pl.when(c == 0)
        def _():
            rows = lax.broadcasted_iota(jnp.int32, (tokens, half), 0)
            cols = lax.broadcasted_iota(jnp.int32, (tokens, half), 1)
            query_pos = token_position(sc, rows, sc[1], tokens)
            for n in range(length // half):
                key_pos = cols + ((n // 2) * tokens + ((n % 2) ^ sc[2]) * half)
                bias_ref[:, n * half : (n + 1) * half] = seen_bias(
                    sc, query_pos, key_pos, piece_count
                )

        low = lax.broadcasted_iota(jnp.int32, (1, LANES), 1) < HEAD_DIM
        mine = low == (c % 2 == 0)
        keys = k_ref[...].astype(F32)
        keys = jnp.where(mine, keys, pltpu.roll(keys, HEAD_DIM, 1)).astype(BF16)
        vals = v_ref[...].astype(F32)
        vals = jnp.where(mine, vals, pltpu.roll(vals, HEAD_DIM, 1)).astype(BF16)
        query = q_ref[...]
        zero = jnp.zeros_like(query)
        outs, lses = [], []
        for part in (jnp.where(low, query, zero), jnp.where(low, zero, query)):
            scores = dot_nt(part, keys) + bias_ref[...]
            top = jnp.max(scores, axis=-1, keepdims=True)
            expo = jnp.exp(scores - top)
            total = jnp.sum(expo, axis=-1, keepdims=True)
            probs = expo * (1.0 / total)
            outs.append(dot_nn(probs.astype(BF16), vals))
            lses.append(top + jnp.log(total))
        mixed_ref[:, pl.ds(pl.multiple_of(c * LANES, LANES), LANES)] = jnp.where(
            low, outs[0], outs[1]
        ).astype(BF16)
        lse_ref[...] = jnp.where(low, lses[0], lses[1])

        @pl.when(c == kv_heads - 1)
        def _():
            mixed = mixed_ref[...]
            for p in range(count):
                part = dot_nt(mixed, out_refs[p][...])
                own_ref[:, columns(sc, p, quarter)] = part[:half]
                send_ref[:, columns(sc, p, quarter)] = part[half:].astype(BF16)

    return pl.pallas_call(
        body,
        out_shape=[
            sds((tokens, q_width), BF16),
            sds((tokens, kv_heads * LANES), F32),
            sds((half, model), F32),
            sds((half, model), BF16),
        ],
        grid_spec=pltpu.PrefetchScalarGridSpec(
            num_scalar_prefetch=1,
            grid=(kv_heads,),
            in_specs=[
                pl.BlockSpec((tokens, LANES), lambda c, sc: (0, c)),
                pl.BlockSpec((length, LANES), lambda c, sc: (0, c // 2)),
                pl.BlockSpec((length, LANES), lambda c, sc: (0, pair_blocks + c // 2)),
            ]
            + [pl.BlockSpec((quarter, q_width), lambda c, sc: (0, heads // q_width))] * count,
            out_specs=[
                whole((tokens, q_width)),
                pl.BlockSpec((tokens, LANES), lambda c, sc: (0, c)),
                whole((half, model)),
                whole((half, model)),
            ],
            scratch_shapes=[pltpu.VMEM((tokens, length), F32)],
        ),
        compiler_params=params(58),
        cost_estimate=cost(
            16 * tokens * length * LANES + 2 * tokens * q_width * model,
            4 * length * kv2 + 8 * tokens * model,
            2 * kv_heads * tokens * length,
        ),
        name="attend",
    )(scalars, queries, kv_all, kv_all, *out_pieces)


def second_norm(scalars, layer_input, own, received, gains):
    tokens, model = layer_input.shape
    half = tokens // 2

    def body(sc, x_ref, own_ref, rec_ref, gain_ref, res_ref, norm_ref):
        start = pl.multiple_of(sc[2] * half, half)
        residual = (
            x_ref[pl.ds(start, half)].astype(F32) + own_ref[...] + rec_ref[...].astype(F32)
        )
        inverse = lax.rsqrt(jnp.mean(residual * residual, axis=-1, keepdims=True) + EPS)
        res_ref[...] = residual
        norm_ref[...] = (residual * inverse * gain_ref[1:2, :]).astype(BF16)

    return pl.pallas_call(
        body,
        out_shape=[sds((half, model), F32), sds((half, model), BF16)],
        grid_spec=pltpu.PrefetchScalarGridSpec(
            num_scalar_prefetch=1,
            grid=(1,),
            in_specs=[
                whole((tokens, model)),
                whole((half, model)),
                whole((half, model)),
                whole((8, model)),
            ],
            out_specs=[whole((half, model)), whole((half, model))],
        ),
        compiler_params=params(8),
        cost_estimate=cost(10 * half * model, 16 * half * model),
        name="second_norm",
    )(scalars, layer_input, own, received, gains)


def experts(scalars, fars, rows_in, grads_in, weights):
    k = len(fars)
    half, model = rows_in[0].shape
    tokens = 2 * half
    local, quarter, hidden = weights[0].shape
    count = model // quarter
    per_group = 2 * local
    blocks = [(side, g) for side in range(2) for g in range(k)]
    rows_each = len(blocks) * CAP

    def body(sc, *refs):
        x_ins, refs = refs[: 4 * k], refs[4 * k :]
        g_refs, refs = refs[:2], refs[2:]
        w_refs, refs = refs[: len(weights)], refs[len(weights) :]
        na_out, nb_out, ya_out, yb_out, h_out, d_out, go_out = refs[:7]
        st_ref, gate_ref, ns_ref, ys_ref, h_ref, d_ref, go_ref, g_held, w_held, x_held, sum_ref, sems = refs[7:]

        def weight(p, e, m):
            return w_held[3 * p + m, e]

        copies = (
            pltpu.make_async_copy(d_ref, d_out, sems.at[0]),
            pltpu.make_async_copy(go_ref, go_out, sems.at[1]),
        )
        hidden_copy = pltpu.make_async_copy(h_ref, h_out, sems.at[2])
        grad_copies = [
            pltpu.make_async_copy(g_refs[side].at[sc[1] ^ fars[g]], g_held.at[n], sems.at[3 + n])
            for n, (side, g) in enumerate(blocks)
        ]
        first_sem = 3 + len(blocks) + len(weights)
        row_copies = [
            pltpu.make_async_copy(x_ins[n], x_held.at[n], sems.at[first_sem + n])
            for n in range(4 * k)
        ]
        sum_copies = [
            pltpu.make_async_copy(sum_ref.at[n], out, sems.at[first_sem + 4 * k + n])
            for n, out in enumerate((na_out, nb_out, ya_out, yb_out))
        ]
        weight_copies = [
            pltpu.make_async_copy(w_refs[n], w_held.at[n], sems.at[3 + len(blocks) + n])
            for n in range(len(weights))
        ]
        for n in range(len(blocks)):
            for copy in (grad_copies[n], row_copies[2 * n], row_copies[2 * n + 1]):
                copy.start()
        for copy in weight_copies:
            copy.start()
        base = sc[1] * per_group + (sc[0] % 2) * local
        slot_row = lax.broadcasted_iota(jnp.int32, (CAP, tokens), 0).astype(F32)
        for n, (side, g) in enumerate(blocks):
            rows = slice(n * CAP, (n + 1) * CAP)
            grad_copies[n].wait()
            table = g_held[n, :, model : model + LANES].astype(F32).T
            ids, slots = table[:TOPK], table[TOPK : 2 * TOPK] - CAP
            gates = table[2 * TOPK : 3 * TOPK] + table[3 * TOPK : 4 * TOPK]
            picks = []
            for e in range(local):
                hit = ids == (base + e).astype(F32)
                slot = jnp.sum(jnp.where(hit, slots, 0.0), axis=0, keepdims=True) + CAP
                gate = jnp.sum(jnp.where(hit, gates, 0.0), axis=0, keepdims=True)
                pick = slot_row == slot
                value = jnp.sum(jnp.where(pick, gate, 0.0), axis=1, keepdims=True)
                gate_ref[e, rows, :] = jnp.broadcast_to(value, (CAP, LANES))
                picks.append(jnp.where(pick, 1.0, 0.0))
            row_copies[2 * n].wait()
            row_copies[2 * n + 1].wait()
            pick = jnp.concatenate(picks, axis=0)
            st_ref[n] = pick.T.astype(BF16)
            pick = pick.astype(BF16)
            for p in range(count):
                cols = columns(sc, p, quarter)
                values = jnp.concatenate(
                    [x_held[2 * n, :, cols], x_held[2 * n + 1, :, cols]], axis=0
                )
                got = dot_nn(pick, values).astype(BF16)
                grad = dot_nn(pick, g_held[n, :, cols])
                for e in range(local):
                    here = slice(e * CAP, (e + 1) * CAP)
                    d_ref[e, rows, p * quarter : (p + 1) * quarter] = got[here]
                    go_ref[e, rows, p * quarter : (p + 1) * quarter] = (
                        grad[here] * gate_ref[e, rows, 0:1]
                    ).astype(BF16)
        for copy in copies:
            copy.start()
        for copy in weight_copies:
            copy.wait()

        @pl.loop(0, local)
        def _(e):
            gate = up = act_grad = None
            for p in range(count):
                cols = slice(p * quarter, (p + 1) * quarter)
                rows = d_ref[e, :, cols]
                a = dot_nn(rows, weight(p, e, 0))
                b = dot_nn(rows, weight(p, e, 1))
                c = dot_nn(go_ref[e, :, cols], weight(p, e, 2))
                gate = a if gate is None else gate + a
                up = b if up is None else up + b
                act_grad = c if act_grad is None else act_grad + c
            sig = jax.nn.sigmoid(gate)
            silu = gate * sig
            act = (silu * up).astype(BF16)
            up_grad = (act_grad * silu).astype(BF16)
            gate_grad = (act_grad * up * sig * (1.0 + gate * (1.0 - sig))).astype(BF16)
            h_ref[e, :, :hidden] = act
            h_ref[e, :, hidden : 2 * hidden] = gate_grad
            h_ref[e, :, 2 * hidden :] = up_grad
            scale = gate_ref[e, :, 0:1]
            for p in range(count):
                cols = slice(p * quarter, (p + 1) * quarter)
                ns_ref[e, :, cols] = (
                    dot_nt(gate_grad, weight(p, e, 0)) + dot_nt(up_grad, weight(p, e, 1))
                ).astype(BF16)
                ys_ref[e, :, cols] = (dot_nt(act, weight(p, e, 2)) * scale).astype(BF16)

        hidden_copy.start()
        for at, source in ((0, ns_ref), (2, ys_ref)):
            for n, (side, g) in enumerate(blocks):
                rows = slice(n * CAP, (n + 1) * CAP)
                for p in range(count):
                    cols = slice(p * quarter, (p + 1) * quarter)
                    stacked = jnp.concatenate([source[e, rows, cols] for e in range(local)], axis=0)
                    sum_ref[at + side, g, :, columns(sc, p, quarter)] = dot_nn(
                        st_ref[n], stacked
                    ).astype(BF16)
                if g == k - 1:
                    sum_copies[at + side].start()
        for copy in (*copies, hidden_copy, *sum_copies):
            copy.wait()

    outside = pl.BlockSpec(memory_space=pltpu.HBM)
    sums = sds((k, tokens, model), BF16)
    rows = sds((local, rows_each, model), BF16)
    return pl.pallas_call(
        body,
        out_shape=[sums] * 4 + [sds((local, rows_each, 3 * hidden), BF16), rows, rows],
        grid_spec=pltpu.PrefetchScalarGridSpec(
            num_scalar_prefetch=1,
            grid=(1,),
            in_specs=[outside] * (4 * k + 2 + len(weights)),
            out_specs=[outside] * 7,
            scratch_shapes=[
                pltpu.VMEM((len(blocks), tokens, local * CAP), BF16),
                pltpu.VMEM((local, rows_each, LANES), F32),
                pltpu.VMEM((local, rows_each, model), BF16),
                pltpu.VMEM((local, rows_each, model), BF16),
                pltpu.VMEM((local, rows_each, 3 * hidden), BF16),
                pltpu.VMEM((local, rows_each, model), BF16),
                pltpu.VMEM((local, rows_each, model), BF16),
                pltpu.VMEM((len(blocks), tokens, model + LANES), BF16),
                pltpu.VMEM((len(weights), local, quarter, hidden), BF16),
                pltpu.VMEM((4 * k, half, model), BF16),
                pltpu.VMEM((4, k, tokens, model), BF16),
                pltpu.SemaphoreType.DMA((3 + len(blocks) + len(weights) + 4 * k + 4,)),
            ],
        ),
        compiler_params=params(58),
        cost_estimate=cost(
            2 * local * rows_each * model * (6 * hidden + 4 * tokens),
            2 * 3 * count * local * quarter * hidden + 24 * k * tokens * model,
            local * rows_each * hidden,
        ),
        name="experts",
    )(scalars, *rows_in, *grads_in, *weights)


def far_sets(local):
    mate = [(1, e) for e in range(local)]
    own = [(0, e) for e in range(local)]
    if local != 4:
        return [[v] for v in (*mate, *own)]
    return [mate[:1], mate[1:2], mate[2:] + own[:1], own[1:2], own[2:]]


def expert_weight_grads(row_sets, grad_sets, hidden_sets, quarter):
    groups = len(row_sets)
    local, _, model = row_sets[0].shape
    sets = far_sets(local)
    hidden = hidden_sets[0].shape[2] // 3
    count = model // quarter
    chunks, rows = [[]], 0
    for g in range(groups):
        if sum(row_sets[k].shape[1] for k in chunks[-1]) >= 8 * CAP:
            chunks.append([])
        chunks[-1].append(g)
        rows += row_sets[g].shape[1]

    def body(*refs):
        d_refs, go_refs, h_refs = refs[:groups], refs[groups : 2 * groups], refs[2 * groups : 3 * groups]
        keep_refs, far_refs = refs[3 * groups : 3 * groups + 2], refs[3 * groups + 2 :]
        expert = pl.program_id(0)
        far = []
        for p in range(count):
            cols = slice(p * quarter, (p + 1) * quarter)
            sums = [None, None, None]
            for chosen in chunks:
                left = jnp.concatenate([d_refs[g][0, :, cols] for g in chosen], axis=0)
                left_out = jnp.concatenate([go_refs[g][0, :, cols] for g in chosen], axis=0)
                right = jnp.concatenate([h_refs[g][0] for g in chosen], axis=0)
                parts = (
                    dot_tn(left, right[:, hidden : 2 * hidden]),
                    dot_tn(left, right[:, 2 * hidden :]),
                    dot_tn(left_out, right[:, :hidden]),
                )
                sums = [a if b is None else a + b for a, b in zip(parts, sums)]
            for k in range(3):
                if p < 2:
                    keep_refs[p][0, k] = sums[k].astype(BF16)
                else:
                    far.append(sums[k].astype(BF16))
        for ref, chosen in zip(far_refs, sets):
            for n, (which, e) in enumerate(chosen):

                @pl.when(expert == e)
                def _():
                    for k in range(3):
                        ref[3 * n + k] = far[3 * which + k]

    by_expert = lambda shape: pl.BlockSpec((1,) + shape, lambda e: (e,) + (0,) * len(shape))
    fars = [(3 * len(chosen), quarter, hidden) for chosen in sets]
    return pl.pallas_call(
        body,
        out_shape=[sds((local, 3, quarter, hidden), BF16)] * 2 + [sds(f, BF16) for f in fars],
        grid=(local,),
        in_specs=[by_expert(a.shape[1:]) for a in (*row_sets, *grad_sets, *hidden_sets)],
        out_specs=[by_expert((3, quarter, hidden))] * 2 + [whole(f) for f in fars],
        compiler_params=params(56),
        cost_estimate=cost(
            6 * local * rows * model * hidden,
            2 * local * rows * (2 * model + 3 * hidden) + 3 * local * 3 * model * hidden,
        ),
        name="expert_weight_grads",
    )(*row_sets, *grad_sets, *hidden_sets)


def middle_grad(scalars, parts, residual, grad_out, gains):
    tokens, model = grad_out.shape
    half = tokens // 2
    count = len(parts)

    def body(sc, *refs):
        part_refs = refs[:count]
        res_ref, go_ref, gain_ref, rg_ref, branch_ref, sum_ref = refs[count:]
        total = part_refs[0][...].astype(F32)
        for k in range(1, count):
            total = total + part_refs[k][...].astype(F32)
        residual = res_ref[...]
        start = pl.multiple_of(sc[2] * half, half)
        inverse = lax.rsqrt(jnp.mean(residual * residual, axis=-1, keepdims=True) + EPS)
        scaled = gain_ref[1:2, :] * total
        shift = jnp.mean(scaled * residual, axis=-1, keepdims=True)
        grad = (
            go_ref[pl.ds(start, half)].astype(F32)
            + inverse * scaled
            - residual * (inverse * inverse * inverse * shift)
        )
        rg_ref[...] = grad
        branch_ref[...] = grad.astype(BF16)
        sum_ref[...] = jnp.broadcast_to(
            jnp.sum(total * residual * inverse, axis=0, keepdims=True), (8, model)
        )

    return pl.pallas_call(
        body,
        out_shape=[sds((half, model), F32), sds((half, model), BF16), sds((8, model), F32)],
        grid_spec=pltpu.PrefetchScalarGridSpec(
            num_scalar_prefetch=1,
            grid=(1,),
            in_specs=[whole((half, model))] * (count + 1)
            + [whole((tokens, model)), whole((8, model))],
            out_specs=[whole((half, model)), whole((half, model)), whole((8, model))],
        ),
        compiler_params=params(12),
        cost_estimate=cost(20 * half * model, 24 * half * model),
        name="middle_grad",
    )(scalars, *parts, residual, grad_out, gains)


def attend_grad(scalars, branch, queries, kv_all, lse, out_pieces, cos_table, sin_table, piece_count):
    tokens, q_width = queries.shape
    length, kv2 = kv_all.shape
    kv_width = kv2 // 2
    kv_heads = kv_width // HEAD_DIM
    heads = q_width + kv2
    pair_blocks = kv_width // LANES
    count = len(out_pieces)
    quarter = out_pieces[0].shape[0]
    model = quarter * count
    half = tokens // 2

    def body(sc, b0_ref, b1_ref, q_ref, k_ref, v_ref, lse_ref, cos_ref, sin_ref, *rest):
        own = rows_at(sc[1], tokens)
        out_refs = rest[:count]
        dq_ref, dkv_ref, mg_ref, bias_ref = rest[count:]
        c = pl.program_id(0)

        @pl.when(c == 0)
        def _():
            cols = lax.broadcasted_iota(jnp.int32, (half, tokens), 0)
            rows = lax.broadcasted_iota(jnp.int32, (half, tokens), 1)
            query_pos = token_position(sc, rows, sc[1], tokens)
            for n in range(length // half):
                key_pos = cols + ((n // 2) * tokens + ((n % 2) ^ sc[2]) * half)
                bias_ref[n * half : (n + 1) * half] = seen_bias(
                    sc, query_pos, key_pos, piece_count
                )
            total = None
            for p in range(count):
                col = columns(sc, p, quarter)
                block = jnp.concatenate([b0_ref[:, col], b1_ref[:, col]], axis=0)
                part = dot_nn(block, out_refs[p][...])
                total = part if total is None else total + part
            mg_ref[...] = total.astype(BF16)

        low = lax.broadcasted_iota(jnp.int32, (1, LANES), 1) < HEAD_DIM
        mine = low == (c % 2 == 0)
        keys = k_ref[...].astype(F32)
        keys = jnp.where(mine, keys, pltpu.roll(keys, HEAD_DIM, 1)).astype(BF16)
        vals = v_ref[...].astype(F32)
        vals = jnp.where(mine, vals, pltpu.roll(vals, HEAD_DIM, 1)).astype(BF16)
        query = q_ref[...]
        grad = mg_ref[:, pl.ds(pl.multiple_of(c * LANES, LANES), LANES)]
        zero = jnp.zeros_like(query)
        lse_t = lse_ref[...].T
        dqs = []
        dk = dv = None
        for g in range(2):
            query_g = jnp.where(low, query, zero) if g == 0 else jnp.where(low, zero, query)
            grad_g = jnp.where(low, grad, zero) if g == 0 else jnp.where(low, zero, grad)
            scores = dot_nt(keys, query_g) + bias_ref[...]
            probs = jnp.exp(scores - lse_t[g * HEAD_DIM : g * HEAD_DIM + 1])
            prob_grad = dot_nt(vals, grad_g)
            delta = jnp.sum(probs * prob_grad, axis=0, keepdims=True)
            score_grad = (probs * (prob_grad - delta)).astype(BF16)
            dqs.append(dot_tn(score_grad, keys))
            dk_g = dot_nn(score_grad, query_g)
            dv_g = dot_nn(probs.astype(BF16), grad_g)
            dk = dk_g if dk is None else dk + dk_g
            dv = dv_g if dv is None else dv + dv_g
        dq = jnp.where(low, dqs[0], dqs[1]) * HEAD_DIM**-0.5
        dq_ref[...] = turn(dq, cos_ref[own], -sin_ref[own]).astype(BF16)
        dk = turn(dk, cos_ref[...], -sin_ref[...])
        for k, value in ((0, dk), (pair_blocks, dv)):
            value = (value + pltpu.roll(value, HEAD_DIM, 1)).astype(BF16)
            where = pl.ds(pl.multiple_of((k + c // 2) * LANES, LANES), LANES)
            dkv_ref[:, where] = jnp.where(mine, value, dkv_ref[:, where])

    return pl.pallas_call(
        body,
        out_shape=[sds((tokens, q_width), BF16), sds((length, kv2), BF16)],
        grid_spec=pltpu.PrefetchScalarGridSpec(
            num_scalar_prefetch=1,
            grid=(kv_heads,),
            in_specs=[
                whole((half, model)),
                whole((half, model)),
                pl.BlockSpec((tokens, LANES), lambda c, sc: (0, c)),
                pl.BlockSpec((length, LANES), lambda c, sc: (0, c // 2)),
                pl.BlockSpec((length, LANES), lambda c, sc: (0, pair_blocks + c // 2)),
                pl.BlockSpec((tokens, LANES), lambda c, sc: (0, c)),
                whole((length, LANES)),
                whole((length, LANES)),
            ]
            + [pl.BlockSpec((quarter, q_width), lambda c, sc: (0, heads // q_width))] * count,
            out_specs=[
                pl.BlockSpec((tokens, LANES), lambda c, sc: (0, c)),
                whole((length, kv2)),
            ],
            scratch_shapes=[
                pltpu.VMEM((tokens, q_width), BF16),
                pltpu.VMEM((length, tokens), F32),
            ],
        ),
        compiler_params=params(58),
        cost_estimate=cost(
            40 * tokens * length * LANES + 2 * tokens * q_width * model,
            6 * length * kv2 + 8 * tokens * model,
            2 * kv_heads * tokens * length,
        ),
        name="attend_grad",
    )(scalars, *branch, queries, kv_all, kv_all, lse, cos_table, sin_table, *out_pieces)


def weight_grads(scalars, normed, dq, dkv, branch, mixed, extra, quarter):
    length, model = normed.shape
    tokens, q_width = dq.shape
    kv2 = dkv.shape[1]
    width = q_width + kv2 + mixed.shape[1]
    count = model // quarter
    outs = [((quarter, width + LANES), BF16)] * 2 + [((2, quarter, width + LANES), BF16)]

    def body(sc, xn_ref, dq_ref, dkv_ref, b0_ref, b1_ref, mixed_ref, extra_ref, *out_refs):
        own = rows_at(sc[1], tokens)
        rows = lax.broadcasted_iota(jnp.int32, (quarter, quarter), 0)
        diagonal = rows == lax.broadcasted_iota(jnp.int32, (quarter, quarter), 1)
        for p in range(count):
            cols = columns(sc, p, quarter)
            ref = (out_refs[0], None, out_refs[1], None)[p]
            block = jnp.concatenate([b0_ref[:, cols], b1_ref[:, cols]], axis=0)
            column = jnp.sum(jnp.where(diagonal, extra_ref[0:1, cols], 0.0), axis=1, keepdims=True)
            at = 0
            for value in (
                dot_tn(xn_ref[own, cols], dq_ref[...]),
                dot_tn(xn_ref[:, cols], dkv_ref[...]),
                dot_tn(block, mixed_ref[...]),
                jnp.broadcast_to(column, (quarter, LANES)),
            ):
                here = slice(at, at + value.shape[1])
                at += value.shape[1]
                if ref is not None:
                    ref[:, here] = value.astype(BF16)
                else:
                    out_refs[2][p // 2, :, here] = value.astype(BF16)

    arrays = (normed, dq, dkv, *branch, mixed, extra)
    return pl.pallas_call(
        body,
        out_shape=[sds(*o) for o in outs],
        grid_spec=pltpu.PrefetchScalarGridSpec(
            num_scalar_prefetch=1,
            grid=(1,),
            in_specs=[whole(a.shape) for a in arrays],
            out_specs=[whole(o[0]) for o in outs],
        ),
        compiler_params=params(58),
        cost_estimate=cost(
            2 * model * (tokens * (q_width + mixed.shape[1]) + length * kv2),
            2 * length * (model + kv2) + 3 * model * width,
        ),
        name="weight_grads",
    )(scalars, *arrays)


def gather_expert_grads(scalars, keep, far, mates, sent):
    local, _, quarter, hidden = keep.shape
    sets = far_sets(local)
    chosen = range(len(sets) - len(far), len(sets)) if sent is not None else range(len(far))
    places = [
        (i, 3 * k, v[1])
        for i, n in enumerate(chosen)
        for k, v in enumerate(sets[n])
        if v[0] == 0
    ]
    used = sorted({i for i, _, _ in places})
    experts_here = [e for _, _, e in places]
    lowest = min(experts_here) if experts_here else 0
    count = len(experts_here)
    held = [] if sent is None else [sent]
    mates_here = [] if mates is None else [mates]
    steps = count + (local if mates_here else 0)

    def place(step, sc):
        core = sc[0] % 2
        mine = core * local + lowest + step
        return jnp.where(step < count, mine, (1 - core) * local + step - count)

    def body(sc, keep_ref, *rest):
        far_refs, out_ref = dict(zip(used, rest)), rest[-1]
        step = pl.program_id(0)
        for i, start, expert in places:

            @pl.when(step == expert - lowest)
            def _():
                out_ref[0] = keep_ref[0].astype(F32) + far_refs[i][start : start + 3].astype(F32)

        if mates_here:

            @pl.when(step >= count)
            def _():
                out_ref[0] = rest[len(used)][0].astype(F32)

    block = (1, 3, quarter, hidden)
    own = lambda step, sc: (lowest + jnp.minimum(step, max(count - 1, 0)), 0, 0, 0)
    other = lambda step, sc: (jnp.maximum(step - count, 0), 0, 0, 0)
    arrays = [keep, *[far[i] for i in used], *mates_here, *held]
    return pl.pallas_call(
        body,
        out_shape=sds((2 * local, 3, quarter, hidden), F32),
        grid_spec=pltpu.PrefetchScalarGridSpec(
            num_scalar_prefetch=1,
            grid=(steps,),
            in_specs=[pl.BlockSpec(block, own)]
            + [whole(far[i].shape) for i in used]
            + [pl.BlockSpec(block, other)] * len(mates_here)
            + [pl.BlockSpec(memory_space=pl.ANY)] * len(held),
            out_specs=pl.BlockSpec(block, lambda step, sc: (place(step, sc), 0, 0, 0)),
        ),
        input_output_aliases={len(arrays): 0} if held else {},
        compiler_params=params(24),
        cost_estimate=cost(3 * steps * quarter * hidden, 3 * 10 * steps * quarter * hidden),
        name="gather_expert_grads",
    )(scalars, *arrays)


def back(scalars, dq, dkv, pieces):
    tokens, q_width = dq.shape
    groups, _, kv2 = dkv.shape
    heads = q_width + kv2
    count = len(pieces)
    quarter = pieces[0].shape[0]
    model = count * quarter
    half = tokens // 2

    def body(sc, dq_ref, dkv_ref, *rest):
        piece_refs = rest[:count]
        own_ref, send_ref = rest[count:]
        total = dkv_ref[0].astype(F32)
        for g in range(1, groups):
            total = total + dkv_ref[g].astype(F32)
        dl_kv = total.astype(BF16)
        dl_q = dq_ref[...]
        for p in range(count):
            cols = columns(sc, p, quarter)
            part = dot_nt(dl_q, piece_refs[p][:, :q_width]) + dot_nt(
                dl_kv, piece_refs[p][:, q_width:heads]
            )
            own_ref[:, cols] = part[:half]
            send_ref[:, cols] = part[half:].astype(BF16)

    arrays = (dq, dkv, *pieces)
    return pl.pallas_call(
        body,
        out_shape=[sds((half, model), F32), sds((half, model), BF16)],
        grid_spec=pltpu.PrefetchScalarGridSpec(
            num_scalar_prefetch=1,
            grid=(1,),
            in_specs=[whole(dq.shape), whole(dkv.shape)] + [whole((quarter, heads))] * count,
            out_specs=[whole((half, model))] * 2,
        ),
        compiler_params=params(58),
        cost_estimate=cost(2 * tokens * model * heads, 2 * model * (heads + 2 * tokens)),
        name="back",
    )(scalars, *arrays)


def last_grad(scalars, layer_input, own, received, residual_grad, gains):
    tokens, model = layer_input.shape
    half = tokens // 2

    def body(sc, x_ref, own_ref, rec_ref, rg_ref, gain_ref, out_ref):
        start = pl.multiple_of(sc[2] * half, half)
        values = x_ref[pl.ds(start, half)].astype(F32)
        inverse = lax.rsqrt(jnp.mean(values * values, axis=-1, keepdims=True) + EPS)
        scaled = gain_ref[0:1, :] * (own_ref[...] + rec_ref[...].astype(F32))
        shift = jnp.mean(scaled * values, axis=-1, keepdims=True)
        out_ref[...] = (
            rg_ref[...] + inverse * scaled - values * (inverse * inverse * inverse * shift)
        ).astype(BF16)

    return pl.pallas_call(
        body,
        out_shape=sds((half, model), BF16),
        grid_spec=pltpu.PrefetchScalarGridSpec(
            num_scalar_prefetch=1,
            grid=(1,),
            in_specs=[
                whole((tokens, model)),
                whole((half, model)),
                whole((half, model)),
                whole((half, model)),
                whole((8, model)),
            ],
            out_specs=whole((half, model)),
        ),
        compiler_params=params(8),
        cost_estimate=cost(12 * half * model, 14 * half * model),
        name="last_grad",
    )(scalars, layer_input, own, received, residual_grad, gains)


def local(
    layer_input,
    attn_norm,
    w_query,
    w_key,
    w_value,
    w_out,
    moe_norm,
    expert_weights,
    expert_ids,
    slot_ids,
    gate_values,
    piece_starts,
    grad_out,
):
    _, tokens, model = layer_input.shape
    half = tokens // 2
    groups = lax.axis_size("ctx")
    shard = lax.axis_index("shard")
    group = lax.axis_index("ctx")
    side = lax.axis_index("tp")
    piece_count = piece_starts.shape[1]
    scalars = jnp.concatenate(
        [jnp.stack([shard, group, side]).astype(jnp.int32), piece_starts[0]]
    )
    flat_input = layer_input[0]
    flat_grad = grad_out[0]
    q_width, kv_width = w_query.shape[1], w_key.shape[1]
    rows_here = w_query.shape[0]
    quarter = rows_here * groups

    own_input = jnp.where(side == 0, flat_input[:half], flat_input[half:])
    local_experts = expert_weights.shape[0] // 2
    core = shard % 2


    def experts_of(which, m):
        start = (which * local_experts, m, 0, 0)
        size = (local_experts, 1) + expert_weights.shape[2:]
        return lax.dynamic_slice(expert_weights, start, size)[:, 0]

    mine = [experts_of(core, m) for m in range(3)]
    given = [experts_of(1 - core, m) for m in range(3)]
    weight_block = jnp.concatenate(
        [
            w_query,
            w_key,
            w_value,
            w_out.T,
            attn_norm[:, None],
            moe_norm[:, None],
            jnp.zeros((rows_here, LANES - 2), BF16),
        ],
        axis=1,
    )

    index = jnp.arange(groups * tokens, dtype=jnp.int32)
    positions = (index ^ (side * half).astype(jnp.int32)).astype(F32)
    lane = jnp.arange(LANES, dtype=jnp.int32)
    step = (lane % (HEAD_DIM // 2)).astype(F32)
    angles = positions[:, None] * (1.0 / 10000.0 ** (step * 2.0 / HEAD_DIM))[None, :]
    cos_table = jnp.cos(angles)
    sin_table = jnp.sin(angles) * jnp.where(lane % HEAD_DIM < HEAD_DIM // 2, -1.0, 1.0)[None, :]

    gate_high = gate_values[0].astype(BF16)
    gate_low = (gate_values[0] - gate_high.astype(F32)).astype(BF16)
    routing = jnp.concatenate(
        [
            expert_ids[0].astype(BF16),
            slot_ids[0].astype(BF16),
            gate_high,
            gate_low,
            jnp.zeros((tokens, LANES - 4 * TOPK), BF16),
        ],
        axis=1,
    )
    grad_block = spread_grads(scalars, flat_grad, routing, groups)

    near = [1, 3] if groups == 4 else [1]
    rest = [b for b in range(1, groups) if b not in near]
    block_0, own_input, cos_table, sin_table, grad_block, far_0, far_1, *kept = fence(
        spread(weight_block, "ctx").reshape(quarter, -1),
        own_input,
        cos_table,
        sin_table,
        grad_block,
        swap(mine[0], "shard", 2),
        swap(mine[1], "shard", 2),
        *mine,
        *given,
        *[swap(own_input, "ctx", b) for b in near],
    )
    mine, given = kept[:3], kept[3:6]
    input_at = dict(zip(near, kept[6:]))
    halves = [swap(input_at[b], "tp", 1) for b in near]
    block_0, block_2, *kept = fence(
        block_0,
        swap(block_0, "shard", 2),
        *halves,
        *[swap(own_input, "ctx", b) for b in rest],
    )
    crossed = dict(zip(near, kept[: len(near)]))
    input_at.update(dict(zip(rest, kept[len(near) :])))
    grads_own = lax.all_to_all(after(grad_block, block_2), "ctx", 0, 0, tiled=True)
    block_0, block_1, block_2, block_3, taken_0, *kept = fence(
        block_0,
        swap(block_0, "shard", 1),
        block_2,
        swap(block_2, "shard", 1),
        swap(after(given[0], block_2), "shard", 1),
        *[swap(input_at[b], "tp", 1) for b in rest],
    )
    crossed.update(dict(zip(rest, kept)))
    pieces = [block_0, block_1, block_2, block_3]
    others = [v for b in range(1, groups) for v in (input_at[b], crossed[b])]

    normed_all, queries, kv_all, gains = front(
        scalars, flat_input, others, pieces, cos_table, sin_table, (q_width, kv_width)
    )
    mixed, lse, attention_own, attention_send = attend(
        scalars, queries, kv_all, pieces, piece_count
    )
    attention_send, far_2, far_3, taken_2, taken_1 = fence(
        attention_send,
        swap(after(mine[2], block_1), "shard", 2),
        swap(after(taken_0, block_1), "shard", 2),
        swap(after(given[2], block_1), "shard", 1),
        swap(after(given[1], block_1), "shard", 1),
    )
    attention_got, far_4 = fence(
        swap(attention_send, "tp", 1), swap(after(taken_1, attention_send), "shard", 2)
    )
    residual, normed_two = second_norm(
        scalars, flat_input, attention_own, attention_got, gains
    )

    calls = [[0], *[[b, b + 1] for b in range(1, groups - 1, 2)], [groups - 1]]
    far_5 = swap(after(taken_2, far_4), "shard", 2)
    grads_own = after(grads_own, residual)
    normed_two, crossed, grads_own, grads_mate, far_5, *arrived = fence(
        normed_two,
        swap(normed_two, "tp", 1),
        grads_own,
        swap(grads_own, "shard", 1),
        far_5,
        *[swap(normed_two, "ctx", b) for b in calls[1]],
    )
    tokens_at = {0: normed_two, **dict(zip(calls[1], arrived))}
    grads_in = [grads_own, grads_mate]
    taken = [taken_0, taken_1, taken_2]
    expert_pieces = [*mine, *taken, far_0, far_1, far_2, far_3, far_4, far_5]
    rows_in = [normed_two, crossed, swap(normed_two, "shard", 1), swap(crossed, "shard", 1)]

    def summed(own, got, part):
        return own[:, part].astype(F32) + got[:, part].astype(F32)

    low, high = slice(0, half), slice(half, tokens)
    row_sets, grad_sets, hidden_sets = [], [], []
    norm_parts, out_parts, out_sets = {}, {}, []
    waiting = None
    order = scalars
    for n, call in enumerate(calls):
        own, mate, out_own, out_mate, hiddens, rows, grads = experts(
            order, call, rows_in, grads_in, expert_pieces
        )
        row_sets.append(rows)
        grad_sets.append(grads)
        hidden_sets.append(hiddens)
        out_sets.append((call, out_own, out_mate))
        later = calls[n + 1] if n + 1 < len(calls) else []
        latest = calls[n + 2] if n + 2 < len(calls) else []
        own, mate, *arrived = fence(
            own,
            mate,
            *[swap(tokens_at[b], "tp", 1) for b in later],
            *[swap(tokens_at[b], "shard", 1) for b in later],
            *[swap(normed_two, "ctx", b) for b in latest],
            *([waiting[3]] if waiting is not None else []),
        )
        crossed, arrived = arrived[: len(later)], arrived[len(later) :]
        mates, arrived = arrived[: len(later)], arrived[len(later) :]
        tokens_at.update(dict(zip(latest, arrived)))
        if later:
            here = [v for b, c in zip(later, crossed) for v in (tokens_at[b], c)]
            there = [v for m, c in zip(mates, crossed) for v in (m, swap(c, "shard", 1))]
            rows_in = [*here, *there]
        got = swap(mate, "shard", 1)
        sent = summed(own, got, high).astype(BF16)
        if waiting is not None:
            old_call, kept_own, old_got, _ = waiting
            kept = summed(kept_own, old_got, low) + arrived[-1].astype(F32)
            for i, b in enumerate(old_call):
                norm_parts[b] = kept[i] if b == 0 else swap(kept[i].astype(BF16), "ctx", b)
        waiting = (call, own, got, swap(sent, "tp", 1))
        order = after(scalars, sent)

    hidden_sets[-1] = after(hidden_sets[-1], sent)
    call, own, got, crossed = waiting
    early = [b for b in norm_parts if b > 0]
    mates = [swap(after(s[2], sent), "shard", 1) for s in out_sets[:-1]]
    keep_0, keep_1, *arrived = fence(
        *expert_weight_grads(row_sets, grad_sets, hidden_sets, quarter),
        crossed,
        *[norm_parts[b] for b in early],
        *mates,
    )
    fars = len(arrived) - 1 - len(early) - len(mates)
    far_sent, crossed, arrived = arrived[:fars], arrived[fars], arrived[fars + 1 :]
    far_got = []

    def send_far(count, *ready):
        start = len(far_got)
        got = [swap(after(v, *ready), "shard", 2) for v in far_sent[start : start + count]]
        far_got.extend(got)
        return got

    def keep_far(got):
        if got:
            far_got[len(far_got) - len(got) :] = got

    norm_parts.update(dict(zip(early, arrived)))
    mates = arrived[len(early) :]
    kept = summed(own, got, low) + crossed.astype(F32)
    for i, b in enumerate(call):
        norm_parts[b] = swap(kept[i].astype(BF16), "ctx", b)

    outs = [(s[0], after(s[1], kept), m) for s, m in zip(out_sets, mates)]
    middle, edges = outs[1:], outs[:1]
    out_crossed = [swap(summed(own, got, high).astype(BF16), "tp", 1) for _, own, got in middle]
    out_last = swap(after(out_sets[-1][2], kept), "shard", 1)
    sending = send_far(1, crossed)
    residual, out_last, *arrived = fence(
        residual, out_last, *[norm_parts[b] for b in range(groups)], *sending, *out_crossed
    )
    keep_far(arrived[groups : groups + len(sending)])
    out_crossed = arrived[groups + len(sending) :]
    arrived = arrived[:groups]
    residual_grad, branch_own, gain_row = middle_grad(
        scalars, arrived, residual, flat_grad, gains
    )
    sending = send_far(1, out_last)
    branch_own, branch_crossed, *sending = fence(branch_own, swap(branch_own, "tp", 1), *sending)
    keep_far(sending)
    branch = [branch_own, branch_crossed]
    for (call, own, got), crossed in zip(middle, out_crossed):
        kept = summed(after(own, branch_own), got, low) + crossed.astype(F32)
        for i, b in enumerate(call):
            out_parts[b] = swap(fence(kept[i].astype(BF16))[0], "ctx", b)
    moved = list(out_parts)
    edges.append((*out_sets[-1][:2], out_last))
    edges = [(call, after(own, branch_own), got) for call, own, got in edges]
    out_crossed = [swap(summed(own, got, high).astype(BF16), "tp", 1) for _, own, got in edges]

    dq, dkv_parts = attend_grad(
        scalars, branch, queries, kv_all, lse, pieces, cos_table, sin_table, piece_count
    )
    sending = send_far(1, branch_crossed)
    dq, dkv_parts, out_first, out_last, *arrived = fence(
        dq, dkv_parts, *out_crossed, *[out_parts[b] for b in moved], *sending
    )
    out_crossed = [out_first, out_last]
    out_parts.update(dict(zip(moved, arrived)))
    keep_far(arrived[len(moved) :])

    for (call, own, got), crossed in zip(edges, out_crossed):
        kept = summed(after(own, dq), got, low) + crossed.astype(F32)
        for i, b in enumerate(call):
            out_parts[b] = kept[i] if b == 0 else swap(fence(kept[i].astype(BF16))[0], "ctx", b)
    sending = send_far(1, dq)
    own_grads, far_grads, sent_grads, dkv_parts, *arrived = fence(
        *weight_grads(scalars, normed_all, dq, dkv_parts, branch, mixed, gain_row, quarter),
        dkv_parts,
        *[out_parts[b] for b in calls[-1]],
        *sending,
    )
    out_parts.update(dict(zip(calls[-1], arrived)))
    keep_far(arrived[len(calls[-1]) :])

    got_grads = fence(swap(sent_grads, "shard", 1))[0]
    passed = (far_grads.astype(F32) + got_grads[1].astype(F32)).astype(BF16)
    places = {
        v[1]: (n, 3 * k)
        for n, chosen in enumerate(far_sets(local_experts))
        for k, v in enumerate(chosen)
        if v[0] == 1
    }
    mates = jnp.stack(
        [
            (keep_1[e].astype(F32) + far_got[n][start : start + 3].astype(F32)).astype(BF16)
            for e, (n, start) in sorted(places.items())
        ]
    )
    kept_grads = (after(own_grads, mates).astype(F32) + got_grads[0].astype(F32)).astype(BF16)
    def natural(own, other):
        return jnp.where(
            side == 0,
            jnp.concatenate([own, other], axis=0),
            jnp.concatenate([other, own], axis=0),
        )[None]

    out_sum = after(residual, kept_grads)
    for b in range(groups):
        out_sum = out_sum + out_parts[b].astype(F32)
    out_half = out_sum.astype(BF16)
    output = natural(out_half, swap(out_half, "tp", 1))
    dkv, passed, kept_grads, output, mates = fence(
        lax.all_to_all(
            dkv_parts.reshape(groups, tokens, 2 * kv_width), "ctx", 0, 0, tiled=True
        ),
        swap(passed, "shard", 2),
        kept_grads,
        output,
        swap(mates, "shard", 1),
    )

    total = fence((kept_grads.astype(F32) + passed.astype(F32)).astype(BF16))[0]
    normed_own, normed_send = back(scalars, dq, dkv, pieces)
    input_half = last_grad(
        scalars, flat_input, normed_own, swap(normed_send, "tp", 1), residual_grad, gains
    )
    early = list(far_got)
    sending = send_far(len(far_sent), dkv)
    expert_grad = gather_expert_grads(scalars, keep_0, early, mates, None)
    total, input_half, input_other, expert_grad, *sending = fence(
        lax.all_to_all(
            total.reshape(groups, rows_here, total.shape[1]), "ctx", 0, 0, tiled=True
        ),
        input_half,
        swap(input_half, "tp", 1),
        expert_grad,
        *sending,
    )
    keep_far(sending)
    input_grad = natural(input_half, input_other)
    if sending:
        expert_grad = gather_expert_grads(scalars, keep_0, sending, None, expert_grad)
    total = jnp.sum(total.astype(F32), axis=0)
    query_grad = total[:, :q_width]
    key_grad = total[:, q_width : q_width + kv_width]
    value_grad = total[:, q_width + kv_width : q_width + 2 * kv_width]
    heads = q_width + 2 * kv_width
    out_grad = total[:, heads : heads + q_width].T
    moe_sum = total[:, heads + q_width]
    attn_sum = (
        jnp.sum(w_query.astype(F32) * query_grad, axis=1)
        + jnp.sum(w_key.astype(F32) * key_grad, axis=1)
        + jnp.sum(w_value.astype(F32) * value_grad, axis=1)
    )
    sums = jnp.stack([attn_sum, moe_sum])
    attn_sum, moe_norm_grad = sums + swap(sums, "tp", 1)
    attn_norm_grad = attn_sum / attn_norm.astype(F32)
    return (
        output,
        input_grad,
        attn_norm_grad,
        query_grad,
        key_grad,
        value_grad,
        out_grad,
        moe_norm_grad,
        expert_grad,
    )


def solution(mesh):
    in_specs = (
        P("shard", "ctx", None),
        P(("shard", "ctx")),
        P(("shard", "ctx"), "tp"),
        P(("shard", "ctx"), "tp"),
        P(("shard", "ctx"), "tp"),
        P("tp", ("shard", "ctx")),
        P(("shard", "ctx")),
        P("ctx", None, "shard", "tp"),
        P("shard", "ctx", None),
        P("shard", "ctx", None),
        P("shard", "ctx", None),
        P("shard", None),
        P("shard", "ctx", None),
    )
    out_specs = (
        P("shard", "ctx", None),
        P("shard", "ctx", None),
        P(("shard", "ctx")),
        P(("shard", "ctx"), "tp"),
        P(("shard", "ctx"), "tp"),
        P(("shard", "ctx"), "tp"),
        P("tp", ("shard", "ctx")),
        P(("shard", "ctx")),
        P("ctx", None, "shard", "tp"),
    )
    return jax.shard_map(local, mesh=mesh, in_specs=in_specs, out_specs=out_specs, check_vma=False)
```

```python
import functools

import jax
import jax.numpy as jnp
from jax import lax
from jax.experimental import pallas as pl
from jax.experimental.pallas import tpu as pltpu
from jax.sharding import PartitionSpec as P

HEAD_DIM = 64
EXPERTS = 32
TOPK = 8
PIECE = 256
CAP = 96
EPS = 1e-06
MASKED = -1e30
LANES = 128
F32 = jnp.float32
BF16 = jnp.bfloat16


def swap(value, axis, distance):
    size = lax.axis_size(axis)
    return lax.ppermute(value, axis, [(i, i ^ distance) for i in range(size)])


def spread(value, axis):
    size = lax.axis_size(axis)
    copies = jnp.broadcast_to(value[None], (size,) + value.shape)
    return lax.all_to_all(copies, axis, 0, 0, tiled=True)


def after(value, *others):
    return lax.optimization_barrier((value,) + others)[0]


def fence(*values):
    return lax.optimization_barrier(values)


def dot_nn(a, b):
    return lax.dot_general(a, b, (((1,), (0,)), ((), ())), preferred_element_type=F32)


def dot_nt(a, b):
    return lax.dot_general(a, b, (((1,), (1,)), ((), ())), preferred_element_type=F32)


def dot_tn(a, b):
    return lax.dot_general(a, b, (((0,), (0,)), ((), ())), preferred_element_type=F32)


def cost(flops, moved, special=0):
    return pl.CostEstimate(flops=int(flops), bytes_accessed=int(moved), transcendentals=int(special))


def params(megabytes, length=0):
    megabytes = 58 if length > 1024 else megabytes
    return pltpu.CompilerParams(vmem_limit_bytes=megabytes * 1024 * 1024)


def sds(shape, dtype):
    return jax.ShapeDtypeStruct(shape, dtype)


def whole(shape):
    return pl.BlockSpec(shape, lambda *_: (0,) * len(shape))


def turn(value, cosine, sine):
    lane = lax.broadcasted_iota(jnp.int32, (value.shape[0], LANES), 1) % HEAD_DIM
    first = lane < HEAD_DIM // 2
    parts = []
    for j in range(value.shape[1] // LANES):
        chunk = value[:, j * LANES : (j + 1) * LANES]
        partner = jnp.where(
            first,
            pltpu.roll(chunk, LANES - HEAD_DIM // 2, 1),
            pltpu.roll(chunk, HEAD_DIM // 2, 1),
        )
        parts.append(chunk * cosine + partner * sine)
    return parts[0] if len(parts) == 1 else jnp.concatenate(parts, axis=1)


def rows_at(index, size):
    return pl.ds(pl.multiple_of(index * size, size), size)


def columns(scalars, p, width):
    return pl.ds(pl.multiple_of((scalars[0] ^ p) * width, width), width)


def spread_grads(scalars, grads, routing, groups):
    tokens, model = grads.shape
    half = tokens // 2
    out = (groups, tokens, model + LANES)

    def body(sc, grads_ref, routing_ref, out_ref):
        for h in range(2):
            here = rows_at(sc[2] ^ h, half)
            out_ref[0, h * half : (h + 1) * half, :model] = grads_ref[here]
            out_ref[0, h * half : (h + 1) * half, model:] = routing_ref[here]

    return pl.pallas_call(
        body,
        out_shape=sds(out, BF16),
        grid_spec=pltpu.PrefetchScalarGridSpec(
            num_scalar_prefetch=1,
            grid=(groups,),
            in_specs=[whole(grads.shape), whole(routing.shape)],
            out_specs=pl.BlockSpec((1,) + out[1:], lambda g, sc: (g, 0, 0)),
        ),
        compiler_params=params(12),
        cost_estimate=cost(0, 2 * (groups + 1) * tokens * (model + LANES)),
        name="spread_grads",
    )(scalars, grads, routing)


def front(scalars, layer_input, others, pieces, cos_table, sin_table, widths):
    tokens, model = layer_input.shape
    quarter = pieces[0].shape[0]
    q_width, kv_width = widths
    heads = q_width + 2 * kv_width
    gain_column = pieces[0].shape[1] - LANES
    half = tokens // 2
    count = len(pieces)
    groups = 1 + len(others) // 2
    length = groups * tokens

    def body(sc, x_ref, *rest):
        other_refs, rest = rest[: len(others)], rest[len(others) :]
        piece_refs = rest[:count]
        cos_ref, sin_ref, xn_ref, q_ref, kv_ref, gain_ref = rest[count:]
        rows = lax.broadcasted_iota(jnp.int32, (quarter, quarter), 0)
        diagonal = rows == lax.broadcasted_iota(jnp.int32, (quarter, quarter), 1)
        for p in range(count):
            gains = piece_refs[p][:, gain_column : gain_column + LANES].astype(F32)
            for k in range(2):
                row = jnp.sum(jnp.where(diagonal, gains[:, k : k + 1], 0.0), axis=0, keepdims=True)
                gain_ref[k : k + 1, columns(sc, p, quarter)] = row
        gain = gain_ref[0:1, :]
        for b in range(groups):
            for h in range(2):
                if b == 0:
                    values = x_ref[rows_at(sc[2] ^ h, half)].astype(F32)
                else:
                    values = other_refs[2 * (b - 1) + h][...].astype(F32)
                inverse = lax.rsqrt(jnp.mean(values * values, axis=-1, keepdims=True) + EPS)
                xn_ref[rows_at(2 * (sc[1] ^ b) + h, half)] = (values * inverse * gain).astype(BF16)

        own = rows_at(sc[1], tokens)
        total = None
        for p in range(count):
            part = dot_nn(xn_ref[own, columns(sc, p, quarter)], piece_refs[p][:, :q_width])
            total = part if total is None else total + part
        total = turn(total, cos_ref[own], sin_ref[own]).astype(BF16)
        q_ref[...] = (total * HEAD_DIM**-0.5).astype(BF16)

        @pl.loop(0, groups)
        def _(g):
            here = rows_at(g, tokens)
            total = None
            for p in range(count):
                part = dot_nn(xn_ref[here, columns(sc, p, quarter)], piece_refs[p][:, q_width:heads])
                total = part if total is None else total + part
            kv_ref[here, :kv_width] = turn(total[:, :kv_width], cos_ref[here], sin_ref[here]).astype(
                BF16
            )
            kv_ref[here, kv_width:] = total[:, kv_width:].astype(BF16)

    outs = [
        ((length, model), BF16),
        ((tokens, q_width), BF16),
        ((length, 2 * kv_width), BF16),
        ((8, model), F32),
    ]
    arrays = (layer_input, *others, *pieces, cos_table, sin_table)
    return pl.pallas_call(
        body,
        out_shape=[sds(*o) for o in outs],
        grid_spec=pltpu.PrefetchScalarGridSpec(
            num_scalar_prefetch=1,
            grid=(1,),
            in_specs=[whole(a.shape) for a in arrays],
            out_specs=[whole(o[0]) for o in outs],
        ),
        compiler_params=params(58),
        cost_estimate=cost(
            2 * model * (tokens * q_width + length * 2 * kv_width),
            2 * model * (2 * length + heads) + 2 * length * (kv_width + 2 * LANES),
        ),
        name="front",
    )(scalars, *arrays)


def inside_piece(position, start):
    return (position >= start) & (position < start + PIECE)


def seen_bias(sc, query_pos, key_pos, piece_count):
    seen = key_pos <= query_pos
    for k in range(piece_count):
        start = sc[3 + k]
        seen = seen | (inside_piece(query_pos, start) & inside_piece(key_pos, start))
    return jnp.where(seen, 0.0, MASKED)


def token_position(sc, index, group, tokens):
    return group * tokens + (index ^ (sc[2] * (tokens // 2)))


def attend(scalars, queries, kv_all, out_pieces, piece_count):
    tokens, q_width = queries.shape
    length, kv2 = kv_all.shape
    kv_width = kv2 // 2
    kv_heads = kv_width // HEAD_DIM
    heads = q_width + kv2
    pair_blocks = kv_width // LANES
    count = len(out_pieces)
    quarter = out_pieces[0].shape[0]
    model = quarter * count
    half = tokens // 2

    def body(sc, q_ref, k_ref, v_ref, *rest):
        out_refs = rest[:count]
        mixed_ref, lse_ref, own_ref, send_ref, bias_ref = rest[count:]
        c = pl.program_id(0)

        @pl.when(c == 0)
        def _():
            rows = lax.broadcasted_iota(jnp.int32, (tokens, half), 0)
            cols = lax.broadcasted_iota(jnp.int32, (tokens, half), 1)
            query_pos = token_position(sc, rows, sc[1], tokens)
            for n in range(length // half):
                key_pos = cols + ((n // 2) * tokens + ((n % 2) ^ sc[2]) * half)
                bias_ref[:, n * half : (n + 1) * half] = seen_bias(
                    sc, query_pos, key_pos, piece_count
                )

        low = lax.broadcasted_iota(jnp.int32, (1, LANES), 1) < HEAD_DIM
        mine = low == (c % 2 == 0)
        keys = k_ref[...].astype(F32)
        keys = jnp.where(mine, keys, pltpu.roll(keys, HEAD_DIM, 1)).astype(BF16)
        vals = v_ref[...].astype(F32)
        vals = jnp.where(mine, vals, pltpu.roll(vals, HEAD_DIM, 1)).astype(BF16)
        query = q_ref[...]
        zero = jnp.zeros_like(query)
        outs, lses = [], []
        for part in (jnp.where(low, query, zero), jnp.where(low, zero, query)):
            scores = dot_nt(part, keys) + bias_ref[...]
            top = jnp.max(scores, axis=-1, keepdims=True)
            expo = jnp.exp(scores - top)
            total = jnp.sum(expo, axis=-1, keepdims=True)
            probs = expo * (1.0 / total)
            outs.append(dot_nn(probs.astype(BF16), vals))
            lses.append(top + jnp.log(total))
        mixed_ref[:, pl.ds(pl.multiple_of(c * LANES, LANES), LANES)] = jnp.where(
            low, outs[0], outs[1]
        ).astype(BF16)
        lse_ref[...] = jnp.where(low, lses[0], lses[1])

        @pl.when(c == kv_heads - 1)
        def _():
            mixed = mixed_ref[...]
            for p in range(count):
                part = dot_nt(mixed, out_refs[p][...])
                own_ref[:, columns(sc, p, quarter)] = part[:half]
                send_ref[:, columns(sc, p, quarter)] = part[half:].astype(BF16)

    return pl.pallas_call(
        body,
        out_shape=[
            sds((tokens, q_width), BF16),
            sds((tokens, kv_heads * LANES), F32),
            sds((half, model), F32),
            sds((half, model), BF16),
        ],
        grid_spec=pltpu.PrefetchScalarGridSpec(
            num_scalar_prefetch=1,
            grid=(kv_heads,),
            in_specs=[
                pl.BlockSpec((tokens, LANES), lambda c, sc: (0, c)),
                pl.BlockSpec((length, LANES), lambda c, sc: (0, c // 2)),
                pl.BlockSpec((length, LANES), lambda c, sc: (0, pair_blocks + c // 2)),
            ]
            + [pl.BlockSpec((quarter, q_width), lambda c, sc: (0, heads // q_width))] * count,
            out_specs=[
                whole((tokens, q_width)),
                pl.BlockSpec((tokens, LANES), lambda c, sc: (0, c)),
                whole((half, model)),
                whole((half, model)),
            ],
            scratch_shapes=[pltpu.VMEM((tokens, length), F32)],
        ),
        compiler_params=params(58),
        cost_estimate=cost(
            16 * tokens * length * LANES + 2 * tokens * q_width * model,
            4 * length * kv2 + 8 * tokens * model,
            2 * kv_heads * tokens * length,
        ),
        name="attend",
    )(scalars, queries, kv_all, kv_all, *out_pieces)


def second_norm(scalars, layer_input, own, received, gains):
    tokens, model = layer_input.shape
    half = tokens // 2

    def body(sc, x_ref, own_ref, rec_ref, gain_ref, res_ref, norm_ref):
        start = pl.multiple_of(sc[2] * half, half)
        residual = (
            x_ref[pl.ds(start, half)].astype(F32) + own_ref[...] + rec_ref[...].astype(F32)
        )
        inverse = lax.rsqrt(jnp.mean(residual * residual, axis=-1, keepdims=True) + EPS)
        res_ref[...] = residual
        norm_ref[...] = (residual * inverse * gain_ref[1:2, :]).astype(BF16)

    return pl.pallas_call(
        body,
        out_shape=[sds((half, model), F32), sds((half, model), BF16)],
        grid_spec=pltpu.PrefetchScalarGridSpec(
            num_scalar_prefetch=1,
            grid=(1,),
            in_specs=[
                whole((tokens, model)),
                whole((half, model)),
                whole((half, model)),
                whole((8, model)),
            ],
            out_specs=[whole((half, model)), whole((half, model))],
        ),
        compiler_params=params(8),
        cost_estimate=cost(10 * half * model, 16 * half * model),
        name="second_norm",
    )(scalars, layer_input, own, received, gains)


def experts(scalars, fars, rows_in, grads_in, weights):
    k = len(fars)
    half, model = rows_in[0].shape
    tokens = 2 * half
    local, quarter, hidden = weights[0].shape
    count = model // quarter
    per_group = 2 * local
    blocks = [(side, g) for side in range(2) for g in range(k)]
    rows_each = len(blocks) * CAP

    def body(sc, *refs):
        x_ins, refs = refs[: 4 * k], refs[4 * k :]
        g_refs, refs = refs[:2], refs[2:]
        w_refs, refs = refs[: len(weights)], refs[len(weights) :]
        na_out, nb_out, ya_out, yb_out, h_out, d_out, go_out = refs[:7]
        st_ref, gate_ref, ns_ref, ys_ref, h_ref, d_ref, go_ref, g_held, w_held, x_held, sum_ref, sems = refs[7:]

        def weight(p, e, m):
            return w_held[3 * p + m, e]

        copies = (
            pltpu.make_async_copy(d_ref, d_out, sems.at[0]),
            pltpu.make_async_copy(go_ref, go_out, sems.at[1]),
        )
        hidden_copy = pltpu.make_async_copy(h_ref, h_out, sems.at[2])
        grad_copies = [
            pltpu.make_async_copy(g_refs[side].at[sc[1] ^ fars[g]], g_held.at[n], sems.at[3 + n])
            for n, (side, g) in enumerate(blocks)
        ]
        first_sem = 3 + len(blocks) + len(weights)
        row_copies = [
            pltpu.make_async_copy(x_ins[n], x_held.at[n], sems.at[first_sem + n])
            for n in range(4 * k)
        ]
        sum_copies = [
            pltpu.make_async_copy(sum_ref.at[n], out, sems.at[first_sem + 4 * k + n])
            for n, out in enumerate((na_out, nb_out, ya_out, yb_out))
        ]
        weight_copies = [
            pltpu.make_async_copy(w_refs[n], w_held.at[n], sems.at[3 + len(blocks) + n])
            for n in range(len(weights))
        ]
        for n in range(len(blocks)):
            for copy in (grad_copies[n], row_copies[2 * n], row_copies[2 * n + 1]):
                copy.start()
        for copy in weight_copies:
            copy.start()
        base = sc[1] * per_group + (sc[0] % 2) * local
        slot_row = lax.broadcasted_iota(jnp.int32, (CAP, tokens), 0).astype(F32)
        for n, (side, g) in enumerate(blocks):
            rows = slice(n * CAP, (n + 1) * CAP)
            grad_copies[n].wait()
            table = g_held[n, :, model : model + LANES].astype(F32).T
            ids, slots = table[:TOPK], table[TOPK : 2 * TOPK] - CAP
            gates = table[2 * TOPK : 3 * TOPK] + table[3 * TOPK : 4 * TOPK]
            picks = []
            for e in range(local):
                hit = ids == (base + e).astype(F32)
                slot = jnp.sum(jnp.where(hit, slots, 0.0), axis=0, keepdims=True) + CAP
                gate = jnp.sum(jnp.where(hit, gates, 0.0), axis=0, keepdims=True)
                pick = slot_row == slot
                value = jnp.sum(jnp.where(pick, gate, 0.0), axis=1, keepdims=True)
                gate_ref[e, rows, :] = jnp.broadcast_to(value, (CAP, LANES))
                picks.append(jnp.where(pick, 1.0, 0.0))
            row_copies[2 * n].wait()
            row_copies[2 * n + 1].wait()
            pick = jnp.concatenate(picks, axis=0)
            st_ref[n] = pick.T.astype(BF16)
            pick = pick.astype(BF16)
            for p in range(count):
                cols = columns(sc, p, quarter)
                values = jnp.concatenate(
                    [x_held[2 * n, :, cols], x_held[2 * n + 1, :, cols]], axis=0
                )
                got = dot_nn(pick, values).astype(BF16)
                grad = dot_nn(pick, g_held[n, :, cols])
                for e in range(local):
                    here = slice(e * CAP, (e + 1) * CAP)
                    d_ref[e, rows, p * quarter : (p + 1) * quarter] = got[here]
                    go_ref[e, rows, p * quarter : (p + 1) * quarter] = (
                        grad[here] * gate_ref[e, rows, 0:1]
                    ).astype(BF16)
        for copy in copies:
            copy.start()
        for copy in weight_copies:
            copy.wait()

        @pl.loop(0, local)
        def _(e):
            gate = up = act_grad = None
            for p in range(count):
                cols = slice(p * quarter, (p + 1) * quarter)
                rows = d_ref[e, :, cols]
                a = dot_nn(rows, weight(p, e, 0))
                b = dot_nn(rows, weight(p, e, 1))
                c = dot_nn(go_ref[e, :, cols], weight(p, e, 2))
                gate = a if gate is None else gate + a
                up = b if up is None else up + b
                act_grad = c if act_grad is None else act_grad + c
            sig = jax.nn.sigmoid(gate)
            silu = gate * sig
            act = (silu * up).astype(BF16)
            up_grad = (act_grad * silu).astype(BF16)
            gate_grad = (act_grad * up * sig * (1.0 + gate * (1.0 - sig))).astype(BF16)
            h_ref[e, :, :hidden] = act
            h_ref[e, :, hidden : 2 * hidden] = gate_grad
            h_ref[e, :, 2 * hidden :] = up_grad
            scale = gate_ref[e, :, 0:1]
            for p in range(count):
                cols = slice(p * quarter, (p + 1) * quarter)
                ns_ref[e, :, cols] = (
                    dot_nt(gate_grad, weight(p, e, 0)) + dot_nt(up_grad, weight(p, e, 1))
                ).astype(BF16)
                ys_ref[e, :, cols] = (dot_nt(act, weight(p, e, 2)) * scale).astype(BF16)

        hidden_copy.start()
        for at, source in ((0, ns_ref), (2, ys_ref)):
            for n, (side, g) in enumerate(blocks):
                rows = slice(n * CAP, (n + 1) * CAP)
                for p in range(count):
                    cols = slice(p * quarter, (p + 1) * quarter)
                    stacked = jnp.concatenate([source[e, rows, cols] for e in range(local)], axis=0)
                    sum_ref[at + side, g, :, columns(sc, p, quarter)] = dot_nn(
                        st_ref[n], stacked
                    ).astype(BF16)
                if g == k - 1:
                    sum_copies[at + side].start()
        for copy in (*copies, hidden_copy, *sum_copies):
            copy.wait()

    outside = pl.BlockSpec(memory_space=pltpu.HBM)
    sums = sds((k, tokens, model), BF16)
    rows = sds((local, rows_each, model), BF16)
    return pl.pallas_call(
        body,
        out_shape=[sums] * 4 + [sds((local, rows_each, 3 * hidden), BF16), rows, rows],
        grid_spec=pltpu.PrefetchScalarGridSpec(
            num_scalar_prefetch=1,
            grid=(1,),
            in_specs=[outside] * (4 * k + 2 + len(weights)),
            out_specs=[outside] * 7,
            scratch_shapes=[
                pltpu.VMEM((len(blocks), tokens, local * CAP), BF16),
                pltpu.VMEM((local, rows_each, LANES), F32),
                pltpu.VMEM((local, rows_each, model), BF16),
                pltpu.VMEM((local, rows_each, model), BF16),
                pltpu.VMEM((local, rows_each, 3 * hidden), BF16),
                pltpu.VMEM((local, rows_each, model), BF16),
                pltpu.VMEM((local, rows_each, model), BF16),
                pltpu.VMEM((len(blocks), tokens, model + LANES), BF16),
                pltpu.VMEM((len(weights), local, quarter, hidden), BF16),
                pltpu.VMEM((4 * k, half, model), BF16),
                pltpu.VMEM((4, k, tokens, model), BF16),
                pltpu.SemaphoreType.DMA((3 + len(blocks) + len(weights) + 4 * k + 4,)),
            ],
        ),
        compiler_params=params(58),
        cost_estimate=cost(
            2 * local * rows_each * model * (6 * hidden + 4 * tokens),
            2 * 3 * count * local * quarter * hidden + 24 * k * tokens * model,
            local * rows_each * hidden,
        ),
        name="experts",
    )(scalars, *rows_in, *grads_in, *weights)


def far_sets(local):
    mate = [(1, e) for e in range(local)]
    own = [(0, e) for e in range(local)]
    if local != 4:
        return [[v] for v in (*mate, *own)]
    return [mate[:1], mate[1:2], mate[2:] + own[:1], own[1:2], own[2:]]


def expert_weight_grads(row_sets, grad_sets, hidden_sets, quarter):
    groups = len(row_sets)
    local, _, model = row_sets[0].shape
    sets = far_sets(local)
    hidden = hidden_sets[0].shape[2] // 3
    count = model // quarter
    chunks, rows = [[]], 0
    for g in range(groups):
        if sum(row_sets[k].shape[1] for k in chunks[-1]) >= 8 * CAP:
            chunks.append([])
        chunks[-1].append(g)
        rows += row_sets[g].shape[1]

    def body(*refs):
        d_refs, go_refs, h_refs = refs[:groups], refs[groups : 2 * groups], refs[2 * groups : 3 * groups]
        keep_refs, far_refs = refs[3 * groups : 3 * groups + 2], refs[3 * groups + 2 :]
        expert = pl.program_id(0)
        far = []
        for p in range(count):
            cols = slice(p * quarter, (p + 1) * quarter)
            sums = [None, None, None]
            for chosen in chunks:
                left = jnp.concatenate([d_refs[g][0, :, cols] for g in chosen], axis=0)
                left_out = jnp.concatenate([go_refs[g][0, :, cols] for g in chosen], axis=0)
                right = jnp.concatenate([h_refs[g][0] for g in chosen], axis=0)
                parts = (
                    dot_tn(left, right[:, hidden : 2 * hidden]),
                    dot_tn(left, right[:, 2 * hidden :]),
                    dot_tn(left_out, right[:, :hidden]),
                )
                sums = [a if b is None else a + b for a, b in zip(parts, sums)]
            for k in range(3):
                if p < 2:
                    keep_refs[p][0, k] = sums[k].astype(BF16)
                else:
                    far.append(sums[k].astype(BF16))
        for ref, chosen in zip(far_refs, sets):
            for n, (which, e) in enumerate(chosen):

                @pl.when(expert == e)
                def _():
                    for k in range(3):
                        ref[3 * n + k] = far[3 * which + k]

    by_expert = lambda shape: pl.BlockSpec((1,) + shape, lambda e: (e,) + (0,) * len(shape))
    fars = [(3 * len(chosen), quarter, hidden) for chosen in sets]
    return pl.pallas_call(
        body,
        out_shape=[sds((local, 3, quarter, hidden), BF16)] * 2 + [sds(f, BF16) for f in fars],
        grid=(local,),
        in_specs=[by_expert(a.shape[1:]) for a in (*row_sets, *grad_sets, *hidden_sets)],
        out_specs=[by_expert((3, quarter, hidden))] * 2 + [whole(f) for f in fars],
        compiler_params=params(56),
        cost_estimate=cost(
            6 * local * rows * model * hidden,
            2 * local * rows * (2 * model + 3 * hidden) + 3 * local * 3 * model * hidden,
        ),
        name="expert_weight_grads",
    )(*row_sets, *grad_sets, *hidden_sets)


def middle_grad(scalars, parts, residual, grad_out, gains):
    tokens, model = grad_out.shape
    half = tokens // 2
    count = len(parts)

    def body(sc, *refs):
        part_refs = refs[:count]
        res_ref, go_ref, gain_ref, rg_ref, branch_ref, sum_ref = refs[count:]
        total = part_refs[0][...].astype(F32)
        for k in range(1, count):
            total = total + part_refs[k][...].astype(F32)
        residual = res_ref[...]
        start = pl.multiple_of(sc[2] * half, half)
        inverse = lax.rsqrt(jnp.mean(residual * residual, axis=-1, keepdims=True) + EPS)
        scaled = gain_ref[1:2, :] * total
        shift = jnp.mean(scaled * residual, axis=-1, keepdims=True)
        grad = (
            go_ref[pl.ds(start, half)].astype(F32)
            + inverse * scaled
            - residual * (inverse * inverse * inverse * shift)
        )
        rg_ref[...] = grad
        branch_ref[...] = grad.astype(BF16)
        sum_ref[...] = jnp.broadcast_to(
            jnp.sum(total * residual * inverse, axis=0, keepdims=True), (8, model)
        )

    return pl.pallas_call(
        body,
        out_shape=[sds((half, model), F32), sds((half, model), BF16), sds((8, model), F32)],
        grid_spec=pltpu.PrefetchScalarGridSpec(
            num_scalar_prefetch=1,
            grid=(1,),
            in_specs=[whole((half, model))] * (count + 1)
            + [whole((tokens, model)), whole((8, model))],
            out_specs=[whole((half, model)), whole((half, model)), whole((8, model))],
        ),
        compiler_params=params(12),
        cost_estimate=cost(20 * half * model, 24 * half * model),
        name="middle_grad",
    )(scalars, *parts, residual, grad_out, gains)


def attend_grad(scalars, branch, queries, kv_all, lse, out_pieces, cos_table, sin_table, piece_count):
    tokens, q_width = queries.shape
    length, kv2 = kv_all.shape
    kv_width = kv2 // 2
    kv_heads = kv_width // HEAD_DIM
    heads = q_width + kv2
    pair_blocks = kv_width // LANES
    count = len(out_pieces)
    quarter = out_pieces[0].shape[0]
    model = quarter * count
    half = tokens // 2

    def body(sc, b0_ref, b1_ref, q_ref, k_ref, v_ref, lse_ref, cos_ref, sin_ref, *rest):
        own = rows_at(sc[1], tokens)
        out_refs = rest[:count]
        dq_ref, dkv_ref, mg_ref, bias_ref = rest[count:]
        c = pl.program_id(0)

        @pl.when(c == 0)
        def _():
            cols = lax.broadcasted_iota(jnp.int32, (half, tokens), 0)
            rows = lax.broadcasted_iota(jnp.int32, (half, tokens), 1)
            query_pos = token_position(sc, rows, sc[1], tokens)
            for n in range(length // half):
                key_pos = cols + ((n // 2) * tokens + ((n % 2) ^ sc[2]) * half)
                bias_ref[n * half : (n + 1) * half] = seen_bias(
                    sc, query_pos, key_pos, piece_count
                )
            total = None
            for p in range(count):
                col = columns(sc, p, quarter)
                block = jnp.concatenate([b0_ref[:, col], b1_ref[:, col]], axis=0)
                part = dot_nn(block, out_refs[p][...])
                total = part if total is None else total + part
            mg_ref[...] = total.astype(BF16)

        low = lax.broadcasted_iota(jnp.int32, (1, LANES), 1) < HEAD_DIM
        mine = low == (c % 2 == 0)
        keys = k_ref[...].astype(F32)
        keys = jnp.where(mine, keys, pltpu.roll(keys, HEAD_DIM, 1)).astype(BF16)
        vals = v_ref[...].astype(F32)
        vals = jnp.where(mine, vals, pltpu.roll(vals, HEAD_DIM, 1)).astype(BF16)
        query = q_ref[...]
        grad = mg_ref[:, pl.ds(pl.multiple_of(c * LANES, LANES), LANES)]
        zero = jnp.zeros_like(query)
        lse_t = lse_ref[...].T
        dqs = []
        dk = dv = None
        for g in range(2):
            query_g = jnp.where(low, query, zero) if g == 0 else jnp.where(low, zero, query)
            grad_g = jnp.where(low, grad, zero) if g == 0 else jnp.where(low, zero, grad)
            scores = dot_nt(keys, query_g) + bias_ref[...]
            probs = jnp.exp(scores - lse_t[g * HEAD_DIM : g * HEAD_DIM + 1])
            prob_grad = dot_nt(vals, grad_g)
            delta = jnp.sum(probs * prob_grad, axis=0, keepdims=True)
            score_grad = (probs * (prob_grad - delta)).astype(BF16)
            dqs.append(dot_tn(score_grad, keys))
            dk_g = dot_nn(score_grad, query_g)
            dv_g = dot_nn(probs.astype(BF16), grad_g)
            dk = dk_g if dk is None else dk + dk_g
            dv = dv_g if dv is None else dv + dv_g
        dq = jnp.where(low, dqs[0], dqs[1]) * HEAD_DIM**-0.5
        dq_ref[...] = turn(dq, cos_ref[own], -sin_ref[own]).astype(BF16)
        dk = turn(dk, cos_ref[...], -sin_ref[...])
        for k, value in ((0, dk), (pair_blocks, dv)):
            value = (value + pltpu.roll(value, HEAD_DIM, 1)).astype(BF16)
            where = pl.ds(pl.multiple_of((k + c // 2) * LANES, LANES), LANES)
            dkv_ref[:, where] = jnp.where(mine, value, dkv_ref[:, where])

    return pl.pallas_call(
        body,
        out_shape=[sds((tokens, q_width), BF16), sds((length, kv2), BF16)],
        grid_spec=pltpu.PrefetchScalarGridSpec(
            num_scalar_prefetch=1,
            grid=(kv_heads,),
            in_specs=[
                whole((half, model)),
                whole((half, model)),
                pl.BlockSpec((tokens, LANES), lambda c, sc: (0, c)),
                pl.BlockSpec((length, LANES), lambda c, sc: (0, c // 2)),
                pl.BlockSpec((length, LANES), lambda c, sc: (0, pair_blocks + c // 2)),
                pl.BlockSpec((tokens, LANES), lambda c, sc: (0, c)),
                whole((length, LANES)),
                whole((length, LANES)),
            ]
            + [pl.BlockSpec((quarter, q_width), lambda c, sc: (0, heads // q_width))] * count,
            out_specs=[
                pl.BlockSpec((tokens, LANES), lambda c, sc: (0, c)),
                whole((length, kv2)),
            ],
            scratch_shapes=[
                pltpu.VMEM((tokens, q_width), BF16),
                pltpu.VMEM((length, tokens), F32),
            ],
        ),
        compiler_params=params(58),
        cost_estimate=cost(
            40 * tokens * length * LANES + 2 * tokens * q_width * model,
            6 * length * kv2 + 8 * tokens * model,
            2 * kv_heads * tokens * length,
        ),
        name="attend_grad",
    )(scalars, *branch, queries, kv_all, kv_all, lse, cos_table, sin_table, *out_pieces)


def weight_grads(scalars, normed, dq, dkv, branch, mixed, extra, quarter):
    length, model = normed.shape
    tokens, q_width = dq.shape
    kv2 = dkv.shape[1]
    width = q_width + kv2 + mixed.shape[1]
    count = model // quarter
    outs = [((quarter, width + LANES), BF16)] * 2 + [((2, quarter, width + LANES), BF16)]

    def body(sc, xn_ref, dq_ref, dkv_ref, b0_ref, b1_ref, mixed_ref, extra_ref, *out_refs):
        own = rows_at(sc[1], tokens)
        rows = lax.broadcasted_iota(jnp.int32, (quarter, quarter), 0)
        diagonal = rows == lax.broadcasted_iota(jnp.int32, (quarter, quarter), 1)
        for p in range(count):
            cols = columns(sc, p, quarter)
            ref = (out_refs[0], None, out_refs[1], None)[p]
            block = jnp.concatenate([b0_ref[:, cols], b1_ref[:, cols]], axis=0)
            column = jnp.sum(jnp.where(diagonal, extra_ref[0:1, cols], 0.0), axis=1, keepdims=True)
            at = 0
            for value in (
                dot_tn(xn_ref[own, cols], dq_ref[...]),
                dot_tn(xn_ref[:, cols], dkv_ref[...]),
                dot_tn(block, mixed_ref[...]),
                jnp.broadcast_to(column, (quarter, LANES)),
            ):
                here = slice(at, at + value.shape[1])
                at += value.shape[1]
                if ref is not None:
                    ref[:, here] = value.astype(BF16)
                else:
                    out_refs[2][p // 2, :, here] = value.astype(BF16)

    arrays = (normed, dq, dkv, *branch, mixed, extra)
    return pl.pallas_call(
        body,
        out_shape=[sds(*o) for o in outs],
        grid_spec=pltpu.PrefetchScalarGridSpec(
            num_scalar_prefetch=1,
            grid=(1,),
            in_specs=[whole(a.shape) for a in arrays],
            out_specs=[whole(o[0]) for o in outs],
        ),
        compiler_params=params(58),
        cost_estimate=cost(
            2 * model * (tokens * (q_width + mixed.shape[1]) + length * kv2),
            2 * length * (model + kv2) + 3 * model * width,
        ),
        name="weight_grads",
    )(scalars, *arrays)


def gather_expert_grads(scalars, keep, far, mates, sent):
    local, _, quarter, hidden = keep.shape
    sets = far_sets(local)
    chosen = range(len(sets) - len(far), len(sets)) if sent is not None else range(len(far))
    places = [
        (i, 3 * k, v[1])
        for i, n in enumerate(chosen)
        for k, v in enumerate(sets[n])
        if v[0] == 0
    ]
    used = sorted({i for i, _, _ in places})
    experts_here = [e for _, _, e in places]
    lowest = min(experts_here) if experts_here else 0
    count = len(experts_here)
    held = [] if sent is None else [sent]
    mates_here = [] if mates is None else [mates]
    steps = count + (local if mates_here else 0)

    def place(step, sc):
        core = sc[0] % 2
        mine = core * local + lowest + step
        return jnp.where(step < count, mine, (1 - core) * local + step - count)

    def body(sc, keep_ref, *rest):
        far_refs, out_ref = dict(zip(used, rest)), rest[-1]
        step = pl.program_id(0)
        for i, start, expert in places:

            @pl.when(step == expert - lowest)
            def _():
                out_ref[0] = keep_ref[0].astype(F32) + far_refs[i][start : start + 3].astype(F32)

        if mates_here:

            @pl.when(step >= count)
            def _():
                out_ref[0] = rest[len(used)][0].astype(F32)

    block = (1, 3, quarter, hidden)
    own = lambda step, sc: (lowest + jnp.minimum(step, max(count - 1, 0)), 0, 0, 0)
    other = lambda step, sc: (jnp.maximum(step - count, 0), 0, 0, 0)
    arrays = [keep, *[far[i] for i in used], *mates_here, *held]
    return pl.pallas_call(
        body,
        out_shape=sds((2 * local, 3, quarter, hidden), F32),
        grid_spec=pltpu.PrefetchScalarGridSpec(
            num_scalar_prefetch=1,
            grid=(steps,),
            in_specs=[pl.BlockSpec(block, own)]
            + [whole(far[i].shape) for i in used]
            + [pl.BlockSpec(block, other)] * len(mates_here)
            + [pl.BlockSpec(memory_space=pl.ANY)] * len(held),
            out_specs=pl.BlockSpec(block, lambda step, sc: (place(step, sc), 0, 0, 0)),
        ),
        input_output_aliases={len(arrays): 0} if held else {},
        compiler_params=params(24),
        cost_estimate=cost(3 * steps * quarter * hidden, 3 * 10 * steps * quarter * hidden),
        name="gather_expert_grads",
    )(scalars, *arrays)


def back(scalars, dq, dkv, pieces):
    tokens, q_width = dq.shape
    groups, _, kv2 = dkv.shape
    heads = q_width + kv2
    count = len(pieces)
    quarter = pieces[0].shape[0]
    model = count * quarter
    half = tokens // 2

    def body(sc, dq_ref, dkv_ref, *rest):
        piece_refs = rest[:count]
        own_ref, send_ref = rest[count:]
        total = dkv_ref[0].astype(F32)
        for g in range(1, groups):
            total = total + dkv_ref[g].astype(F32)
        dl_kv = total.astype(BF16)
        dl_q = dq_ref[...]
        for p in range(count):
            cols = columns(sc, p, quarter)
            part = dot_nt(dl_q, piece_refs[p][:, :q_width]) + dot_nt(
                dl_kv, piece_refs[p][:, q_width:heads]
            )
            own_ref[:, cols] = part[:half]
            send_ref[:, cols] = part[half:].astype(BF16)

    arrays = (dq, dkv, *pieces)
    return pl.pallas_call(
        body,
        out_shape=[sds((half, model), F32), sds((half, model), BF16)],
        grid_spec=pltpu.PrefetchScalarGridSpec(
            num_scalar_prefetch=1,
            grid=(1,),
            in_specs=[whole(dq.shape), whole(dkv.shape)] + [whole((quarter, heads))] * count,
            out_specs=[whole((half, model))] * 2,
        ),
        compiler_params=params(58),
        cost_estimate=cost(2 * tokens * model * heads, 2 * model * (heads + 2 * tokens)),
        name="back",
    )(scalars, *arrays)


def last_grad(scalars, layer_input, own, received, residual_grad, gains):
    tokens, model = layer_input.shape
    half = tokens // 2

    def body(sc, x_ref, own_ref, rec_ref, rg_ref, gain_ref, out_ref):
        start = pl.multiple_of(sc[2] * half, half)
        values = x_ref[pl.ds(start, half)].astype(F32)
        inverse = lax.rsqrt(jnp.mean(values * values, axis=-1, keepdims=True) + EPS)
        scaled = gain_ref[0:1, :] * (own_ref[...] + rec_ref[...].astype(F32))
        shift = jnp.mean(scaled * values, axis=-1, keepdims=True)
        out_ref[...] = (
            rg_ref[...] + inverse * scaled - values * (inverse * inverse * inverse * shift)
        ).astype(BF16)

    return pl.pallas_call(
        body,
        out_shape=sds((half, model), BF16),
        grid_spec=pltpu.PrefetchScalarGridSpec(
            num_scalar_prefetch=1,
            grid=(1,),
            in_specs=[
                whole((tokens, model)),
                whole((half, model)),
                whole((half, model)),
                whole((half, model)),
                whole((8, model)),
            ],
            out_specs=whole((half, model)),
        ),
        compiler_params=params(8),
        cost_estimate=cost(12 * half * model, 14 * half * model),
        name="last_grad",
    )(scalars, layer_input, own, received, residual_grad, gains)


def local(
    layer_input,
    attn_norm,
    w_query,
    w_key,
    w_value,
    w_out,
    moe_norm,
    expert_weights,
    expert_ids,
    slot_ids,
    gate_values,
    piece_starts,
    grad_out,
):
    _, tokens, model = layer_input.shape
    half = tokens // 2
    groups = lax.axis_size("ctx")
    shard = lax.axis_index("shard")
    group = lax.axis_index("ctx")
    side = lax.axis_index("tp")
    piece_count = piece_starts.shape[1]
    scalars = jnp.concatenate(
        [jnp.stack([shard, group, side]).astype(jnp.int32), piece_starts[0]]
    )
    flat_input = layer_input[0]
    flat_grad = grad_out[0]
    q_width, kv_width = w_query.shape[1], w_key.shape[1]
    rows_here = w_query.shape[0]
    quarter = rows_here * groups

    own_input = jnp.where(side == 0, flat_input[:half], flat_input[half:])
    local_experts = expert_weights.shape[0] // 2
    core = shard % 2


    def experts_of(which, m):
        start = (which * local_experts, m, 0, 0)
        size = (local_experts, 1) + expert_weights.shape[2:]
        return lax.dynamic_slice(expert_weights, start, size)[:, 0]

    mine = [experts_of(core, m) for m in range(3)]
    given = [experts_of(1 - core, m) for m in range(3)]
    weight_block = jnp.concatenate(
        [
            w_query,
            w_key,
            w_value,
            w_out.T,
            attn_norm[:, None],
            moe_norm[:, None],
            jnp.zeros((rows_here, LANES - 2), BF16),
        ],
        axis=1,
    )

    index = jnp.arange(groups * tokens, dtype=jnp.int32)
    positions = (index ^ (side * half).astype(jnp.int32)).astype(F32)
    lane = jnp.arange(LANES, dtype=jnp.int32)
    step = (lane % (HEAD_DIM // 2)).astype(F32)
    angles = positions[:, None] * (1.0 / 10000.0 ** (step * 2.0 / HEAD_DIM))[None, :]
    cos_table = jnp.cos(angles)
    sin_table = jnp.sin(angles) * jnp.where(lane % HEAD_DIM < HEAD_DIM // 2, -1.0, 1.0)[None, :]

    gate_high = gate_values[0].astype(BF16)
    gate_low = (gate_values[0] - gate_high.astype(F32)).astype(BF16)
    routing = jnp.concatenate(
        [
            expert_ids[0].astype(BF16),
            slot_ids[0].astype(BF16),
            gate_high,
            gate_low,
            jnp.zeros((tokens, LANES - 4 * TOPK), BF16),
        ],
        axis=1,
    )
    grad_block = spread_grads(scalars, flat_grad, routing, groups)

    near = [1, 3] if groups == 4 else [1]
    rest = [b for b in range(1, groups) if b not in near]
    block_0, own_input, cos_table, sin_table, grad_block, far_0, far_1, *kept = fence(
        spread(weight_block, "ctx").reshape(quarter, -1),
        own_input,
        cos_table,
        sin_table,
        grad_block,
        swap(mine[0], "shard", 2),
        swap(mine[1], "shard", 2),
        *mine,
        *given,
        *[swap(own_input, "ctx", b) for b in near],
    )
    mine, given = kept[:3], kept[3:6]
    input_at = dict(zip(near, kept[6:]))
    halves = [swap(input_at[b], "tp", 1) for b in near]
    block_0, block_2, *kept = fence(
        block_0,
        swap(block_0, "shard", 2),
        *halves,
        *[swap(own_input, "ctx", b) for b in rest],
    )
    crossed = dict(zip(near, kept[: len(near)]))
    input_at.update(dict(zip(rest, kept[len(near) :])))
    grads_own = lax.all_to_all(after(grad_block, block_2), "ctx", 0, 0, tiled=True)
    block_0, block_1, block_2, block_3, taken_0, *kept = fence(
        block_0,
        swap(block_0, "shard", 1),
        block_2,
        swap(block_2, "shard", 1),
        swap(after(given[0], block_2), "shard", 1),
        *[swap(input_at[b], "tp", 1) for b in rest],
    )
    crossed.update(dict(zip(rest, kept)))
    pieces = [block_0, block_1, block_2, block_3]
    others = [v for b in range(1, groups) for v in (input_at[b], crossed[b])]

    normed_all, queries, kv_all, gains = front(
        scalars, flat_input, others, pieces, cos_table, sin_table, (q_width, kv_width)
    )
    mixed, lse, attention_own, attention_send = attend(
        scalars, queries, kv_all, pieces, piece_count
    )
    attention_send, far_2, far_3, taken_2, taken_1 = fence(
        attention_send,
        swap(after(mine[2], block_1), "shard", 2),
        swap(after(taken_0, block_1), "shard", 2),
        swap(after(given[2], block_1), "shard", 1),
        swap(after(given[1], block_1), "shard", 1),
    )
    attention_got, far_4 = fence(
        swap(attention_send, "tp", 1), swap(after(taken_1, attention_send), "shard", 2)
    )
    residual, normed_two = second_norm(
        scalars, flat_input, attention_own, attention_got, gains
    )

    calls = [[0], *[[b, b + 1] for b in range(1, groups - 1, 2)], [groups - 1]]
    far_5 = swap(after(taken_2, far_4), "shard", 2)
    grads_own = after(grads_own, residual)
    normed_two, crossed, grads_own, grads_mate, far_5, *arrived = fence(
        normed_two,
        swap(normed_two, "tp", 1),
        grads_own,
        swap(grads_own, "shard", 1),
        far_5,
        *[swap(normed_two, "ctx", b) for b in calls[1]],
    )
    tokens_at = {0: normed_two, **dict(zip(calls[1], arrived))}
    grads_in = [grads_own, grads_mate]
    taken = [taken_0, taken_1, taken_2]
    expert_pieces = [*mine, *taken, far_0, far_1, far_2, far_3, far_4, far_5]
    rows_in = [normed_two, crossed, swap(normed_two, "shard", 1), swap(crossed, "shard", 1)]

    def summed(own, got, part):
        return own[:, part].astype(F32) + got[:, part].astype(F32)

    low, high = slice(0, half), slice(half, tokens)
    row_sets, grad_sets, hidden_sets = [], [], []
    norm_parts, out_parts, out_sets = {}, {}, []
    waiting = None
    order = scalars
    for n, call in enumerate(calls):
        own, mate, out_own, out_mate, hiddens, rows, grads = experts(
            order, call, rows_in, grads_in, expert_pieces
        )
        row_sets.append(rows)
        grad_sets.append(grads)
        hidden_sets.append(hiddens)
        out_sets.append((call, out_own, out_mate))
        later = calls[n + 1] if n + 1 < len(calls) else []
        latest = calls[n + 2] if n + 2 < len(calls) else []
        own, mate, *arrived = fence(
            own,
            mate,
            *[swap(tokens_at[b], "tp", 1) for b in later],
            *[swap(tokens_at[b], "shard", 1) for b in later],
            *[swap(normed_two, "ctx", b) for b in latest],
            *([waiting[3]] if waiting is not None else []),
        )
        crossed, arrived = arrived[: len(later)], arrived[len(later) :]
        mates, arrived = arrived[: len(later)], arrived[len(later) :]
        tokens_at.update(dict(zip(latest, arrived)))
        if later:
            here = [v for b, c in zip(later, crossed) for v in (tokens_at[b], c)]
            there = [v for m, c in zip(mates, crossed) for v in (m, swap(c, "shard", 1))]
            rows_in = [*here, *there]
        got = swap(mate, "shard", 1)
        sent = summed(own, got, high).astype(BF16)
        if waiting is not None:
            old_call, kept_own, old_got, _ = waiting
            kept = summed(kept_own, old_got, low) + arrived[-1].astype(F32)
            for i, b in enumerate(old_call):
                norm_parts[b] = kept[i] if b == 0 else swap(kept[i].astype(BF16), "ctx", b)
        waiting = (call, own, got, swap(sent, "tp", 1))
        order = after(scalars, sent)

    hidden_sets[-1] = after(hidden_sets[-1], sent)
    call, own, got, crossed = waiting
    early = [b for b in norm_parts if b > 0]
    mates = [swap(after(s[2], sent), "shard", 1) for s in out_sets[:-1]]
    keep_0, keep_1, *arrived = fence(
        *expert_weight_grads(row_sets, grad_sets, hidden_sets, quarter),
        crossed,
        *[norm_parts[b] for b in early],
        *mates,
    )
    fars = len(arrived) - 1 - len(early) - len(mates)
    far_sent, crossed, arrived = arrived[:fars], arrived[fars], arrived[fars + 1 :]
    far_got = []

    def send_far(count, *ready):
        start = len(far_got)
        got = [swap(after(v, *ready), "shard", 2) for v in far_sent[start : start + count]]
        far_got.extend(got)
        return got

    def keep_far(got):
        if got:
            far_got[len(far_got) - len(got) :] = got

    norm_parts.update(dict(zip(early, arrived)))
    mates = arrived[len(early) :]
    kept = summed(own, got, low) + crossed.astype(F32)
    for i, b in enumerate(call):
        norm_parts[b] = swap(kept[i].astype(BF16), "ctx", b)

    outs = [(s[0], s[1], m) for s, m in zip(out_sets, mates)]
    middle, edges = outs[1:], outs[:1]
    out_crossed = [swap(summed(own, got, high).astype(BF16), "tp", 1) for _, own, got in middle]
    out_last = swap(after(out_sets[-1][2], kept), "shard", 1)
    sending = send_far(1, crossed)
    residual, out_last, *arrived = fence(
        residual, out_last, *[norm_parts[b] for b in range(groups)], *sending, *out_crossed
    )
    keep_far(arrived[groups : groups + len(sending)])
    out_crossed = arrived[groups + len(sending) :]
    arrived = arrived[:groups]
    residual_grad, branch_own, gain_row = middle_grad(
        scalars, arrived, residual, flat_grad, gains
    )
    sending = send_far(1, out_last)
    branch_own, branch_crossed, *sending = fence(branch_own, swap(branch_own, "tp", 1), *sending)
    keep_far(sending)
    branch = [branch_own, branch_crossed]
    for (call, own, got), crossed in zip(middle, out_crossed):
        kept = summed(after(own, branch_own), got, low) + crossed.astype(F32)
        for i, b in enumerate(call):
            out_parts[b] = swap(fence(kept[i].astype(BF16))[0], "ctx", b)
    moved = list(out_parts)
    edges.append((*out_sets[-1][:2], out_last))
    edges = [(call, after(own, branch_own), got) for call, own, got in edges]
    out_crossed = [swap(summed(own, got, high).astype(BF16), "tp", 1) for _, own, got in edges]

    dq, dkv_parts = attend_grad(
        scalars, branch, queries, kv_all, lse, pieces, cos_table, sin_table, piece_count
    )
    sending = send_far(1, branch_crossed)
    dq, dkv_parts, out_first, out_last, *arrived = fence(
        dq, dkv_parts, *out_crossed, *[out_parts[b] for b in moved], *sending
    )
    out_crossed = [out_first, out_last]
    out_parts.update(dict(zip(moved, arrived)))
    keep_far(arrived[len(moved) :])

    for (call, own, got), crossed in zip(edges, out_crossed):
        kept = summed(after(own, dq), got, low) + crossed.astype(F32)
        for i, b in enumerate(call):
            out_parts[b] = kept[i] if b == 0 else swap(fence(kept[i].astype(BF16))[0], "ctx", b)
    sending = send_far(1, dq)
    own_grads, far_grads, sent_grads, dkv_parts, *arrived = fence(
        *weight_grads(scalars, normed_all, dq, dkv_parts, branch, mixed, gain_row, quarter),
        dkv_parts,
        *[out_parts[b] for b in calls[-1]],
        *sending,
    )
    out_parts.update(dict(zip(calls[-1], arrived)))
    keep_far(arrived[len(calls[-1]) :])

    got_grads = fence(swap(sent_grads, "shard", 1))[0]
    passed = (far_grads.astype(F32) + got_grads[1].astype(F32)).astype(BF16)
    places = {
        v[1]: (n, 3 * k)
        for n, chosen in enumerate(far_sets(local_experts))
        for k, v in enumerate(chosen)
        if v[0] == 1
    }
    mates = jnp.stack(
        [
            (keep_1[e].astype(F32) + far_got[n][start : start + 3].astype(F32)).astype(BF16)
            for e, (n, start) in sorted(places.items())
        ]
    )
    kept_grads = (after(own_grads, mates).astype(F32) + got_grads[0].astype(F32)).astype(BF16)
    def natural(own, other):
        return jnp.where(
            side == 0,
            jnp.concatenate([own, other], axis=0),
            jnp.concatenate([other, own], axis=0),
        )[None]

    out_sum = after(residual, kept_grads)
    for b in range(groups):
        out_sum = out_sum + out_parts[b].astype(F32)
    out_half = out_sum.astype(BF16)
    output = natural(out_half, swap(out_half, "tp", 1))
    dkv, passed, kept_grads, output, mates = fence(
        lax.all_to_all(
            dkv_parts.reshape(groups, tokens, 2 * kv_width), "ctx", 0, 0, tiled=True
        ),
        swap(passed, "shard", 2),
        kept_grads,
        output,
        swap(mates, "shard", 1),
    )

    total = fence((kept_grads.astype(F32) + passed.astype(F32)).astype(BF16))[0]
    normed_own, normed_send = back(scalars, dq, dkv, pieces)
    input_half = last_grad(
        scalars, flat_input, normed_own, swap(normed_send, "tp", 1), residual_grad, gains
    )
    early = list(far_got)
    sending = send_far(len(far_sent), dkv)
    expert_grad = gather_expert_grads(scalars, keep_0, early, mates, None)
    total, input_half, input_other, expert_grad, *sending = fence(
        lax.all_to_all(
            total.reshape(groups, rows_here, total.shape[1]), "ctx", 0, 0, tiled=True
        ),
        input_half,
        swap(input_half, "tp", 1),
        expert_grad,
        *sending,
    )
    keep_far(sending)
    input_grad = natural(input_half, input_other)
    if sending:
        expert_grad = gather_expert_grads(scalars, keep_0, sending, None, expert_grad)
    total = jnp.sum(total.astype(F32), axis=0)
    query_grad = total[:, :q_width]
    key_grad = total[:, q_width : q_width + kv_width]
    value_grad = total[:, q_width + kv_width : q_width + 2 * kv_width]
    heads = q_width + 2 * kv_width
    out_grad = total[:, heads : heads + q_width].T
    moe_sum = total[:, heads + q_width]
    attn_sum = (
        jnp.sum(w_query.astype(F32) * query_grad, axis=1)
        + jnp.sum(w_key.astype(F32) * key_grad, axis=1)
        + jnp.sum(w_value.astype(F32) * value_grad, axis=1)
    )
    sums = jnp.stack([attn_sum, moe_sum])
    attn_sum, moe_norm_grad = sums + swap(sums, "tp", 1)
    attn_norm_grad = attn_sum / attn_norm.astype(F32)
    return (
        output,
        input_grad,
        attn_norm_grad,
        query_grad,
        key_grad,
        value_grad,
        out_grad,
        moe_norm_grad,
        expert_grad,
    )


def solution(mesh):
    in_specs = (
        P("shard", "ctx", None),
        P(("shard", "ctx")),
        P(("shard", "ctx"), "tp"),
        P(("shard", "ctx"), "tp"),
        P(("shard", "ctx"), "tp"),
        P("tp", ("shard", "ctx")),
        P(("shard", "ctx")),
        P("ctx", None, "shard", "tp"),
        P("shard", "ctx", None),
        P("shard", "ctx", None),
        P("shard", "ctx", None),
        P("shard", None),
        P("shard", "ctx", None),
    )
    out_specs = (
        P("shard", "ctx", None),
        P("shard", "ctx", None),
        P(("shard", "ctx")),
        P(("shard", "ctx"), "tp"),
        P(("shard", "ctx"), "tp"),
        P(("shard", "ctx"), "tp"),
        P("tp", ("shard", "ctx")),
        P(("shard", "ctx")),
        P("ctx", None, "shard", "tp"),
    )
    return jax.shard_map(local, mesh=mesh, in_specs=in_specs, out_specs=out_specs, check_vma=False)
```
